32 devices in a mesh: dp: 8 (over y, x, core), seq: 4 (over z).
Axes of the slice: x: 2, y: 2, z: 4, core: 2. Of those that a mesh axis runs over, the one named last changes fastest.
Arguments:
- tokens: bfloat16 [8, 2048, 1024], P('dp', 'seq'), may hold values from -6 to 6
- lengths: int32 [8], P('dp'), may hold values from 1024 to 2048, as said below
- cotangent: bfloat16 [8, 2048, 1024], P('dp', 'seq'), may hold values from -6 to 6
- w_query: bfloat16 [1024, 1024], P('seq'), may hold values from -0.1875 to 0.1875
- w_key: bfloat16 [1024, 512], P('seq'), may hold values from -0.1875 to 0.1875
- w_value: bfloat16 [1024, 512], P('seq'), may hold values from -0.1875 to 0.1875
- w_out: bfloat16 [1024, 1024], P('seq'), may hold values from -0.75 to 0.75
- w_gate: bfloat16 [1024, 4608], P('seq'), may hold values from -0.1875 to 0.1875
- w_up: bfloat16 [1024, 4608], P('seq'), may hold values from -0.1875 to 0.1875
- w_down: bfloat16 [4608, 1024], P('seq'), may hold values from -0.09375 to 0.09375
- gain_attn: bfloat16 [1024], P('seq'), may hold values from 0.5 to 1.5
- gain_ffn: bfloat16 [1024], P('seq'), may hold values from 0.5 to 1.5
- gain_query: bfloat16 [64], P('seq'), may hold values from 1 to 1.59375
- gain_key: bfloat16 [64], P('seq'), may hold values from 1 to 1.59375
Outputs:
- output: bfloat16 [8, 2048, 1024], P('dp', 'seq')
- grad_tokens: float32 [8, 2048, 1024], P('dp', 'seq')
- grad_query: float32 [1024, 1024], P('seq')
- grad_key: float32 [1024, 512], P('seq')
- grad_value: float32 [1024, 512], P('seq')
- grad_out: float32 [1024, 1024], P('seq')
- grad_gate: float32 [1024, 4608], P('seq')
- grad_up: float32 [1024, 4608], P('seq')
- grad_down: float32 [4608, 1024], P('seq')
- grad_gain_attn: float32 [1024], P('seq')
- grad_gain_ffn: float32 [1024], P('seq')
- grad_gain_query: float32 [64], P('seq')
- grad_gain_key: float32 [64], P('seq')
The draws below stay inside these ranges and needn't reach their ends.
Inputs may be any that keep to these rules, and one draw needn't show every extreme that they name: `lengths`: valid positions of each slot; in every draw some slot is full and some slot has exactly 1024.
All inputs are finite; a program needn't handle non-finite values.
Results may differ from the reference program's by a relative error of at most 0.022.
Values may be sent and summed in bfloat16 or wider, within the bound.
No kernel may reach another device: no remote copies, remote signals or barrier semaphores. Data moves between devices by JAX's collectives and lax.ppermute only.
A program may use at most 320 MiB of HBM per device.

```python
import jax
import jax.numpy as jnp
from jax import lax

D = 1024
H = 16
KV = 8
HD = 64
FF = 4608
LENGTH = 2048
SLOTS = 8


def draw_lengths(key, part):
    first, second = jax.random.split(key)
    values = jax.random.randint(first, (SLOTS,), LENGTH // 2, LENGTH + 1)
    order = jax.random.permutation(second, SLOTS)
    values = jnp.where(order == 0, LENGTH, values)
    values = jnp.where(order == 1, LENGTH // 2, values)
    return values.astype(jnp.int32)


def block_levels(own_key, dims, cuts, smallest, largest):
    level, own = 1.0, jax.random.fold_in(own_key, 6)
    for dim, parts in cuts:
        draws = jnp.exp(jax.random.uniform(jax.random.fold_in(own, dim), (parts,), jnp.float32, smallest / len(cuts), largest / len(cuts)))
        level = level * jnp.repeat(draws, dims[dim] // parts).reshape([-1 if axis == dim else 1 for axis in range(len(dims))])
    return level


def noise(own_key, extent, scale, limit, cuts=(), kind=jnp.bfloat16):
    level = block_levels(own_key, extent, cuts, -0.22, 0.18) if cuts else 1.0
    entries = jax.random.normal(own_key, extent, jnp.float32) * scale * level
    return jnp.minimum(jnp.maximum(entries, -limit), limit).astype(kind)


def setup_inputs(seed: int = 0) -> dict:
    splits = jax.random.split(jax.random.key(seed), 15)
    tokens = noise(splits[0], (SLOTS, LENGTH, D), 1.0, 6.0, ((0, 8), (1, 4)))
    lengths = draw_lengths(jax.random.fold_in(splits[14], 71), 0)
    cotangent = noise(splits[2], (SLOTS, LENGTH, D), 1.0, 6.0, ((0, 8), (1, 4)))
    w_query = noise(splits[3], (D, H * HD), D ** -0.5, 0.1875, ((0, 4),))
    w_key = noise(splits[4], (D, KV * HD), D ** -0.5, 0.1875, ((0, 4),))
    w_value = noise(splits[5], (D, KV * HD), D ** -0.5, 0.1875, ((0, 4),))
    w_out = noise(splits[6], (H * HD, D), (H * HD // 16) ** -0.5, 0.75, ((0, 4),))
    w_gate = noise(splits[7], (D, FF), D ** -0.5, 0.1875, ((0, 4),))
    w_up = noise(splits[8], (D, FF), D ** -0.5, 0.1875, ((0, 4),))
    w_down = noise(splits[9], (FF, D), FF ** -0.5, 0.09375, ((0, 4),))
    gain_attn = jnp.clip(1.0 + 0.1 * jax.random.normal(splits[10], (D,), jnp.float32), 0.5, 1.5).astype(jnp.bfloat16)
    gain_ffn = jnp.clip(1.0 + 0.1 * jax.random.normal(splits[11], (D,), jnp.float32), 0.5, 1.5).astype(jnp.bfloat16)
    gain_query = jnp.clip(1.0 + 0.59375 * jax.random.uniform(splits[12], (HD,), jnp.float32) ** block_levels(splits[12], (HD,), ((0, 4),), -0.2, 0.2), 1.0, 1.59375).astype(jnp.bfloat16)
    gain_key = jnp.clip(1.0 + 0.59375 * jax.random.uniform(splits[13], (HD,), jnp.float32) ** block_levels(splits[13], (HD,), ((0, 4),), -0.2, 0.2), 1.0, 1.59375).astype(jnp.bfloat16)
    return dict(tokens=tokens, lengths=lengths, cotangent=cotangent, w_query=w_query, w_key=w_key, w_value=w_value, w_out=w_out, w_gate=w_gate, w_up=w_up, w_down=w_down, gain_attn=gain_attn, gain_ffn=gain_ffn, gain_query=gain_query, gain_key=gain_key)


EPS = 1e-05
rope_base = 1000000.0
negative = -1e+30
highest = lax.Precision.HIGHEST

@jax.custom_vjp
def low(v):
    return lax.optimization_barrier(v.astype(jnp.bfloat16)).astype(jnp.float32)

@jax.custom_vjp
def low_back(v):
    return v

def low_keep(v):
    return (low(v), None)

def low_pass(kept, grad):
    return (grad,)

def back_keep(v):
    return (v, None)

def back_low(kept, grad):
    return (low(grad),)
low.defvjp(low_keep, low_pass)
low_back.defvjp(back_keep, back_low)

def matmul(left, right):
    return jnp.dot(left, right, precision=highest, preferred_element_type=jnp.float32)

def rms_scale(values):
    return lax.rsqrt(lax.optimization_barrier(jnp.mean(values * values, axis=-1, keepdims=True)) + EPS)

def tables(positions, width):
    half = width // 2
    freq = rope_base ** (-(jnp.arange(half, dtype=jnp.float32) * 2.0 / width))
    angle = positions.astype(jnp.float32)[:, None] * freq[None, :]
    angle = jnp.concatenate([angle, angle], axis=1)
    return (jnp.cos(angle)[:, None, :], jnp.sin(angle)[:, None, :])

def rotate_half(values):
    half = values.shape[-1] // 2
    return jnp.concatenate([-values[..., half:], values[..., :half]], axis=-1)

def rotary(values, cosine, sine):
    return values * cosine + rotate_half(values) * sine

def slot_forward(params, inputs, length):
    w_query, w_key, w_value, w_out, w_gate, w_up, w_down, gain_attn, gain_ffn, gain_query, gain_key = params
    positions = jnp.arange(LENGTH, dtype=jnp.int32)
    cosine, sine = tables(positions, HD)
    normed1 = inputs * rms_scale(inputs)
    hidden1 = low(normed1 * gain_attn)
    query_raw = low_back(matmul(hidden1, w_query)).reshape(LENGTH, H, HD)
    key_raw = low_back(matmul(hidden1, w_key)).reshape(LENGTH, KV, HD)
    values = low(low_back(matmul(hidden1, w_value))).reshape(LENGTH, KV, HD)
    query_rot = low(low_back(rotary(query_raw * rms_scale(query_raw) * gain_query, cosine, sine)))
    key_rot = low(low_back(rotary(key_raw * rms_scale(key_raw) * gain_key, cosine, sine)))
    grouped = query_rot.reshape(LENGTH, KV, H // KV, HD)
    raw = low_back(jnp.einsum('bkgd,tkd->kgbt', grouped, key_rot, precision=highest, preferred_element_type=jnp.float32))
    scores = raw * HD ** (-0.5)
    mask = (positions[None, :] <= positions[:, None]) & (positions[None, :] < length)
    scores = jnp.where(mask, scores, negative)
    probs = jax.nn.softmax(scores, axis=-1)
    mixed = jnp.einsum('kgbt,tkd->bkgd', low(probs), values, precision=highest, preferred_element_type=jnp.float32)
    mixed = low(low_back(mixed.reshape(LENGTH, H * HD)))
    resid = inputs + low_back(matmul(mixed, w_out))
    normed2 = resid * rms_scale(resid)
    hidden2 = low(normed2 * gain_ffn)
    gate = low_back(matmul(hidden2, w_gate))
    up_proj = low_back(matmul(hidden2, w_up))
    inner = low(jax.nn.silu(gate) * up_proj)
    result = resid + matmul(inner, w_down)
    return jnp.where((positions < length)[:, None], result, 0.0)

def reference(tokens, lengths, cotangent, w_query, w_key, w_value, w_out, w_gate, w_up, w_down, gain_attn, gain_ffn, gain_query, gain_key):
    params = tuple((item.astype(jnp.float32) for item in (w_query, w_key, w_value, w_out, w_gate, w_up, w_down, gain_attn, gain_ffn, gain_query, gain_key)))
    inputs = tokens.astype(jnp.float32)
    step_fn = jax.checkpoint(slot_forward)

    def forward(inputs, params):

        def visit(carry, pair):
            return (carry, step_fn(params, pair[0], pair[1]))
        unused, outputs = lax.scan(visit, jnp.zeros((), jnp.float32), (inputs, lengths))
        return outputs
    output, pullback = jax.vjp(forward, inputs, params)
    grad_input, grad_params = pullback(cotangent.astype(jnp.float32))
    return (output.astype(jnp.bfloat16), grad_input, grad_params[0], grad_params[1], grad_params[2], grad_params[3], grad_params[4], grad_params[5], grad_params[6], grad_params[7], grad_params[8], grad_params[9], grad_params[10])
```

```python
import functools
import math

import jax
import jax.numpy as jnp
from jax import lax
from jax.experimental import pallas as pl
from jax.experimental.pallas import tpu as pltpu
from jax.sharding import PartitionSpec as P

H = 16
KV = 8
HD = 64
EPS = 1e-05
ROPE_BASE = 1000000.0
LOG2E = math.log2(math.e)
SPLIT = 8
CHUNKS = 3

f32 = jnp.float32
bf16 = jnp.bfloat16
NN = (((1,), (0,)), ((), ()))
NT = (((1,), (1,)), ((), ()))
TN = (((0,), (0,)), ((), ()))


def dot(left, right, dims=NN):
    return lax.dot_general(left, right, dims, preferred_element_type=f32)


def rms_scale(values):
    return lax.rsqrt(jnp.mean(values * values, axis=-1, keepdims=True) + EPS)


def norm_back(grads, normed, scale):
    return scale * (grads - normed * jnp.mean(grads * normed, axis=-1, keepdims=True))


def tables(positions, width):
    half = width // 2
    freq = ROPE_BASE ** (-(jnp.arange(half, dtype=f32) * 2.0 / width))
    angle = positions.astype(f32)[:, None] * freq[None, :]
    angle = jnp.concatenate([angle, angle], axis=1)
    return (jnp.cos(angle)[:, None, :], jnp.sin(angle)[:, None, :])


def rotate_half(values):
    half = values.shape[-1] // 2
    return jnp.concatenate([-values[..., half:], values[..., :half]], axis=-1)


def rotary(values, cosine, sine):
    return values * cosine + rotate_half(values) * sine


def rotary_back(grads, cosine, sine):
    return grads * cosine - rotate_half(grads * sine)


def pair_half(x, first):
    lane = lax.broadcasted_iota(jnp.int32, x.shape, 1)
    rolled = pltpu.roll(x.astype(f32), HD, 1).astype(x.dtype)
    return jnp.where((lane < HD) == first, x, rolled)


def stack_pair(x):
    lane = lax.broadcasted_iota(jnp.int32, x.shape, 1)
    zero = jnp.zeros_like(x)
    return jnp.concatenate([jnp.where(lane < HD, x, zero), jnp.where(lane < HD, zero, x)], axis=0)


def causal(probs, block):
    key = lax.broadcasted_iota(jnp.int32, probs.shape, 0)
    query = lax.broadcasted_iota(jnp.int32, probs.shape, 1)
    query = jnp.where(query >= block, query - block, query)
    return jnp.where(key <= query, probs, 0.0)


def attend_fwd_kernel(block, q_ref, k_ref, v_ref, o_ref, lse_ref, keys, values):
    first = pl.program_id(0) % 2 == 0
    i = pl.program_id(1)

    @pl.when(i == 0)
    def _():
        keys[...] = pair_half(k_ref[...], first)
        values[...] = pair_half(v_ref[...], first)

    queries = stack_pair(q_ref[...])

    def tile(t, diagonal):
        rows = pl.ds(t * block, block)
        probs = jnp.exp2(dot(keys[rows, :], queries, NT) * (HD**-0.5 * LOG2E))
        if diagonal:
            probs = causal(probs, block)
        return dot(values[rows, :], probs.astype(bf16), TN), jnp.sum(probs, axis=0, keepdims=True)

    def body(t, carry):
        part, total = tile(t, False)
        return carry[0] + part, carry[1] + total

    mixed, total = lax.fori_loop(0, i, body, tile(i, True))
    mixed = mixed * (1.0 / total)
    pair = jnp.concatenate([mixed[:HD, :block], mixed[HD:, block:]], axis=0)
    o_ref[...] = pair.T.astype(bf16)
    lse_ref[0, 0] = jnp.log2(total)


def attend_forward(qkv, block):
    length, width = qkv.shape
    kv = width // (4 * HD)
    n = length // block
    key_at = lambda j, i: (0, kv + j // 2)
    value_at = lambda j, i: (0, kv + kv // 2 + j // 2)
    return pl.pallas_call(
        functools.partial(attend_fwd_kernel, block),
        grid=(kv, n),
        in_specs=[
            pl.BlockSpec((block, 2 * HD), lambda j, i: (i, j)),
            pl.BlockSpec((length, 2 * HD), key_at),
            pl.BlockSpec((length, 2 * HD), value_at),
        ],
        out_specs=[
            pl.BlockSpec((block, 2 * HD), lambda j, i: (i, j)),
            pl.BlockSpec((1, 1, 1, 2 * block), lambda j, i: (j, i, 0, 0)),
        ],
        out_shape=[
            jax.ShapeDtypeStruct((length, width // 2), bf16),
            jax.ShapeDtypeStruct((kv, n, 1, 2 * block), f32),
        ],
        scratch_shapes=[pltpu.VMEM((length, 2 * HD), bf16), pltpu.VMEM((length, 2 * HD), bf16)],
        cost_estimate=pl.CostEstimate(
            flops=8 * length * length * 2 * HD * kv,
            transcendentals=length * length * kv,
            bytes_accessed=3 * length * width,
        ),
        name="attend_forward",
    )(qkv, qkv, qkv)


def attend_bwd_kernel(
    block, q_ref, k_ref, v_ref, g_ref, o_ref, lse_ref, dq_ref, dk_ref, dv_ref,
    queries, grads, delta, keys, values, grad_q,
):
    first = pl.program_id(0) % 2 == 0
    n = q_ref.shape[0] // block
    keys[...] = pair_half(k_ref[...], first)
    values[...] = pair_half(v_ref[...], first)
    for i in range(n):
        rows = slice(i * block, (i + 1) * block)
        g = g_ref[rows, :]
        queries[i] = stack_pair(q_ref[rows, :])
        grads[i] = stack_pair(g)
        both = (g.astype(f32) * o_ref[rows, :].astype(f32)).T
        delta[i] = jnp.concatenate(
            [jnp.sum(both[:HD], axis=0, keepdims=True), jnp.sum(both[HD:], axis=0, keepdims=True)],
            axis=1,
        )
        grad_q[i] = jnp.zeros(grad_q.shape[1:], f32)

    def tile(key, value, key_t, i, diagonal):
        query, grad = queries[i], grads[i]
        probs = jnp.exp2(dot(key, query, NT) * (HD**-0.5 * LOG2E) - lse_ref[0, i])
        if diagonal:
            probs = causal(probs, block)
        grad_probs = dot(value, grad, NT)
        grad_scores = (probs * (grad_probs - delta[i]) * HD**-0.5).astype(bf16)
        grad_q[i] += dot(key_t, grad_scores)
        return dot(grad_scores, query), dot(probs.astype(bf16), grad)

    def step(t, _):
        rows = pl.ds(t * block, block)
        key, value = keys[rows, :], values[rows, :]
        key_t = key.astype(f32).T.astype(bf16)

        def body(i, carry):
            part_k, part_v = tile(key, value, key_t, i, False)
            return carry[0] + part_k, carry[1] + part_v

        part_k, part_v = lax.fori_loop(t + 1, n, body, tile(key, value, key_t, t, True))
        part_k = (part_k + pltpu.roll(part_k, HD, 1)).astype(bf16)
        part_v = (part_v + pltpu.roll(part_v, HD, 1)).astype(bf16)

        @pl.when(first)
        def _():
            dk_ref[rows, :] = part_k
            dv_ref[rows, :] = part_v

        @pl.when(jnp.logical_not(first))
        def _():
            upper = lax.broadcasted_iota(jnp.int32, part_k.shape, 1) >= HD
            dk_ref[rows, :] = jnp.where(upper, part_k, dk_ref[rows, :])
            dv_ref[rows, :] = jnp.where(upper, part_v, dv_ref[rows, :])

        return 0

    lax.fori_loop(0, n, step, 0)
    for i in range(n):
        pair = jnp.concatenate([grad_q[i, :HD, :block], grad_q[i, HD:, block:]], axis=0)
        dq_ref[i * block : (i + 1) * block, :] = pair.T.astype(bf16)


def attend_backward(qkv, grads, mixed, lse, block):
    length, width = qkv.shape
    kv = width // (4 * HD)
    n = length // block
    spec = lambda at: pl.BlockSpec((length, 2 * HD), at)
    at_q = lambda j: (0, j)
    at_half = lambda j: (0, j // 2)
    return pl.pallas_call(
        functools.partial(attend_bwd_kernel, block),
        grid=(kv,),
        in_specs=[
            spec(at_q),
            spec(lambda j: (0, kv + j // 2)),
            spec(lambda j: (0, kv + kv // 2 + j // 2)),
            spec(at_q),
            spec(at_q),
            pl.BlockSpec((1, n, 1, 2 * block), lambda j: (j, 0, 0, 0)),
        ],
        out_specs=[spec(at_q), spec(at_half), spec(at_half)],
        out_shape=[
            jax.ShapeDtypeStruct((length, width // 2), bf16),
            jax.ShapeDtypeStruct((length, width // 4), bf16),
            jax.ShapeDtypeStruct((length, width // 4), bf16),
        ],
        scratch_shapes=[
            pltpu.VMEM((n, 2 * block, 2 * HD), bf16),
            pltpu.VMEM((n, 2 * block, 2 * HD), bf16),
            pltpu.VMEM((n, 1, 2 * block), f32),
            pltpu.VMEM((length, 2 * HD), bf16),
            pltpu.VMEM((length, 2 * HD), bf16),
            pltpu.VMEM((n, 2 * HD, 2 * block), f32),
        ],
        cost_estimate=pl.CostEstimate(
            flops=20 * length * length * 2 * HD * kv,
            transcendentals=length * length * kv,
            bytes_accessed=6 * length * width,
        ),
        name="attend_backward",
    )(qkv, qkv, qkv, grads, mixed, lse)


def ffn_kernel(
    shards, z_ref, h_ref, ht_ref, gy_ref, own_g, own_u, own_d, far_g, far_u, far_d,
    out_in, grad_in, out_ref, grad_ref, mine, theirs, down,
):
    t = pl.program_id(0)
    z = z_ref[0]
    even = z_ref[1] == 0
    rows = own_g.shape[0]
    piece = rows // SPLIT
    unit = own_g.shape[1]
    lanes = down.shape[1] // SPLIT
    blocks = unit // piece

    @pl.when(t == 0)
    def _():
        out_ref[...] = out_in[...]
        grad_ref[...] = grad_in[...]
        down[...] = own_d[...]

    @pl.when(t > 0)
    def _():
        for d in range(SPLIT):
            for k in range(blocks):
                down[k * piece : (k + 1) * piece, d * lanes : (d + 1) * lanes] = far_d[
                    d, 0, 0, :, k * lanes : (k + 1) * lanes
                ]

    def shard_of(r):
        return lax.rem(z + shards - r, shards)

    def columns(r):
        return pl.ds(pl.multiple_of(shard_of(r) * rows, rows), rows)

    def weight(own, far, r):
        return own[...] if r == 0 else far[:, r - 1, 0].reshape(rows, unit)

    gate = up = None
    for r in range(shards):
        left = h_ref[:, columns(r)]
        part_g, part_u = dot(left, weight(own_g, far_g, r)), dot(left, weight(own_u, far_u, r))
        gate, up = (part_g, part_u) if r == 0 else (gate + part_g, up + part_u)
    grad_inner = dot(gy_ref[...], down[...], NT)
    sigma = jax.nn.sigmoid(gate)
    active = gate * sigma
    inner = (active * up).astype(bf16)
    grad_g = (grad_inner * up * sigma * (1.0 + gate * (1.0 - sigma))).astype(bf16)
    grad_u = (grad_inner * active).astype(bf16)
    out_ref[...] += dot(inner, down[...])
    seg = pl.ds(pl.multiple_of(shard_of(t) * unit, unit), unit)

    def keep(term, r, at):
        term = term.astype(bf16).reshape(SPLIT // 2, 2, piece, unit)
        mine[:, r, at : at + piece, seg] = jnp.where(even, term[:, 0], term[:, 1])
        theirs[:, r, at : at + piece, seg] = jnp.where(even, term[:, 1], term[:, 0])

    for r in range(shards):
        grad_ref[:, columns(r)] += dot(grad_g, weight(own_g, far_g, r), NT) + dot(
            grad_u, weight(own_u, far_u, r), NT
        )
        left = ht_ref[columns(r), :]
        keep(dot(left, grad_g), r, 0)
        keep(dot(left, grad_u), r, piece)
    term = dot(inner, gy_ref[...], TN).astype(bf16)
    for d in range(0, SPLIT, 2):
        for k in range(blocks):
            rows_k = slice(k * piece, (k + 1) * piece)
            first = term[rows_k, d * lanes : (d + 1) * lanes]
            second = term[rows_k, (d + 1) * lanes : (d + 2) * lanes]
            to = (d // 2, t, slice(2 * piece, 3 * piece), slice(k * lanes, (k + 1) * lanes))
            mine[to] = jnp.where(even, first, second)
            theirs[to] = jnp.where(even, second, first)


def ffn_chunk(c, z, hidden, hidden_t, grad_y, w_gate, w_up, w_down, far, out_in, grad_in):
    rows, width = hidden.shape
    shards = width // w_gate.shape[0]
    depth = w_gate.shape[0]
    unit = w_down.shape[0] // CHUNKS
    piece = depth // SPLIT
    far = far.reshape(SPLIT, shards - 1, 3, piece, shards * unit)
    seg = lambda t, z_ref: lax.rem(z_ref[0] + shards - t, shards)
    whole = lambda shape: pl.BlockSpec(shape, lambda t, z_ref: (0,) * len(shape))
    own = pl.BlockSpec((depth, unit), lambda t, z_ref: (0, seg(t, z_ref) * CHUNKS + c))
    gathered = lambda kind: pl.BlockSpec(
        (SPLIT, shards - 1, 1, piece, unit), lambda t, z_ref: (0, 0, kind, 0, seg(t, z_ref))
    )
    return pl.pallas_call(
        functools.partial(ffn_kernel, shards),
        grid_spec=pltpu.PrefetchScalarGridSpec(
            num_scalar_prefetch=1,
            grid=(shards,),
            in_specs=[
                whole((rows, width)),
                whole((width, rows)),
                whole((rows, width)),
                own,
                own,
                pl.BlockSpec((unit, width), lambda t, z_ref: (c, 0)),
                gathered(0),
                gathered(1),
                pl.BlockSpec(
                    (SPLIT, 1, 1, piece, shards * unit),
                    lambda t, z_ref: (0, jnp.maximum(t - 1, 0), 2, 0, 0),
                ),
                whole((rows, width)),
                whole((rows, width)),
            ],
            out_specs=[
                whole((rows, width)),
                whole((rows, width)),
                whole((SPLIT // 2, shards, 3 * piece, shards * unit)),
                whole((SPLIT // 2, shards, 3 * piece, shards * unit)),
            ],
            scratch_shapes=[pltpu.VMEM((unit, width), bf16)],
        ),
        out_shape=[
            jax.ShapeDtypeStruct((rows, width), f32),
            jax.ShapeDtypeStruct((rows, width), f32),
            jax.ShapeDtypeStruct((SPLIT // 2, shards, 3 * piece, shards * unit), bf16),
            jax.ShapeDtypeStruct((SPLIT // 2, shards, 3 * piece, shards * unit), bf16),
        ],
        cost_estimate=pl.CostEstimate(
            flops=18 * rows * width * shards * unit,
            transcendentals=rows * shards * unit,
            bytes_accessed=12 * width * shards * unit + 20 * rows * width,
        ),
        name="ffn_chunk",
    )(z, hidden, hidden_t, grad_y, w_gate, w_up, w_down, far, far, far, out_in, grad_in)


def unpack_kernel(*refs):
    sources, (gate_ref, up_ref, down_ref) = refs[:-3], refs[-3:]
    c = pl.program_id(0)
    piece = sources[0].shape[1] // 3
    lanes = down_ref.shape[1] // SPLIT
    blocks = down_ref.shape[0] // piece
    for index, ref in enumerate(sources):

        @pl.when(c == index)
        def _(ref=ref):
            gate_ref[...] = ref[:, 0:piece, :].astype(f32).reshape(gate_ref.shape)
            up_ref[...] = ref[:, piece : 2 * piece, :].astype(f32).reshape(up_ref.shape)
            for d in range(SPLIT):
                for k in range(blocks):
                    down_ref[k * piece : (k + 1) * piece, d * lanes : (d + 1) * lanes] = ref[
                        d, 2 * piece :, k * lanes : (k + 1) * lanes
                    ].astype(f32)


def unpack_ffn(sources, depth, shards, unit, width):
    piece = depth // SPLIT
    blocks = shards * unit // (width // SPLIT) // shards
    return pl.pallas_call(
        unpack_kernel,
        grid=(CHUNKS, shards),
        in_specs=[
            pl.BlockSpec((SPLIT, 3 * piece, unit), lambda c, s, i=i: (0, 0, jnp.where(c == i, s, jnp.where(c < i, 0, shards - 1))))
            for i in range(CHUNKS)
        ],
        out_specs=[
            pl.BlockSpec((depth, unit), lambda c, s: (0, s * CHUNKS + c)),
            pl.BlockSpec((depth, unit), lambda c, s: (0, s * CHUNKS + c)),
            pl.BlockSpec((blocks * piece, width), lambda c, s: (c * shards + s, 0)),
        ],
        out_shape=[
            jax.ShapeDtypeStruct((depth, shards * CHUNKS * unit), f32),
            jax.ShapeDtypeStruct((depth, shards * CHUNKS * unit), f32),
            jax.ShapeDtypeStruct((CHUNKS * unit, width), f32),
        ],
        name="unpack_ffn",
    )(*sources)


class Axes:
    def __init__(self, mesh):
        self.n_dp = mesh.shape["dp"]
        self.n_seq = mesh.shape["seq"]
        self.groups = None
        self.across = None
        if self.n_dp > SPLIT:
            self.groups = [[g + i for i in range(SPLIT)] for g in range(0, self.n_dp, SPLIT)]
            self.across = [list(range(i, self.n_dp, SPLIT)) for i in range(SPLIT)]

    def member(self):
        return lax.rem(lax.axis_index("dp"), SPLIT)

    def shift(self, x, r):
        n = self.n_seq
        return lax.ppermute(x, "seq", [(i, (i + r) % n) for i in range(n)])

    def from_others(self, x):
        return [self.shift(x, r) for r in range(1, self.n_seq)]

    def gather(self, x):
        return lax.all_gather(x, "dp", axis=0, tiled=True, axis_index_groups=self.groups)

    def swap(self, x, bit):
        return lax.ppermute(x, "dp", [(i, i ^ bit) for i in range(self.n_dp)])

    def halves(self, terms):
        terms = terms.reshape(SPLIT // 2, 2, *terms.shape[1:])
        parity = lax.rem(lax.axis_index("dp"), 2)
        pick = lambda i: lax.dynamic_index_in_dim(terms, i, axis=1, keepdims=False)
        return pick(parity), pick(1 - parity)


def after(x, *others):
    return lax.optimization_barrier((x, *others))[0]


class Reduction:
    def __init__(self, axes, mine, theirs):
        self.axes = axes
        member = axes.member()
        self.x = lax.rem(lax.div(member, 2), 2)
        self.y = lax.div(member, 4)
        self.mine = mine.reshape(2, 2, *mine.shape[1:])
        self.state = (axes.swap(theirs, 1),)

    def then(self, *others):
        self.state = lax.optimization_barrier((*self.state, *others))[: len(self.state)]

    def _sum(self, y, x, low, *more):
        def cut(arr):
            shards = arr.shape[2] // 2
            start = [y if y is not None else 0, x if x is not None else 0, 0 if low else shards]
            size = [1 if y is not None else 2, 1 if x is not None else 2, shards]
            rest = arr.ndim - 3
            part = lax.dynamic_slice(arr, start + [0] * rest, size + list(arr.shape[3:]))
            drop = tuple(i for i, at in enumerate((y, x)) if at is not None)
            return lax.squeeze(part, drop).astype(f32)

        total = cut(self.mine) + cut(self.recv)
        for arr in more:
            total = total + arr.astype(f32)
        return total

    def first(self):
        (recv,) = self.state
        self.recv = recv.reshape(self.mine.shape)
        to_x = self._sum(None, 1 - self.x, True).astype(bf16)
        to_y = self._sum(1 - self.y, None, False).astype(bf16)
        self.state = (self.axes.swap(to_x, 2), self.axes.swap(to_y, 4))
        return self

    def second(self):
        self.got_x, self.got_y = self.state
        pick = lambda arr, i: lax.dynamic_index_in_dim(arr, i, axis=0, keepdims=False)
        to_y = self._sum(1 - self.y, self.x, True, pick(self.got_x, 1 - self.y)).astype(bf16)
        to_x = self._sum(self.y, 1 - self.x, False, pick(self.got_y, 1 - self.x)).astype(bf16)
        self.state = (self.axes.swap(to_y, 4), self.axes.swap(to_x, 2))
        return self

    def third(self):
        got_y, got_x = self.state
        pick = lambda arr, i: lax.dynamic_index_in_dim(arr, i, axis=0, keepdims=False)
        low = self._sum(self.y, self.x, True, pick(self.got_x, self.y), got_y)
        high = self._sum(self.y, self.x, False, pick(self.got_y, self.x), got_x)
        half = low.shape[0]
        part = lambda r: (low if r < half else high)[r % half]
        n = 2 * half
        self.own = part(0)
        self.state = tuple(self.axes.shift(part(r).astype(bf16), -r) for r in range(1, n))
        return self

    def last(self):
        total = self.own
        for arr in self.state:
            total = total + arr.astype(f32)
        total = total.astype(bf16)
        if self.axes.across:
            total = lax.psum(total, "dp", axis_index_groups=self.axes.across)
        return total


def per_device(
    axes, tokens, lengths, cotangent, w_query, w_key, w_value, w_out, w_gate, w_up, w_down,
    gain_attn, gain_ffn, gain_query, gain_key,
):
    slots, local, width = tokens.shape
    assert slots == 1
    shards = axes.n_seq
    depth = width // shards
    piece = depth // SPLIT
    z = lax.axis_index("seq")
    member = axes.member()
    heads = H // shards
    kv_heads = KV // shards
    unit = w_down.shape[0] // CHUNKS
    lanes = width // SPLIT

    packed = jnp.concatenate([w_query, w_key, w_value, w_out], axis=1)
    packed = lax.dynamic_slice_in_dim(packed, member * piece, piece, axis=0)
    gains = jnp.concatenate([gain_attn, gain_ffn, gain_query, gain_key])
    gains = jnp.pad(gains, (0, piece * 128 - gains.shape[0])).reshape(piece, 128)
    packed = jnp.concatenate([packed, gains], axis=1)
    near = [packed] + axes.from_others(packed)
    gains = [x[:, -128:].reshape(-1) for x in near]
    attn_w = axes.gather(jnp.stack([x[:, :-128] for x in near]))
    attn_w = attn_w.reshape(SPLIT, shards, piece, -1).transpose(1, 0, 2, 3).reshape(width, -1)
    w_qkv, w_o = attn_w[:, : -width], attn_w[:, -width:]

    mine_g = lax.dynamic_slice_in_dim(w_gate, member * piece, piece, axis=0)
    mine_u = lax.dynamic_slice_in_dim(w_up, member * piece, piece, axis=0)
    mine_d = lax.dynamic_slice_in_dim(w_down, member * lanes, lanes, axis=1)
    mine_g = mine_g.reshape(piece, shards, CHUNKS, unit)
    mine_u = mine_u.reshape(piece, shards, CHUNKS, unit)
    own_parts = []
    for c in range(CHUNKS):
        part_d = mine_d[c * unit : (c + 1) * unit].reshape(unit // piece, piece, lanes)
        own = jnp.concatenate(
            [
                mine_g[:, :, c].reshape(piece, shards * unit),
                mine_u[:, :, c].reshape(piece, shards * unit),
                part_d.transpose(1, 0, 2).reshape(piece, shards * unit),
            ],
            axis=0,
        )
        own_parts.append(own)

    def cross(c, *others):
        return jnp.stack(axes.from_others(after(own_parts[c], *others) if others else own_parts[c]))


    def relative(x):
        parts = [
            lax.dynamic_slice_in_dim(x, lax.rem(z + shards - r, shards) * depth, depth, axis=1)
            for r in range(shards)
        ]
        return jnp.concatenate(parts, axis=1)

    def absolute(x):
        return relative_back(x)

    def relative_back(x):
        parts = [
            lax.dynamic_slice_in_dim(x, lax.rem(z + shards - r, shards) * depth, depth, axis=1)
            for r in range(shards)
        ]
        return jnp.concatenate(parts, axis=1)

    def gathered_gain(start, size):
        parts = jnp.stack([g[start : start + size] for g in gains])
        order = lax.rem(z + shards - jnp.arange(shards), shards)
        hot = (order[:, None] == jnp.arange(shards)[None, :]).astype(f32)
        return jnp.sum(hot[:, :, None] * parts.astype(f32)[:, None, :], axis=0).reshape(-1)

    head = HD // shards
    gain1 = gathered_gain(0, depth)
    gain2 = gathered_gain(depth, depth)
    gainq = gathered_gain(2 * depth, head)
    gaink = gathered_gain(2 * depth + head, head)

    positions = z * local + jnp.arange(local, dtype=jnp.int32)
    cosine, sine = tables(positions, HD)
    valid = (positions < lengths[0])[:, None]
    inputs = tokens[0].astype(f32)
    scale1 = rms_scale(inputs)
    normed1 = inputs * scale1
    hidden1 = relative((normed1 * gain1).astype(bf16))
    raw = dot(hidden1, w_qkv)
    query_raw = raw[:, : H * HD].reshape(local, H, HD)
    key_raw = raw[:, H * HD : (H + KV) * HD].reshape(local, KV, HD)
    value = raw[:, (H + KV) * HD :].astype(bf16)
    q_scale = rms_scale(query_raw)
    q_hat = query_raw * q_scale
    k_scale = rms_scale(key_raw)
    k_hat = key_raw * k_scale
    query = rotary(q_hat * gainq, cosine, sine).astype(bf16)
    key = rotary(k_hat * gaink, cosine, sine).astype(bf16)

    def by_head(x, count):
        return x.reshape(local, shards, count * HD).transpose(1, 0, 2)

    def exchange(x):
        return lax.all_to_all(x, "seq", split_axis=0, concat_axis=0, tiled=True)

    send = jnp.concatenate(
        [by_head(query, heads), by_head(key, kv_heads), by_head(value, kv_heads)], axis=2
    )
    far = [axes.gather(after(cross(0), send))]
    qkv = exchange(send).reshape(shards * local, -1)
    block = 512
    mixed_heads, lse = attend_forward(qkv, block)
    far.append(axes.gather(after(cross(1, qkv), mixed_heads)))
    mixed = exchange(mixed_heads.reshape(shards, local, heads * HD))
    mixed = mixed.transpose(1, 0, 2).reshape(local, H * HD)
    mixed_rel = relative(mixed)
    resid = inputs + dot(mixed_rel, w_o)
    scale2 = rms_scale(resid)
    normed2 = resid * scale2
    hidden2 = (normed2 * gain2).astype(bf16)
    hidden2_t = hidden2.T
    far.append(axes.gather(after(cross(2, mixed), hidden2)))
    grad_y = jnp.where(valid, cotangent[0], jnp.zeros((), bf16))

    where = jnp.stack([z, lax.rem(member, 2)]).astype(jnp.int32)
    result, grad_hidden2 = resid, jnp.zeros_like(resid)
    sums = []

    def chunk(c, result, grad_hidden2):
        result, grad_hidden2, mine, theirs = ffn_chunk(
            c, where, hidden2, hidden2_t, grad_y, w_gate, w_up, w_down, far[c], result, grad_hidden2
        )
        sums.append(Reduction(axes, mine, theirs))
        return result, grad_hidden2

    result, grad_hidden2 = chunk(0, result, grad_hidden2)
    result, grad_hidden2 = chunk(1, result, grad_hidden2)
    sums[0].then(result)
    result = after(result, *sums[0].state)
    sums[0].first()
    result, grad_hidden2 = chunk(2, result, grad_hidden2)
    output = jnp.where(valid, result, 0.0).astype(bf16)[None]
    sums[0].then(grad_hidden2)
    sums[1].then(grad_hidden2)
    grad_hidden2 = after(grad_hidden2, *sums[1].state, *sums[0].state)
    sums[1].first()
    sums[0].second()

    term_gain2 = jnp.sum(grad_hidden2 * normed2, axis=0)
    grad_resid = grad_y.astype(f32) + norm_back(grad_hidden2 * gain2, normed2, scale2)
    grad_branch = grad_resid.astype(bf16)

    def by_piece(term):
        return term.reshape(shards, SPLIT, piece, -1).transpose(1, 0, 2, 3)

    term_out = by_piece(dot(mixed_rel, grad_branch, TN).astype(bf16))
    sums.append(Reduction(axes, *axes.halves(term_out)))
    grad_mixed = absolute(dot(grad_branch, w_o, NT).astype(bf16))
    grad_heads = exchange(by_head(grad_mixed, heads)).reshape(shards * local, -1)
    grad_heads = after(grad_heads, *sums[2].state, *sums[1].state, *sums[0].state, *sums[3].state)
    for i in range(4):
        sums[i].then(grad_heads)
    sums[2].first()
    sums[3].first()
    sums[1].second()
    sums[0].third()
    back_q, back_k, back_v = attend_backward(qkv, grad_heads, mixed_heads, lse, block)
    back = jnp.concatenate([back_q, back_k, back_v], axis=1).reshape(shards, local, -1)
    back = after(back, *sums[2].state, *sums[1].state, *sums[0].state, *sums[3].state)
    for i in range(4):
        sums[i].then(back)
    pieces = [axes.gather(sums[0].last()[None])]
    sums[2].second()
    sums[3].second()
    back = exchange(back)
    back = after(back, *sums[2].state, *sums[3].state)
    sums[2].then(back)
    sums[3].then(back)
    sums[1].third()
    sums[2].third()
    sums[3].third()

    def joined(start, count):
        part = back[:, :, start * HD : (start + count) * HD]
        return part.transpose(1, 0, 2).reshape(local, shards * count * HD)

    back_q = joined(0, heads).astype(f32).reshape(local, H, HD)
    back_k = joined(heads, kv_heads).astype(f32).reshape(local, KV, HD)
    back_v = joined(heads + kv_heads, kv_heads)
    grad_qhat = rotary_back(back_q, cosine, sine)
    term_gainq = jnp.sum(grad_qhat * q_hat, axis=(0, 1))
    grad_qraw = norm_back(grad_qhat * gainq, q_hat, q_scale).reshape(local, H * HD).astype(bf16)
    grad_khat = rotary_back(back_k, cosine, sine)
    term_gaink = jnp.sum(grad_khat * k_hat, axis=(0, 1))
    grad_kraw = norm_back(grad_khat * gaink, k_hat, k_scale).reshape(local, KV * HD).astype(bf16)
    grad_raw = jnp.concatenate([grad_qraw, grad_kraw, back_v], axis=1)
    term_qkv = dot(hidden1, grad_raw, TN).astype(bf16)
    grad_hidden1 = absolute(dot(grad_raw, w_qkv, NT))
    term_gain1 = jnp.sum(grad_hidden1 * normed1, axis=0)
    grad_tokens = (grad_resid + norm_back(grad_hidden1 * gain1, normed1, scale1))[None]

    parts = [
        term_gain1.reshape(shards, depth),
        term_gain2.reshape(shards, depth),
        term_gainq.reshape(shards, head),
        term_gaink.reshape(shards, head),
    ]
    parts = jnp.concatenate(parts, axis=1)
    order = lax.rem(z + shards - jnp.arange(shards), shards)
    hot = (order[:, None] == jnp.arange(shards)[None, :]).astype(f32)
    parts = jnp.sum(hot[:, :, None] * parts[None], axis=1)
    each = parts.shape[1] // SPLIT
    parts = parts.reshape(shards, SPLIT, each).transpose(1, 0, 2)
    parts = jnp.pad(parts, ((0, 0), (0, 0), (0, piece * 128 - each)))
    parts = parts.reshape(SPLIT, shards, piece, 128).astype(bf16)
    term_qkv = jnp.concatenate([by_piece(term_qkv), parts], axis=3)
    term_qkv = after(term_qkv, *sums[1].state, *sums[2].state, *sums[3].state)
    for i in range(1, 4):
        sums[i].then(term_qkv)
    pieces += [axes.gather(sums[1].last()[None]), axes.gather(sums[2].last()[None])]
    grad_out = axes.gather(sums[3].last()).astype(f32)
    grad_gate, grad_up, grad_down = unpack_ffn(pieces, depth, shards, unit, width)
    tail = Reduction(axes, *axes.halves(term_qkv)).first().second().third()
    whole = axes.gather(tail.last()).astype(f32)
    grad_query = whole[:, : H * HD]
    grad_key = whole[:, H * HD : (H + KV) * HD]
    grad_value = whole[:, (H + KV) * HD : (H + 2 * KV) * HD]
    sums = whole[:, -128:].reshape(SPLIT, -1)[:, :each].reshape(-1)
    return (
        output,
        grad_tokens,
        grad_query,
        grad_key,
        grad_value,
        grad_out,
        grad_gate,
        grad_up,
        grad_down,
        sums[:depth],
        sums[depth : 2 * depth],
        sums[2 * depth : 2 * depth + head],
        sums[2 * depth + head :],
    )


def solution(mesh):
    rows = P("seq", None)
    whole = P("dp", "seq", None)
    return jax.shard_map(
        functools.partial(per_device, Axes(mesh)),
        mesh=mesh,
        in_specs=(whole, P("dp"), whole) + (rows,) * 7 + (P("seq"),) * 4,
        out_specs=(whole, whole) + (rows,) * 7 + (P("seq"),) * 4,
        check_vma=False,
    )
```

```python
import functools
import math

import jax
import jax.numpy as jnp
from jax import lax
from jax.experimental import pallas as pl
from jax.experimental.pallas import tpu as pltpu
from jax.sharding import PartitionSpec as P

H = 16
KV = 8
HD = 64
EPS = 1e-05
ROPE_BASE = 1000000.0
LOG2E = math.log2(math.e)
SPLIT = 8
CHUNKS = 3

f32 = jnp.float32
bf16 = jnp.bfloat16
NN = (((1,), (0,)), ((), ()))
NT = (((1,), (1,)), ((), ()))
TN = (((0,), (0,)), ((), ()))


def dot(left, right, dims=NN):
    return lax.dot_general(left, right, dims, preferred_element_type=f32)


def rms_scale(values):
    return lax.rsqrt(jnp.mean(values * values, axis=-1, keepdims=True) + EPS)


def norm_back(grads, normed, scale):
    return scale * (grads - normed * jnp.mean(grads * normed, axis=-1, keepdims=True))


def tables(positions):
    half = HD // 2
    freq = ROPE_BASE ** (-(jnp.arange(half, dtype=f32) * 2.0 / HD))
    angle = positions.astype(f32)[:, None] * freq[None, :]
    cosine, sine = jnp.cos(angle), jnp.sin(angle)
    return jnp.tile(cosine, (1, 4)), jnp.concatenate([-sine, sine, -sine, sine], axis=1)


def lanes_of(x):
    return lax.broadcasted_iota(jnp.int32, x.shape, 1)


def pair_mean(x):
    row = lax.broadcasted_iota(jnp.int32, (2 * HD, 2 * HD), 0)
    same = (row < HD) == (lax.broadcasted_iota(jnp.int32, (2 * HD, 2 * HD), 1) < HD)
    ones = jnp.where(same, 1.0 / HD, 0.0).astype(bf16)
    high = x.astype(bf16)
    return dot(high, ones) + dot((x - high.astype(f32)).astype(bf16), ones)


def other_half(x):
    low = lax.rem(lanes_of(x), HD) < HD // 2
    return jnp.where(low, pltpu.roll(x, 3 * HD // 2, 1), pltpu.roll(x, HD // 2, 1))


def pair_half(x, first):
    lane = lax.broadcasted_iota(jnp.int32, x.shape, 1)
    rolled = pltpu.roll(x.astype(f32), HD, 1).astype(x.dtype)
    return jnp.where((lane < HD) == first, x, rolled)


def stack_pair(x):
    lane = lax.broadcasted_iota(jnp.int32, x.shape, 1)
    zero = jnp.zeros_like(x)
    return jnp.concatenate([jnp.where(lane < HD, x, zero), jnp.where(lane < HD, zero, x)], axis=0)


def causal(probs, block):
    key = lax.broadcasted_iota(jnp.int32, probs.shape, 0)
    query = lax.broadcasted_iota(jnp.int32, probs.shape, 1)
    query = jnp.where(query >= block, query - block, query)
    return jnp.where(key <= query, probs, 0.0)


def attend_fwd_kernel(block, q_ref, k_ref, v_ref, o_ref, lse_ref, keys, values):
    first = pl.program_id(0) % 2 == 0
    i = pl.program_id(1)

    @pl.when(i == 0)
    def _():
        keys[...] = pair_half(k_ref[...], first)
        values[...] = pair_half(v_ref[...], first)

    queries = stack_pair(q_ref[...])

    def tile(t, diagonal):
        rows = pl.ds(t * block, block)
        probs = jnp.exp2(dot(keys[rows, :], queries, NT) * (HD**-0.5 * LOG2E))
        if diagonal:
            probs = causal(probs, block)
        return dot(values[rows, :], probs.astype(bf16), TN), jnp.sum(probs, axis=0, keepdims=True)

    def body(t, carry):
        part, total = tile(t, False)
        return carry[0] + part, carry[1] + total

    mixed, total = lax.fori_loop(0, i, body, tile(i, True))
    mixed = mixed * (1.0 / total)
    pair = jnp.concatenate([mixed[:HD, :block], mixed[HD:, block:]], axis=0)
    o_ref[...] = pair.T.astype(bf16)
    lse_ref[0, 0] = jnp.log2(total)


def attend_forward(qkv, block):
    length, width = qkv.shape
    kv = width // (4 * HD)
    n = length // block
    key_at = lambda j, i: (0, kv + j // 2)
    value_at = lambda j, i: (0, kv + kv // 2 + j // 2)
    return pl.pallas_call(
        functools.partial(attend_fwd_kernel, block),
        grid=(kv, n),
        in_specs=[
            pl.BlockSpec((block, 2 * HD), lambda j, i: (i, j)),
            pl.BlockSpec((length, 2 * HD), key_at),
            pl.BlockSpec((length, 2 * HD), value_at),
        ],
        out_specs=[
            pl.BlockSpec((block, 2 * HD), lambda j, i: (i, j)),
            pl.BlockSpec((1, 1, 1, 2 * block), lambda j, i: (j, i, 0, 0)),
        ],
        out_shape=[
            jax.ShapeDtypeStruct((length, width // 2), bf16),
            jax.ShapeDtypeStruct((kv, n, 1, 2 * block), f32),
        ],
        scratch_shapes=[pltpu.VMEM((length, 2 * HD), bf16), pltpu.VMEM((length, 2 * HD), bf16)],
        cost_estimate=pl.CostEstimate(
            flops=8 * length * length * 2 * HD * kv,
            transcendentals=length * length * kv,
            bytes_accessed=3 * length * width,
        ),
        name="attend_forward",
    )(qkv, qkv, qkv)


def attend_bwd_kernel(
    block, kv, q_ref, k_ref, v_ref, g_ref, o_ref, lse_ref, back_ref,
    queries, grads, delta, keys, values, grad_q,
):
    j = pl.program_id(0)
    first = j % 2 == 0
    n = q_ref.shape[0] // block
    at_k = pl.ds(pl.multiple_of((kv + j // 2) * 2 * HD, 2 * HD), 2 * HD)
    at_v = pl.ds(pl.multiple_of((kv + kv // 2 + j // 2) * 2 * HD, 2 * HD), 2 * HD)
    keys[...] = pair_half(k_ref[...], first)
    values[...] = pair_half(v_ref[...], first)
    for i in range(n):
        rows = slice(i * block, (i + 1) * block)
        g = g_ref[rows, :]
        queries[i] = stack_pair(q_ref[rows, :])
        grads[i] = stack_pair(g)
        both = (g.astype(f32) * o_ref[rows, :].astype(f32)).T
        delta[i] = jnp.concatenate(
            [jnp.sum(both[:HD], axis=0, keepdims=True), jnp.sum(both[HD:], axis=0, keepdims=True)],
            axis=1,
        )
        grad_q[i] = jnp.zeros(grad_q.shape[1:], f32)

    def tile(key, value, key_t, i, diagonal):
        query, grad = queries[i], grads[i]
        probs = jnp.exp2(dot(key, query, NT) * (HD**-0.5 * LOG2E) - lse_ref[0, i])
        if diagonal:
            probs = causal(probs, block)
        grad_probs = dot(value, grad, NT)
        grad_scores = (probs * (grad_probs - delta[i]) * HD**-0.5).astype(bf16)
        grad_q[i] += dot(key_t, grad_scores)
        return dot(grad_scores, query), dot(probs.astype(bf16), grad)

    def step(t, _):
        rows = pl.ds(t * block, block)
        key, value = keys[rows, :], values[rows, :]
        key_t = key.astype(f32).T.astype(bf16)

        def body(i, carry):
            part_k, part_v = tile(key, value, key_t, i, False)
            return carry[0] + part_k, carry[1] + part_v

        part_k, part_v = lax.fori_loop(t + 1, n, body, tile(key, value, key_t, t, True))
        part_k = (part_k + pltpu.roll(part_k, HD, 1)).astype(bf16)
        part_v = (part_v + pltpu.roll(part_v, HD, 1)).astype(bf16)

        @pl.when(first)
        def _():
            back_ref[rows, at_k] = part_k
            back_ref[rows, at_v] = part_v

        @pl.when(jnp.logical_not(first))
        def _():
            upper = lax.broadcasted_iota(jnp.int32, part_k.shape, 1) >= HD
            back_ref[rows, at_k] = jnp.where(upper, part_k, back_ref[rows, at_k])
            back_ref[rows, at_v] = jnp.where(upper, part_v, back_ref[rows, at_v])

        return 0

    lax.fori_loop(0, n, step, 0)
    for i in range(n):
        pair = jnp.concatenate([grad_q[i, :HD, :block], grad_q[i, HD:, block:]], axis=0)
        at_q = pl.ds(pl.multiple_of(j * 2 * HD, 2 * HD), 2 * HD)
        back_ref[i * block : (i + 1) * block, at_q] = pair.T.astype(bf16)


def attend_backward(qkv, grads, mixed, lse, block):
    length, width = qkv.shape
    kv = width // (4 * HD)
    n = length // block
    spec = lambda at: pl.BlockSpec((length, 2 * HD), at)
    at_q = lambda j: (0, j)
    return pl.pallas_call(
        functools.partial(attend_bwd_kernel, block, kv),
        grid=(kv,),
        in_specs=[
            spec(at_q),
            spec(lambda j: (0, kv + j // 2)),
            spec(lambda j: (0, kv + kv // 2 + j // 2)),
            spec(at_q),
            spec(at_q),
            pl.BlockSpec((1, n, 1, 2 * block), lambda j: (j, 0, 0, 0)),
        ],
        out_specs=pl.BlockSpec((length, width), lambda j: (0, 0)),
        out_shape=jax.ShapeDtypeStruct((length, width), bf16),
        scratch_shapes=[
            pltpu.VMEM((n, 2 * block, 2 * HD), bf16),
            pltpu.VMEM((n, 2 * block, 2 * HD), bf16),
            pltpu.VMEM((n, 1, 2 * block), f32),
            pltpu.VMEM((length, 2 * HD), bf16),
            pltpu.VMEM((length, 2 * HD), bf16),
            pltpu.VMEM((n, 2 * HD, 2 * block), f32),
        ],
        cost_estimate=pl.CostEstimate(
            flops=20 * length * length * 2 * HD * kv,
            transcendentals=length * length * kv,
            bytes_accessed=6 * length * width,
        ),
        name="attend_backward",
    )(qkv, qkv, qkv, grads, mixed, lse)


def ffn_kernel(
    shards, begins, z_ref, h_ref, ht_ref, gy_ref, own_g, own_u, own_d, far_g, far_u, far_d,
    out_in, grad_in, out_ref, grad_ref, *refs,
):
    terms, down = refs[:-1], refs[-1]
    t = pl.program_id(0)
    z = z_ref[0]
    even = z_ref[1] == 0
    rows = own_g.shape[0]
    piece = rows // SPLIT
    unit = own_g.shape[1]
    lanes = down.shape[1] // SPLIT
    blocks = unit // piece

    @pl.when(t == 0)
    def _():
        out_ref[...] = out_in[...]
        grad_ref[...] = jnp.zeros_like(grad_ref) if begins else grad_in[...]
        down[...] = own_d[...]

    @pl.when(t > 0)
    def _():
        for d in range(SPLIT):
            for k in range(blocks):
                down[k * piece : (k + 1) * piece, d * lanes : (d + 1) * lanes] = far_d[
                    d, 0, 0, :, k * lanes : (k + 1) * lanes
                ]

    def shard_of(r):
        return lax.rem(z + shards - r, shards)

    def columns(r):
        return pl.ds(pl.multiple_of(shard_of(r) * rows, rows), rows)

    def weight(own, far, r):
        return own[...] if r == 0 else far[:, r - 1, 0].reshape(rows, unit)

    gate = up = None
    for r in range(shards):
        left = h_ref[:, columns(r)]
        part_g, part_u = dot(left, weight(own_g, far_g, r)), dot(left, weight(own_u, far_u, r))
        gate, up = (part_g, part_u) if r == 0 else (gate + part_g, up + part_u)
    grad_inner = dot(gy_ref[...], down[...], NT)
    sigma = jax.nn.sigmoid(gate)
    active = gate * sigma
    inner = (active * up).astype(bf16)
    grad_g = (grad_inner * up * sigma * (1.0 + gate * (1.0 - sigma))).astype(bf16)
    grad_u = (grad_inner * active).astype(bf16)
    out_ref[...] += dot(inner, down[...])
    seg = pl.ds(pl.multiple_of(shard_of(t) * unit, unit), unit)

    def keep(term, r, at):
        term = term.astype(bf16)
        if len(terms) == 1:
            terms[0][:, r, at : at + piece, seg] = term.reshape(SPLIT, piece, unit)
            return
        mine, theirs = terms
        term = term.reshape(SPLIT // 2, 2, piece, unit)
        mine[:, r, at : at + piece, seg] = jnp.where(even, term[:, 0], term[:, 1])
        theirs[:, r, at : at + piece, seg] = jnp.where(even, term[:, 1], term[:, 0])

    for r in range(shards):
        grad_ref[:, columns(r)] += dot(grad_g, weight(own_g, far_g, r), NT) + dot(
            grad_u, weight(own_u, far_u, r), NT
        )
        left = ht_ref[columns(r), :]
        keep(dot(left, grad_g), r, 0)
        keep(dot(left, grad_u), r, piece)
    term = dot(inner, gy_ref[...], TN).astype(bf16)
    for d in range(SPLIT):
        for k in range(blocks):
            part = term[k * piece : (k + 1) * piece, d * lanes : (d + 1) * lanes]
            to = (t, slice(2 * piece, 3 * piece), slice(k * lanes, (k + 1) * lanes))
            if len(terms) == 1:
                terms[0][(d, *to)] = part
            elif d % 2 == 0:
                even_part = part
            else:
                even_part = term[k * piece : (k + 1) * piece, (d - 1) * lanes : d * lanes]
                terms[0][(d // 2, *to)] = jnp.where(even, even_part, part)
                terms[1][(d // 2, *to)] = jnp.where(even, part, even_part)


def ffn_chunk(c, kind, parted, z, hidden, hidden_t, grad_y, w_gate, w_up, w_down, far, out_in, grad_in):
    rows, width = hidden.shape
    shards = width // w_gate.shape[0]
    depth = w_gate.shape[0]
    unit = w_down.shape[0] // CHUNKS
    piece = depth // SPLIT
    far = far.reshape(SPLIT, shards - 1, -1, piece, shards * unit)
    terms = (SPLIT // 2 if parted else SPLIT, shards, 3 * piece, shards * unit)
    n_terms = 2 if parted else 1
    seg = lambda t, z_ref: lax.rem(z_ref[0] + shards - t, shards)
    whole = lambda shape: pl.BlockSpec(shape, lambda t, z_ref: (0,) * len(shape))
    own = pl.BlockSpec((depth, unit), lambda t, z_ref: (0, seg(t, z_ref) * CHUNKS + c))
    gathered = lambda at: pl.BlockSpec(
        (SPLIT, shards - 1, 1, piece, unit), lambda t, z_ref: (0, 0, at, 0, seg(t, z_ref))
    )
    return pl.pallas_call(
        functools.partial(ffn_kernel, shards, c == 0),
        grid_spec=pltpu.PrefetchScalarGridSpec(
            num_scalar_prefetch=1,
            grid=(shards,),
            in_specs=[
                whole((rows, width)),
                whole((width, rows)),
                whole((rows, width)),
                own,
                own,
                pl.BlockSpec((unit, width), lambda t, z_ref: (c, 0)),
                gathered(kind),
                gathered(kind + 1),
                pl.BlockSpec(
                    (SPLIT, 1, 1, piece, shards * unit),
                    lambda t, z_ref: (0, jnp.maximum(t - 1, 0), kind + 2, 0, 0),
                ),
                whole((rows, width)),
                whole((rows, width)),
            ],
            out_specs=[
                whole((rows, width)),
                whole((rows, width)),
            ]
            + [whole(terms)] * n_terms,
            scratch_shapes=[pltpu.VMEM((unit, width), bf16)],
        ),
        out_shape=[
            jax.ShapeDtypeStruct((rows, width), f32),
            jax.ShapeDtypeStruct((rows, width), f32),
        ]
        + [jax.ShapeDtypeStruct(terms, bf16)] * n_terms,
        cost_estimate=pl.CostEstimate(
            flops=18 * rows * width * shards * unit,
            transcendentals=rows * shards * unit,
            bytes_accessed=12 * width * shards * unit + 20 * rows * width,
        ),
        name="ffn_chunk",
    )(z, hidden, hidden_t, grad_y, w_gate, w_up, w_down, far, far, far, out_in, grad_in)


def pack_kernel(m_ref, gate, up, down, out, first_ref, last_ref):
    piece, width = out.shape
    unit = down.shape[0] // CHUNKS
    shards = gate.shape[1] // down.shape[0]
    lanes = down.shape[1]
    for c in range(CHUNKS):
        ref = last_ref if c == CHUNKS - 1 else first_ref
        at = 0 if c == CHUNKS - 1 else 3 * piece * c
        for s in range(shards):
            source = slice((s * CHUNKS + c) * unit, (s * CHUNKS + c + 1) * unit)
            ref[at : at + piece, s * unit : (s + 1) * unit] = gate[:, source]
            ref[at + piece : at + 2 * piece, s * unit : (s + 1) * unit] = up[:, source]
        for k in range(unit // piece):
            rows = slice(c * unit + k * piece, c * unit + (k + 1) * piece)
            ref[at + 2 * piece : at + 3 * piece, k * lanes : (k + 1) * lanes] = down[rows, :]
    at = 3 * piece * (CHUNKS - 1)
    first_ref[at:, :width] = out[...]
    first_ref[at:, width:] = jnp.zeros_like(first_ref[at:, width:])


def pack(member, w_gate, w_up, w_down, w_out):
    depth, width = w_out.shape
    piece = depth // SPLIT
    lanes = width // SPLIT
    line = w_gate.shape[1] // CHUNKS
    rows = lambda w: pl.BlockSpec((piece, w.shape[1]), lambda i, m_ref: (m_ref[0], 0))
    outs = [((3 * CHUNKS - 2) * piece, line), (3 * piece, line)]
    return pl.pallas_call(
        pack_kernel,
        grid_spec=pltpu.PrefetchScalarGridSpec(
            num_scalar_prefetch=1,
            grid=(1,),
            in_specs=[
                rows(w_gate),
                rows(w_up),
                pl.BlockSpec((w_down.shape[0], lanes), lambda i, m_ref: (0, m_ref[0])),
                rows(w_out),
            ],
            out_specs=[pl.BlockSpec(shape, lambda i, m_ref: (0, 0)) for shape in outs],
        ),
        out_shape=[jax.ShapeDtypeStruct(shape, bf16) for shape in outs],
        name="pack",
    )(member.reshape(1), w_gate, w_up, w_down, w_out)


def unpack_kernel(source, *refs):
    gate_ref, up_ref, down_ref = refs[-3:]
    piece = source.shape[2]
    lanes = down_ref.shape[1] // SPLIT
    blocks = down_ref.shape[0] // piece
    gate_ref[...] = source[:, 0].astype(f32).reshape(gate_ref.shape)
    up_ref[...] = source[:, 1].astype(f32).reshape(up_ref.shape)
    for d in range(SPLIT):
        for k in range(blocks):
            down_ref[k * piece : (k + 1) * piece, d * lanes : (d + 1) * lanes] = source[
                d, 2, :, k * lanes : (k + 1) * lanes
            ].astype(f32)


def unpack_ffn(source, first, count, before, depth, shards, unit, width):
    piece = depth // SPLIT
    source = source.reshape(SPLIT, -1, piece, shards * unit)
    rows = unit // shards
    columns = pl.BlockSpec((depth, unit), lambda c, s: (0, s * CHUNKS + first + c))
    return pl.pallas_call(
        unpack_kernel,
        grid=(count, shards),
        in_specs=[pl.BlockSpec((SPLIT, 3, piece, unit), lambda c, s: (0, c, 0, s))]
        + [pl.BlockSpec(memory_space=pl.ANY)] * len(before),
        out_specs=[
            columns,
            columns,
            pl.BlockSpec((rows, width), lambda c, s: ((first + c) * shards + s, 0)),
        ],
        out_shape=[
            jax.ShapeDtypeStruct((depth, shards * CHUNKS * unit), f32),
            jax.ShapeDtypeStruct((depth, shards * CHUNKS * unit), f32),
            jax.ShapeDtypeStruct((CHUNKS * unit, width), f32),
        ],
        input_output_aliases={i + 1: i for i in range(len(before))},
        name="unpack_ffn",
    )(source, *before)


def shard_at(z, r, shards):
    return lax.rem(z + shards - r, shards)


def part_of(z, r, shards, size):
    return pl.ds(pl.multiple_of(shard_at(z, r, shards) * size, size), size)


def joined(own, far, r):
    return own[...] if r == 0 else far[:, r - 1].reshape(own.shape)


def qkv_fwd_kernel(
    shards, z_ref, h_ref, cos_ref, sin_ref, gain_q, gain_k, *refs
):
    own, far, (send_ref, raw_ref) = refs[:3], refs[3:6], refs[6:]
    z = z_ref[0]
    depth = own[0].shape[0]
    total = [None] * 3
    for r in range(shards):
        left = h_ref[:, part_of(z, r, shards, depth)]
        for i in range(3):
            part = dot(left, joined(own[i], far[i], r))
            total[i] = part if r == 0 else total[i] + part
    cosine, sine = cos_ref[...], sin_ref[...]
    at = 0
    for values, gain in ((total[0], gain_q), (total[1], gain_k)):
        for i in range(0, values.shape[1], 2 * HD):
            pair = values[:, i : i + 2 * HD]
            raw_ref[:, at : at + 2 * HD] = pair
            scaled = pair * lax.rsqrt(pair_mean(pair * pair) + EPS) * gain[...]
            rotated = scaled * cosine + other_half(scaled) * sine
            send_ref[:, at : at + 2 * HD] = rotated.astype(bf16)
            at += 2 * HD
    send_ref[:, at:] = total[2].astype(bf16)


def projection_specs(shards, depth, piece, columns):
    sizes = [n // shards for n in columns]
    own = [pl.BlockSpec((depth, n), lambda s, z_ref: (0, s)) for n in sizes]
    starts = [sum(columns[:i]) // sizes[i] for i in range(3)]
    far = [
        pl.BlockSpec(
            (SPLIT, shards - 1, piece, n), lambda s, z_ref, start=start: (0, 0, 0, start + s)
        )
        for n, start in zip(sizes, starts)
    ]
    return own + far


def qkv_forward(z, hidden, cosine, sine, gain_q, gain_k, weights, far):
    local, width = hidden.shape
    depth = weights[0].shape[0]
    shards = width // depth
    columns = [w.shape[1] for w in weights]
    each = sum(columns) // shards
    raw = each - columns[2] // shards
    whole = lambda x: pl.BlockSpec(x.shape, lambda s, z_ref: (0,) * x.ndim)
    return pl.pallas_call(
        functools.partial(qkv_fwd_kernel, shards),
        grid_spec=pltpu.PrefetchScalarGridSpec(
            num_scalar_prefetch=1,
            grid=(shards,),
            in_specs=[whole(x) for x in (hidden, cosine, sine, gain_q, gain_k)]
            + projection_specs(shards, depth, far.shape[2], columns),
            out_specs=[
                pl.BlockSpec((local, each), lambda s, z_ref: (s, 0)),
                pl.BlockSpec((local, raw), lambda s, z_ref: (s, 0)),
            ],
        ),
        out_shape=[
            jax.ShapeDtypeStruct((shards * local, each), bf16),
            jax.ShapeDtypeStruct((shards * local, raw), f32),
        ],
        cost_estimate=pl.CostEstimate(
            flops=2 * local * width * sum(columns),
            transcendentals=0,
            bytes_accessed=2 * width * sum(columns) + 8 * local * sum(columns),
        ),
        name="qkv_forward",
    )(z, hidden, cosine, sine, gain_q, gain_k, *weights, far, far, far)


def qkv_bwd_kernel(
    shards, z_ref, ht_ref, cos_ref, sin_ref, gain_q, gain_k, back_ref, raw_ref, *refs
):
    own, far, (grad_ref, mine, theirs, sum_q, sum_k, grads) = refs[:3], refs[3:6], refs[6:]
    z = z_ref[0]
    even = z_ref[1] == 0
    depth = own[0].shape[0]
    piece = depth // SPLIT

    @pl.when(pl.program_id(0) == 0)
    def _():
        grad_ref[...] = jnp.zeros_like(grad_ref)
        sum_q[...] = jnp.zeros_like(sum_q)
        sum_k[...] = jnp.zeros_like(sum_k)

    cosine, sine = cos_ref[...], sin_ref[...]
    at = 0
    for size, gain, total in ((own[0].shape[1], gain_q, sum_q), (own[1].shape[1], gain_k, sum_k)):
        for _ in range(0, size, 2 * HD):
            pair = raw_ref[:, at : at + 2 * HD]
            scale = lax.rsqrt(pair_mean(pair * pair) + EPS)
            hat = pair * scale
            grad = back_ref[:, at : at + 2 * HD].astype(f32)
            grad = grad * cosine + other_half(grad * sine)
            total[...] += jnp.sum(grad * hat, axis=0, keepdims=True)
            grad = grad * gain[...]
            grads[:, at : at + 2 * HD] = (scale * (grad - hat * pair_mean(grad * hat))).astype(bf16)
            at += 2 * HD
    grads[:, at:] = back_ref[:, at:]
    ends = (0, own[0].shape[1], at, grads.shape[1])
    for r in range(shards):
        part = None
        for i in range(3):
            one = dot(grads[:, ends[i] : ends[i + 1]], joined(own[i], far[i], r), NT)
            part = one if i == 0 else part + one
        grad_ref[:, part_of(z, r, shards, depth)] += part
        term = dot(ht_ref[part_of(z, r, shards, depth), :], grads[...]).astype(bf16)
        term = term.reshape(SPLIT // 2, 2, piece, term.shape[1])
        mine[:, r] = jnp.where(even, term[:, 0], term[:, 1])
        theirs[:, r] = jnp.where(even, term[:, 1], term[:, 0])


def qkv_backward(z, hidden_t, cosine, sine, gain_q, gain_k, back, raw, weights, far, extra):
    width, local = hidden_t.shape
    depth = weights[0].shape[0]
    shards = width // depth
    piece = depth // SPLIT
    columns = [w.shape[1] for w in weights]
    each = back.shape[1]
    whole = lambda shape: pl.BlockSpec(shape, lambda s, z_ref: (0,) * len(shape))
    rows = lambda x: pl.BlockSpec((local, x.shape[1]), lambda s, z_ref: (s, 0))
    terms = jax.ShapeDtypeStruct((SPLIT // 2, shards, piece, shards * each + extra), bf16)
    at_terms = pl.BlockSpec((SPLIT // 2, shards, piece, each), lambda s, z_ref: (0, 0, 0, s))
    return pl.pallas_call(
        functools.partial(qkv_bwd_kernel, shards),
        grid_spec=pltpu.PrefetchScalarGridSpec(
            num_scalar_prefetch=1,
            grid=(shards,),
            in_specs=[whole(x.shape) for x in (hidden_t, cosine, sine, gain_q, gain_k)]
            + [rows(back), rows(raw)]
            + projection_specs(shards, depth, piece, columns),
            out_specs=[whole((local, width)), at_terms, at_terms, whole((1, 2 * HD)), whole((1, 2 * HD))],
            scratch_shapes=[pltpu.VMEM((local, each), bf16)],
        ),
        out_shape=[
            jax.ShapeDtypeStruct((local, width), f32),
            terms,
            terms,
            jax.ShapeDtypeStruct((1, 2 * HD), f32),
            jax.ShapeDtypeStruct((1, 2 * HD), f32),
        ],
        cost_estimate=pl.CostEstimate(
            flops=4 * local * width * sum(columns),
            transcendentals=0,
            bytes_accessed=4 * width * sum(columns) + 8 * local * sum(columns),
        ),
        name="qkv_backward",
    )(z, hidden_t, cosine, sine, gain_q, gain_k, back, raw, *weights, far, far, far)


def unpack_qkv_kernel(source, q_ref, k_ref, v_ref):
    at = 0
    for ref in (q_ref, k_ref, v_ref):
        ref[...] = source[:, at : at + ref.shape[1]].astype(f32)
        at += ref.shape[1]


def unpack_qkv(source, shards, columns):
    depth = source.shape[0]
    each = [n // shards for n in columns]
    return pl.pallas_call(
        unpack_qkv_kernel,
        grid=(shards,),
        in_specs=[pl.BlockSpec((depth, sum(each)), lambda s: (0, s))],
        out_specs=[pl.BlockSpec((depth, n), lambda s: (0, s)) for n in each],
        out_shape=[jax.ShapeDtypeStruct((depth, n), f32) for n in columns],
        name="unpack_qkv",
    )(source)


def out_fwd_kernel(shards, z_ref, mixed, tokens, gain, own, far, resid_ref, scale_ref, h_ref, ht_ref):
    z = z_ref[0]
    local = tokens.shape[0]
    resid = tokens[...].astype(f32)
    for r in range(shards):
        weight = own[...] if r == 0 else far[:, r - 1, 0].reshape(own.shape)
        resid = resid + dot(mixed[part_of(z, r, shards, local), :], weight)
    scale = rms_scale(resid)
    hidden = resid * scale * gain[...]
    resid_ref[...] = resid
    scale_ref[...] = scale
    h_ref[...] = hidden.astype(bf16)
    ht_ref[...] = hidden.T.astype(bf16)


def far_out_spec(far, width):
    size = (SPLIT, far.shape[1], 1, far.shape[3], width)
    return pl.BlockSpec(size, lambda i, z_ref: (0, 0, far.shape[2] - 1, 0, 0))


def out_forward(z, mixed, tokens, gain, w_out, far):
    local, width = tokens.shape
    shards = mixed.shape[0] // local
    piece = w_out.shape[0] // SPLIT
    far = far.reshape(SPLIT, shards - 1, -1, piece, far.shape[-1])
    whole = lambda shape: pl.BlockSpec(shape, lambda i, z_ref: (0,) * len(shape))
    outs = [((local, width), f32), ((local, 1), f32), ((local, width), bf16), ((width, local), bf16)]
    return pl.pallas_call(
        functools.partial(out_fwd_kernel, shards),
        grid_spec=pltpu.PrefetchScalarGridSpec(
            num_scalar_prefetch=1,
            grid=(1,),
            in_specs=[whole(x.shape) for x in (mixed, tokens, gain, w_out)]
            + [far_out_spec(far, width)],
            out_specs=[whole(shape) for shape, _ in outs],
        ),
        out_shape=[jax.ShapeDtypeStruct(*out) for out in outs],
        cost_estimate=pl.CostEstimate(
            flops=2 * local * width * width, transcendentals=0, bytes_accessed=14 * local * width
        ),
        name="out_forward",
    )(z, mixed, tokens, gain, w_out, far)


def out_bwd_kernel(
    shards, z_ref, grad, grad_y, resid, scale_ref, gain, own, far, grad_resid, sum_ref, branch, send
):
    z = z_ref[0]
    local = grad.shape[0]
    scale = scale_ref[...]
    normed = resid[...] * scale
    sum_ref[...] = jnp.sum(grad[...] * normed, axis=0, keepdims=True)
    total = grad_y[...].astype(f32) + norm_back(grad[...] * gain[...], normed, scale)
    grad_resid[...] = total
    low = total.astype(bf16)
    branch[...] = low
    for r in range(shards):
        weight = own[...] if r == 0 else far[:, r - 1, 0].reshape(own.shape)
        send[part_of(z, r, shards, local), :] = dot(low, weight, NT).astype(bf16)


def out_backward(z, grad, grad_y, resid, scale, gain, w_out, far):
    local, width = grad.shape
    depth = w_out.shape[0]
    shards = width // depth
    piece = depth // SPLIT
    far = far.reshape(SPLIT, shards - 1, -1, piece, far.shape[-1])
    whole = lambda shape: pl.BlockSpec(shape, lambda i, z_ref: (0,) * len(shape))
    outs = [((local, width), f32), ((1, width), f32), ((local, width), bf16), ((shards * local, depth), bf16)]
    return pl.pallas_call(
        functools.partial(out_bwd_kernel, shards),
        grid_spec=pltpu.PrefetchScalarGridSpec(
            num_scalar_prefetch=1,
            grid=(1,),
            in_specs=[whole(x.shape) for x in (grad, grad_y, resid, scale, gain, w_out)]
            + [far_out_spec(far, width)],
            out_specs=[whole(shape) for shape, _ in outs],
        ),
        out_shape=[jax.ShapeDtypeStruct(*out) for out in outs],
        cost_estimate=pl.CostEstimate(
            flops=2 * local * width * width, transcendentals=0, bytes_accessed=20 * local * width
        ),
        name="out_backward",
    )(z, grad, grad_y, resid, scale, gain, w_out, far)


def out_terms_kernel(shards, z_ref, mixed, branch, terms):
    term = dot(mixed[...], branch[...], TN).astype(bf16)
    terms[:, 0] = term.reshape(terms.shape[0], terms.shape[2], terms.shape[3])


def out_terms(z, mixed, branch):
    local, width = branch.shape
    shards = mixed.shape[0] // local
    depth = mixed.shape[1]
    piece = depth // SPLIT
    return pl.pallas_call(
        functools.partial(out_terms_kernel, shards),
        grid_spec=pltpu.PrefetchScalarGridSpec(
            num_scalar_prefetch=1,
            grid=(shards,),
            in_specs=[
                pl.BlockSpec((local, depth), lambda r, z_ref: (shard_at(z_ref[0], r, shards), 0)),
                pl.BlockSpec((local, width), lambda r, z_ref: (0, 0)),
            ],
            out_specs=pl.BlockSpec((SPLIT, 1, piece, width), lambda r, z_ref: (0, r, 0, 0)),
        ),
        out_shape=jax.ShapeDtypeStruct((SPLIT, shards, piece, width), bf16),
        cost_estimate=pl.CostEstimate(
            flops=2 * local * width * width, transcendentals=0, bytes_accessed=8 * local * width
        ),
        name="out_terms",
    )(z, mixed, branch)


class Axes:
    def __init__(self, mesh):
        self.n_dp = mesh.shape["dp"]
        self.n_seq = mesh.shape["seq"]
        self.groups = None
        self.across = None
        if self.n_dp > SPLIT:
            self.groups = [[g + i for i in range(SPLIT)] for g in range(0, self.n_dp, SPLIT)]
            self.across = [list(range(i, self.n_dp, SPLIT)) for i in range(SPLIT)]

    def member(self):
        return lax.rem(lax.axis_index("dp"), SPLIT)

    def shift(self, x, r):
        n = self.n_seq
        return lax.ppermute(x, "seq", [(i, (i + r) % n) for i in range(n)])

    def from_others(self, x):
        return [self.shift(x, r) for r in range(1, self.n_seq)]

    def passed_on(self, x):
        n = self.n_seq
        z = lax.axis_index("seq")
        up = down = x
        below, above = [], []
        for step in range(1, n):
            up = lax.ppermute(up, "seq", [(i, i + 1) for i in range(step - 1, n - 1)])
            down = lax.ppermute(down, "seq", [(i + 1, i) for i in range(n - step)])
            below.append(up)
            above.append(down)
        return [jnp.where(z >= r, below[r - 1], above[n - r - 1]) for r in range(1, n)]

    def gather(self, x):
        return lax.all_gather(x, "dp", axis=0, tiled=True, axis_index_groups=self.groups)

    def scatter(self, terms):
        flat = terms.reshape(SPLIT * terms.shape[1], *terms.shape[2:])
        return lax.psum_scatter(
            flat, "dp", scatter_dimension=0, tiled=True, axis_index_groups=self.groups
        )

    def over_groups(self, x):
        return lax.psum(x, "dp", axis_index_groups=self.across) if self.across else x

    def swap(self, x, bit):
        return lax.ppermute(x, "dp", [(i, i ^ bit) for i in range(self.n_dp)])


def after(x, *others):
    return lax.optimization_barrier((x, *others))[0]


class Reduction:
    def __init__(self, axes, mine, theirs):
        self.axes = axes
        member = axes.member()
        self.x = lax.rem(lax.div(member, 2), 2)
        self.y = lax.div(member, 4)
        self.mine = mine.reshape(2, 2, *mine.shape[1:])
        self.state = (axes.swap(theirs, 1),)

    def then(self, *others):
        self.state = lax.optimization_barrier((*self.state, *others))[: len(self.state)]

    def _sum(self, y, x, low, *more):
        def cut(arr):
            shards = arr.shape[2] // 2
            start = [y if y is not None else 0, x if x is not None else 0, 0 if low else shards]
            size = [1 if y is not None else 2, 1 if x is not None else 2, shards]
            rest = arr.ndim - 3
            part = lax.dynamic_slice(arr, start + [0] * rest, size + list(arr.shape[3:]))
            drop = tuple(i for i, at in enumerate((y, x)) if at is not None)
            return lax.squeeze(part, drop).astype(f32)

        total = cut(self.mine) + cut(self.recv)
        for arr in more:
            total = total + arr.astype(f32)
        return total

    def first(self):
        (recv,) = self.state
        self.recv = recv.reshape(self.mine.shape)
        to_x = self._sum(None, 1 - self.x, True).astype(bf16)
        to_y = self._sum(1 - self.y, None, False).astype(bf16)
        self.sent = (to_x, to_y)
        self.state = (self.axes.swap(to_x, 2), self.axes.swap(to_y, 4))
        return self

    def second(self):
        self.got_x, self.got_y = self.state
        pick = lambda arr, i: lax.dynamic_index_in_dim(arr, i, axis=0, keepdims=False)
        to_y = self._sum(1 - self.y, self.x, True, pick(self.got_x, 1 - self.y)).astype(bf16)
        to_x = self._sum(self.y, 1 - self.x, False, pick(self.got_y, 1 - self.x)).astype(bf16)
        self.sent = (to_x, to_y)
        self.state = (self.axes.swap(to_y, 4), self.axes.swap(to_x, 2))
        return self

    def third(self):
        got_y, got_x = self.state
        pick = lambda arr, i: lax.dynamic_index_in_dim(arr, i, axis=0, keepdims=False)
        low = self._sum(self.y, self.x, True, pick(self.got_x, self.y), got_y)
        high = self._sum(self.y, self.x, False, pick(self.got_y, self.x), got_x)
        return jnp.concatenate([low, high], axis=0).astype(bf16)


def per_device(
    axes, tokens, lengths, cotangent, w_query, w_key, w_value, w_out, w_gate, w_up, w_down,
    gain_attn, gain_ffn, gain_query, gain_key,
):
    slots, local, width = tokens.shape
    assert slots == 1
    shards = axes.n_seq
    depth = width // shards
    piece = depth // SPLIT
    z = lax.axis_index("seq")
    member = axes.member()
    unit = w_down.shape[0] // CHUNKS
    lanes = width // SPLIT
    head = HD // shards
    weights = (w_query, w_key, w_value)
    columns = [w.shape[1] for w in weights]
    where = jnp.stack([z, lax.rem(member, 2)]).astype(jnp.int32)
    mine = lambda x: lax.dynamic_slice_in_dim(x, member * piece, piece, axis=0)

    def by_owner(parts):
        pick = lambda i: lax.dynamic_index_in_dim(parts, lax.rem(z + shards - i, shards), 0)
        return jnp.concatenate([pick(i) for i in range(shards)], axis=0)

    def total(parts):
        return axes.over_groups(jnp.sum(parts.astype(f32), axis=0).astype(bf16))

    gains = jnp.concatenate([gain_attn, gain_ffn, gain_query, gain_key])
    gains = jnp.pad(gains, (0, piece * 128 - gains.shape[0])).reshape(piece, 128)
    packed = jnp.concatenate([mine(w_query), mine(w_key), mine(w_value), gains], axis=1)
    near = axes.from_others(packed)
    far_qkv = axes.gather(jnp.stack([x[:, :-128] for x in near]))
    far_qkv = far_qkv.reshape(SPLIT, shards - 1, piece, -1)
    gains = jnp.stack([x[:, -128:].reshape(-1) for x in [packed] + near])
    order = lax.rem(z + shards - jnp.arange(shards), shards)
    hot = (order[:, None] == jnp.arange(shards)[None, :]).astype(f32)
    gains = jnp.sum(hot[:, :, None] * gains.astype(f32)[:, None, :], axis=0)

    def gathered_gain(start, size):
        return gains[:, start : start + size].reshape(1, -1)

    gain1 = gathered_gain(0, depth)
    gain2 = gathered_gain(depth, depth)
    gain_q = jnp.tile(gathered_gain(2 * depth, head), (1, 2))
    gain_k = jnp.tile(gathered_gain(2 * depth + head, head), (1, 2))

    first_chunks, last_chunk = pack(member, w_gate, w_up, w_down, w_out)

    def stack_after(parts, *others):
        return jnp.stack([after(x, *others) for x in parts])

    positions = z * local + jnp.arange(local, dtype=jnp.int32)
    cosine, sine = tables(positions)
    valid = (positions < lengths[0])[:, None]
    grad_y = jnp.where(valid, cotangent[0], jnp.zeros((), bf16))
    inputs = tokens[0].astype(f32)
    scale1 = rms_scale(inputs)
    hidden1 = (inputs * scale1 * gain1).astype(bf16)
    hidden1_t = hidden1.T

    def exchange(x):
        return lax.all_to_all(x, "seq", split_axis=0, concat_axis=0, tiled=True)

    crossed = axes.passed_on(after(first_chunks, *near))
    send, raw = qkv_forward(where, hidden1, cosine, sine, gain_q, gain_k, weights, far_qkv)
    far = axes.gather(stack_after(crossed, send))
    qkv = exchange(send)
    crossed = axes.from_others(after(last_chunk, qkv))
    block = 512
    mixed_heads, lse = attend_forward(qkv, block)
    mixed = exchange(after(mixed_heads, *crossed))
    crossed = stack_after(crossed, mixed_heads)
    far_last = axes.gather(crossed)
    resid, scale2, hidden2, hidden2_t = out_forward(where, mixed, tokens[0], gain2, w_out, far)
    hidden2 = after(hidden2, crossed)

    result, grad_hidden2 = resid, resid

    def chunk(c, result, grad_hidden2):
        last = c == CHUNKS - 1
        source, kind = (far_last, 0) if last else (far, 3 * c)
        return ffn_chunk(
            c, kind, last, where, hidden2, hidden2_t, grad_y, w_gate, w_up, w_down, source,
            result, grad_hidden2,
        )

    result, grad_hidden2, terms0 = chunk(0, result, grad_hidden2)
    sum0 = axes.scatter(terms0)
    result, grad_hidden2, terms1 = chunk(1, result, grad_hidden2)
    sum1 = axes.scatter(terms1)
    result, grad_hidden2, *terms2 = chunk(2, result, grad_hidden2)
    sum2 = Reduction(axes, *terms2)

    grad_resid, term_gain2, branch, send = out_backward(
        where, grad_hidden2, grad_y, resid, scale2, gain2, w_out, far
    )
    grad_heads = exchange(send)
    terms_out = out_terms(where, mixed, after(branch, send))
    sum_out = axes.scatter(terms_out)
    sum2.then(terms_out)
    sum2.first()
    parts0 = by_owner(after(sum0, grad_heads))
    grad_heads = after(grad_heads, terms_out, *sum2.sent, parts0)
    parts0 = exchange(parts0)
    back = attend_backward(qkv, grad_heads, mixed_heads, lse, block)
    back_rows = exchange(after(back, parts0))
    sum2.then(back)
    sum2.second()
    piece0 = total(after(parts0, back))
    parts1 = by_owner(after(sum1, back))
    parts2 = by_owner(sum2.third())
    back_rows = after(back_rows, *sum2.sent, piece0, parts1, parts2)
    piece0 = axes.gather(piece0[None])
    parts1 = exchange(after(parts1, back_rows))
    parts2 = exchange(after(parts2, back_rows))
    grad_hidden1, terms, other, sum_q, sum_k = qkv_backward(
        where, hidden1_t, cosine, sine, gain_q, gain_k, back_rows, raw, weights, far_qkv, 128
    )
    piece1 = axes.gather(total(after(parts1, grad_hidden1))[None])
    normed1 = inputs * scale1
    term_gain1 = jnp.sum(grad_hidden1 * normed1, axis=0)
    grad_tokens = (grad_resid + norm_back(grad_hidden1 * gain1, normed1, scale1))[None]

    parts = [
        term_gain1.reshape(shards, depth),
        term_gain2.reshape(shards, depth),
        (sum_q[0, :HD] + sum_q[0, HD:]).reshape(shards, head),
        (sum_k[0, :HD] + sum_k[0, HD:]).reshape(shards, head),
    ]
    parts = jnp.concatenate(parts, axis=1)
    parts = jnp.sum(hot[:, :, None] * parts[None], axis=1)
    each = parts.shape[1] // SPLIT
    parts = parts.reshape(shards, SPLIT, each).transpose(1, 0, 2)
    parts = jnp.pad(parts, ((0, 0), (0, 0), (0, piece * 128 - each)))
    parts = parts.reshape(SPLIT // 2, 2, shards, piece, 128).astype(bf16)
    parity = lax.rem(member, 2)
    pick = lambda i: lax.dynamic_index_in_dim(parts, i, axis=1, keepdims=False)
    start = (0, 0, 0, terms.shape[3] - 128)
    terms = lax.dynamic_update_slice(terms, pick(parity), start)
    other = lax.dynamic_update_slice(other, pick(1 - parity), start)
    tail = Reduction(axes, terms, other).first()
    parts2 = after(parts2, *tail.sent)
    piece2 = axes.gather(total(parts2)[None])
    tail.second()
    tail = by_owner(jnp.concatenate([tail.third(), sum_out], axis=2))
    whole = axes.gather(total(exchange(tail)))
    grads = unpack_ffn(piece0, 0, 1, (), depth, shards, unit, width)
    grads = unpack_ffn(piece1, 1, 1, grads, depth, shards, unit, width)
    grads = unpack_ffn(piece2, 2, 1, grads, depth, shards, unit, width)
    grad_gate, grad_up, grad_down = grads
    output = jnp.where(valid, result, 0.0).astype(bf16)[None]
    grad_out = whole[:, -width:].astype(f32)
    grad_query, grad_key, grad_value = unpack_qkv(whole, shards, columns)
    sums = whole[:, sum(columns) : sum(columns) + 128].astype(f32).reshape(SPLIT, -1)[:, :each].reshape(-1)
    return (
        output,
        grad_tokens,
        grad_query,
        grad_key,
        grad_value,
        grad_out,
        grad_gate,
        grad_up,
        grad_down,
        sums[:depth],
        sums[depth : 2 * depth],
        sums[2 * depth : 2 * depth + head],
        sums[2 * depth + head :],
    )


def solution(mesh):
    rows = P("seq", None)
    whole = P("dp", "seq", None)
    return jax.shard_map(
        functools.partial(per_device, Axes(mesh)),
        mesh=mesh,
        in_specs=(whole, P("dp"), whole) + (rows,) * 7 + (P("seq"),) * 4,
        out_specs=(whole, whole) + (rows,) * 7 + (P("seq"),) * 4,
        check_vma=False,
    )
```

```python
import functools
import math

import jax
import jax.numpy as jnp
from jax import lax
from jax.experimental import pallas as pl
from jax.experimental.pallas import tpu as pltpu
from jax.sharding import PartitionSpec as P

H = 16
KV = 8
HD = 64
EPS = 1e-05
ROPE_BASE = 1000000.0
LOG2E = math.log2(math.e)
SPLIT = 8
CHUNKS = 3

f32 = jnp.float32
bf16 = jnp.bfloat16
NN = (((1,), (0,)), ((), ()))
NT = (((1,), (1,)), ((), ()))
TN = (((0,), (0,)), ((), ()))


def dot(left, right, dims=NN):
    return lax.dot_general(left, right, dims, preferred_element_type=f32)


def rms_scale(values):
    return lax.rsqrt(jnp.mean(values * values, axis=-1, keepdims=True) + EPS)


def norm_back(grads, normed, scale):
    return scale * (grads - normed * jnp.mean(grads * normed, axis=-1, keepdims=True))


def tables(positions):
    half = HD // 2
    freq = ROPE_BASE ** (-(jnp.arange(half, dtype=f32) * 2.0 / HD))
    angle = positions.astype(f32)[:, None] * freq[None, :]
    cosine, sine = jnp.cos(angle), jnp.sin(angle)
    return jnp.tile(cosine, (1, 4)), jnp.concatenate([-sine, sine, -sine, sine], axis=1)


def lanes_of(x):
    return lax.broadcasted_iota(jnp.int32, x.shape, 1)


def pair_mean(x):
    row = lax.broadcasted_iota(jnp.int32, (2 * HD, 2 * HD), 0)
    same = (row < HD) == (lax.broadcasted_iota(jnp.int32, (2 * HD, 2 * HD), 1) < HD)
    ones = jnp.where(same, 1.0 / HD, 0.0).astype(bf16)
    high = x.astype(bf16)
    return dot(high, ones) + dot((x - high.astype(f32)).astype(bf16), ones)


def other_half(x):
    low = lax.rem(lanes_of(x), HD) < HD // 2
    return jnp.where(low, pltpu.roll(x, 3 * HD // 2, 1), pltpu.roll(x, HD // 2, 1))


def pair_half(x, first):
    lane = lax.broadcasted_iota(jnp.int32, x.shape, 1)
    rolled = pltpu.roll(x.astype(f32), HD, 1).astype(x.dtype)
    return jnp.where((lane < HD) == first, x, rolled)


def stack_pair(x):
    lane = lax.broadcasted_iota(jnp.int32, x.shape, 1)
    zero = jnp.zeros_like(x)
    return jnp.concatenate([jnp.where(lane < HD, x, zero), jnp.where(lane < HD, zero, x)], axis=0)


def causal(probs, block):
    key = lax.broadcasted_iota(jnp.int32, probs.shape, 0)
    query = lax.broadcasted_iota(jnp.int32, probs.shape, 1)
    query = jnp.where(query >= block, query - block, query)
    return jnp.where(key <= query, probs, 0.0)


def attend_fwd_kernel(block, q_ref, k_ref, v_ref, o_ref, lse_ref, keys, values):
    first = pl.program_id(0) % 2 == 0
    i = pl.program_id(1)

    @pl.when(i == 0)
    def _():
        keys[...] = pair_half(k_ref[...], first)
        values[...] = pair_half(v_ref[...], first)

    queries = stack_pair(q_ref[...])

    def tile(t, diagonal):
        rows = pl.ds(t * block, block)
        probs = jnp.exp2(dot(keys[rows, :], queries, NT) * (HD**-0.5 * LOG2E))
        if diagonal:
            probs = causal(probs, block)
        return dot(values[rows, :], probs.astype(bf16), TN), jnp.sum(probs, axis=0, keepdims=True)

    def body(t, carry):
        part, total = tile(t, False)
        return carry[0] + part, carry[1] + total

    mixed, total = lax.fori_loop(0, i, body, tile(i, True))
    mixed = mixed * (1.0 / total)
    pair = jnp.concatenate([mixed[:HD, :block], mixed[HD:, block:]], axis=0)
    o_ref[...] = pair.T.astype(bf16)
    lse_ref[0, 0] = jnp.log2(total)


def attend_forward(qkv, block):
    length, width = qkv.shape
    kv = width // (4 * HD)
    n = length // block
    key_at = lambda j, i: (0, kv + j // 2)
    value_at = lambda j, i: (0, kv + kv // 2 + j // 2)
    return pl.pallas_call(
        functools.partial(attend_fwd_kernel, block),
        grid=(kv, n),
        in_specs=[
            pl.BlockSpec((block, 2 * HD), lambda j, i: (i, j)),
            pl.BlockSpec((length, 2 * HD), key_at),
            pl.BlockSpec((length, 2 * HD), value_at),
        ],
        out_specs=[
            pl.BlockSpec((block, 2 * HD), lambda j, i: (i, j)),
            pl.BlockSpec((1, 1, 1, 2 * block), lambda j, i: (j, i, 0, 0)),
        ],
        out_shape=[
            jax.ShapeDtypeStruct((length, width // 2), bf16),
            jax.ShapeDtypeStruct((kv, n, 1, 2 * block), f32),
        ],
        scratch_shapes=[pltpu.VMEM((length, 2 * HD), bf16), pltpu.VMEM((length, 2 * HD), bf16)],
        cost_estimate=pl.CostEstimate(
            flops=8 * length * length * 2 * HD * kv,
            transcendentals=length * length * kv,
            bytes_accessed=3 * length * width,
        ),
        name="attend_forward",
    )(qkv, qkv, qkv)


def attend_bwd_kernel(
    block, j, q_ref, k_ref, v_ref, g_ref, o_ref, lse_ref, back_ref,
    queries, grads, delta, keys, values, grad_q,
):
    first = j % 2 == 0
    n = q_ref.shape[0] // block
    keys[...] = pair_half(k_ref[...], first)
    values[...] = pair_half(v_ref[...], first)
    for i in range(n):
        rows = slice(i * block, (i + 1) * block)
        g = g_ref[rows, :]
        queries[i] = stack_pair(q_ref[rows, :])
        grads[i] = stack_pair(g)
        both = (g.astype(f32) * o_ref[rows, :].astype(f32)).T
        delta[i] = jnp.concatenate(
            [jnp.sum(both[:HD], axis=0, keepdims=True), jnp.sum(both[HD:], axis=0, keepdims=True)],
            axis=1,
        )
        grad_q[i] = jnp.zeros(grad_q.shape[1:], f32)

    def tile(key, value, key_t, i, diagonal):
        query, grad = queries[i], grads[i]
        probs = jnp.exp2(dot(key, query, NT) * (HD**-0.5 * LOG2E) - lse_ref[0, i])
        if diagonal:
            probs = causal(probs, block)
        grad_probs = dot(value, grad, NT)
        grad_scores = (probs * (grad_probs - delta[i]) * HD**-0.5).astype(bf16)
        grad_q[i] += dot(key_t, grad_scores)
        return dot(grad_scores, query), dot(probs.astype(bf16), grad)

    def step(t, _):
        rows = pl.ds(t * block, block)
        key, value = keys[rows, :], values[rows, :]
        key_t = key.astype(f32).T.astype(bf16)

        def body(i, carry):
            part_k, part_v = tile(key, value, key_t, i, False)
            return carry[0] + part_k, carry[1] + part_v

        part_k, part_v = lax.fori_loop(t + 1, n, body, tile(key, value, key_t, t, True))
        part_k = part_k + pltpu.roll(part_k, HD, 1)
        part_v = part_v + pltpu.roll(part_v, HD, 1)
        both = jnp.where(lanes_of(part_k) < HD, part_k, part_v)
        back_ref[rows, 2 * HD :] = both.astype(bf16)
        return 0

    lax.fori_loop(0, n, step, 0)
    for i in range(n):
        pair = jnp.concatenate([grad_q[i, :HD, :block], grad_q[i, HD:, block:]], axis=0)
        back_ref[i * block : (i + 1) * block, : 2 * HD] = pair.T.astype(bf16)


def attend_backward(qkv, grads, mixed, lse, block, j):
    length, width = qkv.shape
    kv = width // (4 * HD)
    n = length // block
    column = lambda c: pl.BlockSpec((length, 2 * HD), lambda i: (0, c))
    return pl.pallas_call(
        functools.partial(attend_bwd_kernel, block, j),
        grid=(1,),
        in_specs=[
            column(j),
            column(kv + j // 2),
            column(kv + kv // 2 + j // 2),
            column(j),
            column(j),
            pl.BlockSpec((1, n, 1, 2 * block), lambda i: (j, 0, 0, 0)),
        ],
        out_specs=pl.BlockSpec((length, 4 * HD), lambda i: (0, 0)),
        out_shape=jax.ShapeDtypeStruct((length, 4 * HD), bf16),
        scratch_shapes=[
            pltpu.VMEM((n, 2 * block, 2 * HD), bf16),
            pltpu.VMEM((n, 2 * block, 2 * HD), bf16),
            pltpu.VMEM((n, 1, 2 * block), f32),
            pltpu.VMEM((length, 2 * HD), bf16),
            pltpu.VMEM((length, 2 * HD), bf16),
            pltpu.VMEM((n, 2 * HD, 2 * block), f32),
        ],
        cost_estimate=pl.CostEstimate(
            flops=20 * length * length * 2 * HD,
            transcendentals=length * length,
            bytes_accessed=6 * length * 4 * HD,
        ),
        name="attend_backward",
    )(qkv, qkv, qkv, grads, mixed, lse)


def ffn_kernel(
    shards, begins, z_ref, h_ref, ht_ref, gy_ref, own_g, own_u, own_d, far_g, far_u, far_d,
    out_in, grad_in, valid, out_ref, grad_ref, *refs,
):
    terms, (down, total) = refs[:-2], refs[-2:]
    t = pl.program_id(0)
    z = z_ref[0]
    even = z_ref[1] == 0
    rows = own_g.shape[0]
    piece = rows // SPLIT
    unit = own_g.shape[1]
    lanes = down.shape[1] // SPLIT
    blocks = unit // piece

    @pl.when(t == 0)
    def _():
        total[...] = out_in[...]
        grad_ref[...] = jnp.zeros_like(grad_ref) if begins else grad_in[...]
        down[...] = own_d[...]

    @pl.when(t > 0)
    def _():
        for d in range(SPLIT):
            for k in range(blocks):
                down[k * piece : (k + 1) * piece, d * lanes : (d + 1) * lanes] = far_d[
                    d, 0, 0, :, k * lanes : (k + 1) * lanes
                ]

    def shard_of(r):
        return lax.rem(z + shards - r, shards)

    def weight(own, far):
        parts = [own[...]]
        for r in range(1, shards):
            parts.append(far[:, r - 1, 0].reshape(rows, unit))
        return jnp.concatenate(parts, axis=0)

    weight_g, weight_u = weight(own_g, far_g), weight(own_u, far_u)
    gate, up = dot(h_ref[...], weight_g), dot(h_ref[...], weight_u)
    grad_inner = dot(gy_ref[...], down[...], NT)
    sigma = jax.nn.sigmoid(gate)
    active = gate * sigma
    inner = (active * up).astype(bf16)
    grad_g = (grad_inner * up * sigma * (1.0 + gate * (1.0 - sigma))).astype(bf16)
    grad_u = (grad_inner * active).astype(bf16)
    total[...] += dot(inner, down[...])
    grad_ref[...] += dot(grad_g, weight_g, NT) + dot(grad_u, weight_u, NT)
    seg = pl.ds(pl.multiple_of(shard_of(t) * unit, unit), unit)

    def keep(term, at):
        term = term.astype(bf16)
        for r in range(shards):
            part = term[r * rows : (r + 1) * rows]
            if len(terms) == 1:
                terms[0][:, r, at : at + piece, seg] = part.reshape(SPLIT, piece, unit)
                continue
            part = part.reshape(SPLIT // 2, 2, piece, unit)
            mine, theirs = terms
            mine[:, r, at : at + piece, seg] = jnp.where(even, part[:, 0], part[:, 1])
            theirs[:, r, at : at + piece, seg] = jnp.where(even, part[:, 1], part[:, 0])

    keep(dot(ht_ref[...], grad_g), 0)
    keep(dot(ht_ref[...], grad_u), piece)

    @pl.when(t == shards - 1)
    def _():
        out = total[...]
        if out_ref.dtype == bf16:
            out = jnp.where(valid[...] > 0, out, 0.0).astype(bf16)
        out_ref[...] = out

    term = dot(inner, gy_ref[...], TN).astype(bf16)
    for d in range(SPLIT):
        for k in range(blocks):
            part = term[k * piece : (k + 1) * piece, d * lanes : (d + 1) * lanes]
            to = (t, slice(2 * piece, 3 * piece), slice(k * lanes, (k + 1) * lanes))
            if len(terms) == 1:
                terms[0][(d, *to)] = part
            elif d % 2 == 0:
                even_part = part
            else:
                even_part = term[k * piece : (k + 1) * piece, (d - 1) * lanes : d * lanes]
                terms[0][(d // 2, *to)] = jnp.where(even, even_part, part)
                terms[1][(d // 2, *to)] = jnp.where(even, part, even_part)


def ffn_chunk(
    c, kind, parted, z, hidden, hidden_t, grad_y, w_gate, w_up, w_down, far, out_in, grad_in, valid
):
    rows, width = hidden.shape
    shards = width // w_gate.shape[0]
    depth = w_gate.shape[0]
    unit = w_down.shape[0] // CHUNKS
    piece = depth // SPLIT
    n_far = shards - 1
    far = far.reshape(SPLIT, n_far, -1, piece, shards * unit)
    terms = (SPLIT // 2 if parted else SPLIT, shards, 3 * piece, shards * unit)
    n_terms = 2 if parted else 1
    seg = lambda t, z_ref: lax.rem(z_ref[0] + shards - t, shards)
    whole = lambda shape: pl.BlockSpec(shape, lambda t, z_ref: (0,) * len(shape))
    own = pl.BlockSpec((depth, unit), lambda t, z_ref: (0, seg(t, z_ref) * CHUNKS + c))
    gathered = lambda at: pl.BlockSpec(
        (SPLIT, n_far, 1, piece, unit), lambda t, z_ref: (0, 0, at, 0, seg(t, z_ref))
    )
    source = lambda t, z_ref: jnp.maximum(t - 1, 0)
    return pl.pallas_call(
        functools.partial(ffn_kernel, shards, c == 0),
        grid_spec=pltpu.PrefetchScalarGridSpec(
            num_scalar_prefetch=1,
            grid=(shards,),
            in_specs=[
                whole((rows, width)),
                whole((width, rows)),
                whole((rows, width)),
                own,
                own,
                pl.BlockSpec((unit, width), lambda t, z_ref: (c, 0)),
                gathered(kind),
                gathered(kind + 1),
                pl.BlockSpec(
                    (SPLIT, 1, 1, piece, shards * unit),
                    lambda t, z_ref: (0, source(t, z_ref), kind + 2, 0, 0),
                ),
                whole((rows, width)),
                whole((rows, width)),
                whole((rows, 1)),
            ],
            out_specs=[
                whole((rows, width)),
                whole((rows, width)),
            ]
            + [whole(terms)] * n_terms,
            scratch_shapes=[pltpu.VMEM((unit, width), bf16), pltpu.VMEM((rows, width), f32)],
        ),
        out_shape=[
            jax.ShapeDtypeStruct((rows, width), bf16 if c == CHUNKS - 1 else f32),
            jax.ShapeDtypeStruct((rows, width), f32),
        ]
        + [jax.ShapeDtypeStruct(terms, bf16)] * n_terms,
        cost_estimate=pl.CostEstimate(
            flops=18 * rows * width * shards * unit,
            transcendentals=rows * shards * unit,
            bytes_accessed=12 * width * shards * unit + 20 * rows * width,
        ),
        name="ffn_chunk",
    )(z, hidden, hidden_t, grad_y, w_gate, w_up, w_down, far, far, far, out_in, grad_in, valid)


def pack_kernel(m_ref, gate, up, down, out, first_ref, last_ref):
    piece, width = out.shape
    unit = down.shape[0] // CHUNKS
    shards = gate.shape[1] // down.shape[0]
    lanes = down.shape[1]
    for c in range(CHUNKS):
        ref = last_ref if c == CHUNKS - 1 else first_ref
        at = 0 if c == CHUNKS - 1 else 3 * piece * c
        for s in range(shards):
            source = slice((s * CHUNKS + c) * unit, (s * CHUNKS + c + 1) * unit)
            ref[at : at + piece, s * unit : (s + 1) * unit] = gate[:, source]
            ref[at + piece : at + 2 * piece, s * unit : (s + 1) * unit] = up[:, source]
        for k in range(unit // piece):
            rows = slice(c * unit + k * piece, c * unit + (k + 1) * piece)
            ref[at + 2 * piece : at + 3 * piece, k * lanes : (k + 1) * lanes] = down[rows, :]
    at = 3 * piece * (CHUNKS - 1)
    first_ref[at:, :width] = out[...]
    first_ref[at:, width:] = jnp.zeros_like(first_ref[at:, width:])


def pack(member, w_gate, w_up, w_down, w_out):
    depth, width = w_out.shape
    piece = depth // SPLIT
    lanes = width // SPLIT
    line = w_gate.shape[1] // CHUNKS
    rows = lambda w: pl.BlockSpec((piece, w.shape[1]), lambda i, m_ref: (m_ref[0], 0))
    outs = [((3 * CHUNKS - 2) * piece, line), (3 * piece, line)]
    return pl.pallas_call(
        pack_kernel,
        grid_spec=pltpu.PrefetchScalarGridSpec(
            num_scalar_prefetch=1,
            grid=(1,),
            in_specs=[
                rows(w_gate),
                rows(w_up),
                pl.BlockSpec((w_down.shape[0], lanes), lambda i, m_ref: (0, m_ref[0])),
                rows(w_out),
            ],
            out_specs=[pl.BlockSpec(shape, lambda i, m_ref: (0, 0)) for shape in outs],
        ),
        out_shape=[jax.ShapeDtypeStruct(shape, bf16) for shape in outs],
        name="pack",
    )(member.reshape(1), w_gate, w_up, w_down, w_out)


def unpack_kernel(source, *refs):
    gate_ref, up_ref, down_ref = refs[-3:]
    piece = source.shape[2]
    lanes = down_ref.shape[1] // SPLIT
    blocks = down_ref.shape[0] // piece
    gate_ref[...] = source[:, 0].astype(f32).reshape(gate_ref.shape)
    up_ref[...] = source[:, 1].astype(f32).reshape(up_ref.shape)
    for d in range(SPLIT):
        for k in range(blocks):
            down_ref[k * piece : (k + 1) * piece, d * lanes : (d + 1) * lanes] = source[
                d, 2, :, k * lanes : (k + 1) * lanes
            ].astype(f32)


def unpack_ffn(source, first, count, before, depth, shards, unit, width):
    piece = depth // SPLIT
    source = source.reshape(SPLIT, -1, piece, shards * unit)
    rows = unit // shards
    columns = pl.BlockSpec((depth, unit), lambda c, s: (0, s * CHUNKS + first + c))
    return pl.pallas_call(
        unpack_kernel,
        grid=(count, shards),
        in_specs=[pl.BlockSpec((SPLIT, 3, piece, unit), lambda c, s: (0, c, 0, s))]
        + [pl.BlockSpec(memory_space=pl.ANY)] * len(before),
        out_specs=[
            columns,
            columns,
            pl.BlockSpec((rows, width), lambda c, s: ((first + c) * shards + s, 0)),
        ],
        out_shape=[
            jax.ShapeDtypeStruct((depth, shards * CHUNKS * unit), f32),
            jax.ShapeDtypeStruct((depth, shards * CHUNKS * unit), f32),
            jax.ShapeDtypeStruct((CHUNKS * unit, width), f32),
        ],
        input_output_aliases={i + 1: i for i in range(len(before))},
        name="unpack_ffn",
    )(source, *before)


def shard_at(z, r, shards):
    return lax.rem(z + shards - r, shards)


def part_of(z, r, shards, size):
    return pl.ds(pl.multiple_of(shard_at(z, r, shards) * size, size), size)


def joined(own, far, r):
    return own[...] if r == 0 else far[:, r - 1].reshape(own.shape)


def qkv_fwd_kernel(
    shards, z_ref, h_ref, cos_ref, sin_ref, gain_q, gain_k, *refs
):
    own, far, (send_ref, raw_ref) = refs[:3], refs[3:6], refs[6:]
    z = z_ref[0]
    depth = own[0].shape[0]
    total = [None] * 3
    for r in range(shards):
        left = h_ref[:, part_of(z, r, shards, depth)]
        for i in range(3):
            part = dot(left, joined(own[i], far[i], r))
            total[i] = part if r == 0 else total[i] + part
    cosine, sine = cos_ref[...], sin_ref[...]
    at = 0
    for values, gain in ((total[0], gain_q), (total[1], gain_k)):
        for i in range(0, values.shape[1], 2 * HD):
            pair = values[:, i : i + 2 * HD]
            raw_ref[:, at : at + 2 * HD] = pair
            scaled = pair * lax.rsqrt(pair_mean(pair * pair) + EPS) * gain[...]
            rotated = scaled * cosine + other_half(scaled) * sine
            send_ref[:, at : at + 2 * HD] = rotated.astype(bf16)
            at += 2 * HD
    send_ref[:, at:] = total[2].astype(bf16)


def projection_specs(shards, depth, piece, columns):
    sizes = [n // shards for n in columns]
    own = [pl.BlockSpec((depth, n), lambda s, z_ref: (0, s)) for n in sizes]
    starts = [sum(columns[:i]) // sizes[i] for i in range(3)]
    far = [
        pl.BlockSpec(
            (SPLIT, shards - 1, piece, n), lambda s, z_ref, start=start: (0, 0, 0, start + s)
        )
        for n, start in zip(sizes, starts)
    ]
    return own + far


def qkv_forward(z, hidden, cosine, sine, gain_q, gain_k, weights, far):
    local, width = hidden.shape
    depth = weights[0].shape[0]
    shards = width // depth
    columns = [w.shape[1] for w in weights]
    each = sum(columns) // shards
    raw = each - columns[2] // shards
    whole = lambda x: pl.BlockSpec(x.shape, lambda s, z_ref: (0,) * x.ndim)
    return pl.pallas_call(
        functools.partial(qkv_fwd_kernel, shards),
        grid_spec=pltpu.PrefetchScalarGridSpec(
            num_scalar_prefetch=1,
            grid=(shards,),
            in_specs=[whole(x) for x in (hidden, cosine, sine, gain_q, gain_k)]
            + projection_specs(shards, depth, far.shape[2], columns),
            out_specs=[
                pl.BlockSpec((local, each), lambda s, z_ref: (s, 0)),
                pl.BlockSpec((local, raw), lambda s, z_ref: (s, 0)),
            ],
        ),
        out_shape=[
            jax.ShapeDtypeStruct((shards * local, each), bf16),
            jax.ShapeDtypeStruct((shards * local, raw), f32),
        ],
        cost_estimate=pl.CostEstimate(
            flops=2 * local * width * sum(columns),
            transcendentals=0,
            bytes_accessed=2 * width * sum(columns) + 8 * local * sum(columns),
        ),
        name="qkv_forward",
    )(z, hidden, cosine, sine, gain_q, gain_k, *weights, far, far, far)


def qkv_bwd_kernel(
    shards, heads, z_ref, ht_ref, cos_ref, sin_ref, gain_q, gain_k,
    tokens, scale_ref, gain_1, resid, raw_ref, *refs,
):
    back, refs = refs[:heads], refs[heads:]
    own, far, refs = refs[:3], refs[3:6], refs[6:]
    tokens_ref, mine, theirs, sum_q, sum_k, sum_1, grads, grad_ref = refs
    z = z_ref[0]
    even = z_ref[1] == 0
    depth = own[0].shape[0]
    piece = depth // SPLIT

    @pl.when(pl.program_id(0) == 0)
    def _():
        grad_ref[...] = jnp.zeros_like(grad_ref)
        sum_q[...] = jnp.zeros_like(sum_q)
        sum_k[...] = jnp.zeros_like(sum_k)

    cosine, sine = cos_ref[...], sin_ref[...]
    at = 0
    halves = [ref[:, 2 * HD :] for ref in back]
    swapped = [pltpu.roll(half.astype(f32), HD, 1).astype(bf16) for half in halves]
    low = lanes_of(halves[0]) < HD
    arrived = [[ref[:, : 2 * HD] for ref in back]]
    arrived.append([jnp.where(low, halves[i], swapped[i + 1]) for i in range(0, heads, 2)])
    arrived.append([jnp.where(low, swapped[i], halves[i + 1]) for i in range(0, heads, 2)])
    for pairs, gain, total in ((arrived[0], gain_q, sum_q), (arrived[1], gain_k, sum_k)):
        for grad in pairs:
            pair = raw_ref[:, at : at + 2 * HD]
            scale = lax.rsqrt(pair_mean(pair * pair) + EPS)
            hat = pair * scale
            grad = grad.astype(f32)
            grad = grad * cosine + other_half(grad * sine)
            total[...] += jnp.sum(grad * hat, axis=0, keepdims=True)
            grad = grad * gain[...]
            grads[:, at : at + 2 * HD] = (scale * (grad - hat * pair_mean(grad * hat))).astype(bf16)
            at += 2 * HD
    for i, pair in enumerate(arrived[2]):
        grads[:, at + i * 2 * HD : at + (i + 1) * 2 * HD] = pair
    ends = (0, own[0].shape[1], at, grads.shape[1])
    for r in range(shards):
        part = None
        for i in range(3):
            one = dot(grads[:, ends[i] : ends[i + 1]], joined(own[i], far[i], r), NT)
            part = one if i == 0 else part + one
        grad_ref[:, part_of(z, r, shards, depth)] += part
        term = dot(ht_ref[part_of(z, r, shards, depth), :], grads[...]).astype(bf16)
        term = term.reshape(SPLIT // 2, 2, piece, term.shape[1])
        mine[:, r] = jnp.where(even, term[:, 0], term[:, 1])
        theirs[:, r] = jnp.where(even, term[:, 1], term[:, 0])

    @pl.when(pl.program_id(0) == shards - 1)
    def _():
        scale = scale_ref[...]
        normed = tokens[...].astype(f32) * scale
        grad = grad_ref[...]
        sum_1[...] = jnp.sum(grad * normed, axis=0, keepdims=True)
        tokens_ref[...] = resid[...] + norm_back(grad * gain_1[...], normed, scale)


def qkv_backward(z, hidden_t, tables_gains, first_norm, back, raw, weights, far, extra):
    width, local = hidden_t.shape
    depth = weights[0].shape[0]
    shards = width // depth
    piece = depth // SPLIT
    columns = [w.shape[1] for w in weights]
    each = sum(columns) // shards
    whole = lambda shape: pl.BlockSpec(shape, lambda s, z_ref: (0,) * len(shape))
    rows = lambda x: pl.BlockSpec((local, x.shape[1]), lambda s, z_ref: (s, 0))
    terms = jax.ShapeDtypeStruct((SPLIT // 2, shards, piece, shards * each + extra), bf16)
    at_terms = pl.BlockSpec((SPLIT // 2, shards, piece, each), lambda s, z_ref: (0, 0, 0, s))
    return pl.pallas_call(
        functools.partial(qkv_bwd_kernel, shards, len(back)),
        grid_spec=pltpu.PrefetchScalarGridSpec(
            num_scalar_prefetch=1,
            grid=(shards,),
            in_specs=[whole(x.shape) for x in (hidden_t, *tables_gains, *first_norm)]
            + [rows(x) for x in (raw, *back)]
            + projection_specs(shards, depth, piece, columns),
            out_specs=[whole((local, width)), at_terms, at_terms]
            + [whole((1, n)) for n in (2 * HD, 2 * HD, width)],
            scratch_shapes=[pltpu.VMEM((local, each), bf16), pltpu.VMEM((local, width), f32)],
        ),
        out_shape=[
            jax.ShapeDtypeStruct((local, width), f32),
            terms,
            terms,
        ]
        + [jax.ShapeDtypeStruct((1, n), f32) for n in (2 * HD, 2 * HD, width)],
        cost_estimate=pl.CostEstimate(
            flops=4 * local * width * sum(columns),
            transcendentals=0,
            bytes_accessed=4 * width * sum(columns) + 8 * local * sum(columns),
        ),
        name="qkv_backward",
    )(z, hidden_t, *tables_gains, *first_norm, raw, *back, *weights, far, far, far)


def unpack_qkv_kernel(shards, m_ref, even, odd, *refs):
    piece = even.shape[1]
    for b in range(SPLIT):
        source = (odd if b % 2 else even)[b // 2].astype(f32)
        rows = pl.ds(pl.multiple_of(jnp.bitwise_xor(m_ref[0], b) * piece, piece), piece)
        at = 0
        for s in range(shards):
            for ref in refs[:3]:
                n = ref.shape[1] // shards
                ref[rows, s * n : (s + 1) * n] = source[:, at : at + n]
                at += n
        for ref in refs[3:]:
            ref[rows, :] = source[:, at : at + ref.shape[1]]
            at += ref.shape[1]


def unpack_qkv(member, even, odd, shards, columns):
    piece = even.shape[1]
    whole = lambda shape: pl.BlockSpec(shape, lambda i, m_ref: (0,) * len(shape))
    return pl.pallas_call(
        functools.partial(unpack_qkv_kernel, shards),
        grid_spec=pltpu.PrefetchScalarGridSpec(
            num_scalar_prefetch=1,
            grid=(1,),
            in_specs=[whole(even.shape), whole(odd.shape)],
            out_specs=[whole((SPLIT * piece, n)) for n in columns],
        ),
        out_shape=[jax.ShapeDtypeStruct((SPLIT * piece, n), f32) for n in columns],
        name="unpack_qkv",
    )(member.reshape(1), even, odd)


def out_fwd_kernel(shards, z_ref, mixed, tokens, gain, own, far, resid_ref, scale_ref, h_ref, ht_ref):
    z = z_ref[0]
    local = tokens.shape[0]
    resid = tokens[...].astype(f32)
    for r in range(shards):
        weight = own[...] if r == 0 else far[:, r - 1, 0].reshape(own.shape)
        resid = resid + dot(mixed[part_of(z, r, shards, local), :], weight)
    scale = rms_scale(resid)
    hidden = resid * scale * gain[...]
    resid_ref[...] = resid
    scale_ref[...] = scale
    turned = hidden.T.astype(bf16)
    low = hidden.astype(bf16)
    depth = own.shape[0]
    for s in range(shards):
        at = part_of(z, s, shards, depth)
        h_ref[:, at] = low[:, s * depth : (s + 1) * depth]
        ht_ref[at, :] = turned[s * depth : (s + 1) * depth]


def far_out_spec(far, width):
    size = (SPLIT, far.shape[1], 1, far.shape[3], width)
    return pl.BlockSpec(size, lambda i, z_ref: (0, 0, far.shape[2] - 1, 0, 0))


def out_forward(z, mixed, tokens, gain, w_out, far):
    local, width = tokens.shape
    shards = mixed.shape[0] // local
    piece = w_out.shape[0] // SPLIT
    far = far.reshape(SPLIT, shards - 1, -1, piece, far.shape[-1])
    whole = lambda shape: pl.BlockSpec(shape, lambda i, z_ref: (0,) * len(shape))
    outs = [((local, width), f32), ((local, 1), f32), ((local, width), bf16), ((width, local), bf16)]
    return pl.pallas_call(
        functools.partial(out_fwd_kernel, shards),
        grid_spec=pltpu.PrefetchScalarGridSpec(
            num_scalar_prefetch=1,
            grid=(1,),
            in_specs=[whole(x.shape) for x in (mixed, tokens, gain, w_out)]
            + [far_out_spec(far, width)],
            out_specs=[whole(shape) for shape, _ in outs],
        ),
        out_shape=[jax.ShapeDtypeStruct(*out) for out in outs],
        cost_estimate=pl.CostEstimate(
            flops=2 * local * width * width, transcendentals=0, bytes_accessed=14 * local * width
        ),
        name="out_forward",
    )(z, mixed, tokens, gain, w_out, far)


def out_bwd_kernel(
    shards, z_ref, grad, grad_y, resid, scale_ref, gain, own, far, grad_resid, sum_ref, branch, send
):
    z = z_ref[0]
    local = grad.shape[0]
    scale = scale_ref[...]
    normed = resid[...] * scale
    depth = own.shape[0]
    parts = [grad[:, part_of(z, s, shards, depth)] for s in range(shards)]
    come = jnp.concatenate(parts, axis=1)
    sum_ref[...] = jnp.sum(come * normed, axis=0, keepdims=True)
    total = grad_y[...].astype(f32) + norm_back(come * gain[...], normed, scale)
    grad_resid[...] = total
    low = total.astype(bf16)
    branch[...] = low
    for r in range(shards):
        weight = own[...] if r == 0 else far[:, r - 1, 0].reshape(own.shape)
        send[part_of(z, r, shards, local), :] = dot(low, weight, NT).astype(bf16)


def out_backward(z, grad, grad_y, resid, scale, gain, w_out, far):
    local, width = grad.shape
    depth = w_out.shape[0]
    shards = width // depth
    piece = depth // SPLIT
    far = far.reshape(SPLIT, shards - 1, -1, piece, far.shape[-1])
    whole = lambda shape: pl.BlockSpec(shape, lambda i, z_ref: (0,) * len(shape))
    outs = [((local, width), f32), ((1, width), f32), ((local, width), bf16), ((shards * local, depth), bf16)]
    return pl.pallas_call(
        functools.partial(out_bwd_kernel, shards),
        grid_spec=pltpu.PrefetchScalarGridSpec(
            num_scalar_prefetch=1,
            grid=(1,),
            in_specs=[whole(x.shape) for x in (grad, grad_y, resid, scale, gain, w_out)]
            + [far_out_spec(far, width)],
            out_specs=[whole(shape) for shape, _ in outs],
        ),
        out_shape=[jax.ShapeDtypeStruct(*out) for out in outs],
        cost_estimate=pl.CostEstimate(
            flops=2 * local * width * width, transcendentals=0, bytes_accessed=20 * local * width
        ),
        name="out_backward",
    )(z, grad, grad_y, resid, scale, gain, w_out, far)


def out_terms_kernel(shards, z_ref, mixed, branch, terms):
    term = dot(mixed[...], branch[...], TN).astype(bf16)
    terms[:, 0] = term.reshape(terms.shape[0], terms.shape[2], terms.shape[3])


def out_terms(z, mixed, branch):
    local, width = branch.shape
    shards = mixed.shape[0] // local
    depth = mixed.shape[1]
    piece = depth // SPLIT
    return pl.pallas_call(
        functools.partial(out_terms_kernel, shards),
        grid_spec=pltpu.PrefetchScalarGridSpec(
            num_scalar_prefetch=1,
            grid=(shards,),
            in_specs=[
                pl.BlockSpec((local, depth), lambda r, z_ref: (shard_at(z_ref[0], r, shards), 0)),
                pl.BlockSpec((local, width), lambda r, z_ref: (0, 0)),
            ],
            out_specs=pl.BlockSpec((SPLIT, 1, piece, width), lambda r, z_ref: (0, r, 0, 0)),
        ),
        out_shape=jax.ShapeDtypeStruct((SPLIT, shards, piece, width), bf16),
        cost_estimate=pl.CostEstimate(
            flops=2 * local * width * width, transcendentals=0, bytes_accessed=8 * local * width
        ),
        name="out_terms",
    )(z, mixed, branch)


class Axes:
    def __init__(self, mesh):
        self.n_dp = mesh.shape["dp"]
        self.n_seq = mesh.shape["seq"]
        self.groups = None
        self.across = None
        if self.n_dp > SPLIT:
            self.groups = [[g + i for i in range(SPLIT)] for g in range(0, self.n_dp, SPLIT)]
            self.across = [list(range(i, self.n_dp, SPLIT)) for i in range(SPLIT)]

    def member(self):
        return lax.rem(lax.axis_index("dp"), SPLIT)

    def shift(self, x, r):
        n = self.n_seq
        return lax.ppermute(x, "seq", [(i, (i + r) % n) for i in range(n)])

    def from_others(self, x):
        return [self.shift(x, r) for r in range(1, self.n_seq)]

    def pass_on(self, x):
        n = self.n_seq
        up = down = x
        below, above = [], []
        for step in range(1, n):
            up = lax.ppermute(up, "seq", [(i, i + 1) for i in range(step - 1, n - 1)])
            down = lax.ppermute(down, "seq", [(i + 1, i) for i in range(n - step)])
            below.append(up)
            above.append(down)
        return below + above

    def either(self, came):
        n = self.n_seq
        z = lax.axis_index("seq")
        return [jnp.where(z >= r, came[r - 1], came[2 * n - 2 - r]) for r in range(1, n)]

    def gather_all(self, x):
        if self.groups:
            x = self.gather(lax.all_gather(x, "seq")[None])
        else:
            x = lax.all_gather(x, ("dp", "seq"))
        return x.reshape(SPLIT, self.n_seq, *x.shape[-2:])

    def gather_near(self, x):
        even = jnp.stack([x] + [self.swap(x, bit) for bit in (2, 4, 6)])
        return even, self.swap(even, 1)

    def gather(self, x):
        return lax.all_gather(x, "dp", axis=0, tiled=True, axis_index_groups=self.groups)

    def scatter(self, terms):
        flat = terms.reshape(SPLIT * terms.shape[1], *terms.shape[2:])
        return lax.psum_scatter(
            flat, "dp", scatter_dimension=0, tiled=True, axis_index_groups=self.groups
        )

    def over_groups(self, x):
        return lax.psum(x, "dp", axis_index_groups=self.across) if self.across else x

    def swap(self, x, bit):
        return lax.ppermute(x, "dp", [(i, i ^ bit) for i in range(self.n_dp)])


def after(x, *others):
    return lax.optimization_barrier((x, *others))[0]


class Reduction:
    def __init__(self, axes, mine, theirs):
        self.axes = axes
        member = axes.member()
        self.x = lax.rem(lax.div(member, 2), 2)
        self.y = lax.div(member, 4)
        self.mine = mine.reshape(2, 2, *mine.shape[1:])
        self.state = (axes.swap(theirs, 1),)

    def then(self, *others):
        self.state = lax.optimization_barrier((*self.state, *others))[: len(self.state)]

    def _sum(self, y, x, low, *more):
        def cut(arr):
            shards = arr.shape[2] // 2
            start = [y if y is not None else 0, x if x is not None else 0, 0 if low else shards]
            size = [1 if y is not None else 2, 1 if x is not None else 2, shards]
            rest = arr.ndim - 3
            part = lax.dynamic_slice(arr, start + [0] * rest, size + list(arr.shape[3:]))
            drop = tuple(i for i, at in enumerate((y, x)) if at is not None)
            return lax.squeeze(part, drop).astype(f32)

        total = cut(self.mine) + cut(self.recv)
        for arr in more:
            total = total + arr.astype(f32)
        return total

    def first(self):
        (recv,) = self.state
        self.recv = recv.reshape(self.mine.shape)
        to_x = self._sum(None, 1 - self.x, True).astype(bf16)
        to_y = self._sum(1 - self.y, None, False).astype(bf16)
        self.sent = (to_x, to_y)
        return self

    def send_first(self):
        self.state = (self.axes.swap(self.sent[0], 2), self.axes.swap(self.sent[1], 4))
        return self

    def second(self):
        self.got_x, self.got_y = self.state
        pick = lambda arr, i: lax.dynamic_index_in_dim(arr, i, axis=0, keepdims=False)
        to_y = self._sum(1 - self.y, self.x, True, pick(self.got_x, 1 - self.y)).astype(bf16)
        to_x = self._sum(self.y, 1 - self.x, False, pick(self.got_y, 1 - self.x)).astype(bf16)
        self.sent = (to_x, to_y)
        return self

    def send_second(self):
        self.state = (self.axes.swap(self.sent[1], 4), self.axes.swap(self.sent[0], 2))
        return self

    def third(self):
        got_y, got_x = self.state
        pick = lambda arr, i: lax.dynamic_index_in_dim(arr, i, axis=0, keepdims=False)
        low = self._sum(self.y, self.x, True, pick(self.got_x, self.y), got_y)
        high = self._sum(self.y, self.x, False, pick(self.got_y, self.x), got_x)
        return jnp.concatenate([low, high], axis=0).astype(bf16)


def per_device(
    axes, tokens, lengths, cotangent, w_query, w_key, w_value, w_out, w_gate, w_up, w_down,
    gain_attn, gain_ffn, gain_query, gain_key,
):
    slots, local, width = tokens.shape
    assert slots == 1
    shards = axes.n_seq
    depth = width // shards
    piece = depth // SPLIT
    z = lax.axis_index("seq")
    member = axes.member()
    unit = w_down.shape[0] // CHUNKS
    lanes = width // SPLIT
    head = HD // shards
    weights = (w_query, w_key, w_value)
    columns = [w.shape[1] for w in weights]
    where = jnp.stack([z, lax.rem(member, 2)]).astype(jnp.int32)
    mine = lambda x: lax.dynamic_slice_in_dim(x, member * piece, piece, axis=0)

    def cut(parts):
        return lax.optimization_barrier(tuple(parts[r] for r in range(shards)))

    def cross_back(parts):
        return tuple(axes.shift(parts[r], -r) for r in range(1, shards))

    def add(own, others):
        own = own.astype(f32)
        for arr in others:
            own = own + arr.astype(f32)
        return axes.over_groups(own.astype(bf16))

    def by_owner(parts):
        pick = lambda i: lax.dynamic_index_in_dim(parts, lax.rem(z + shards - i, shards), 0)
        return jnp.concatenate([pick(i) for i in range(shards)], axis=0)

    def total(parts):
        return axes.over_groups(jnp.sum(parts.astype(f32), axis=0).astype(bf16))

    gains = jnp.concatenate([gain_attn, gain_ffn, gain_query, gain_key])
    gains = jnp.pad(gains, (0, piece * 128 - gains.shape[0])).reshape(piece, 128)
    packed = jnp.concatenate([mine(w_query), mine(w_key), mine(w_value), gains], axis=1)
    near = axes.from_others(packed)
    far_qkv = axes.gather(jnp.stack([x[:, :-128] for x in near]))
    far_qkv = far_qkv.reshape(SPLIT, shards - 1, piece, -1)
    gains = jnp.stack([x[:, -128:].reshape(-1) for x in [packed] + near])
    order = lax.rem(z + shards - jnp.arange(shards), shards)
    hot = (order[:, None] == jnp.arange(shards)[None, :]).astype(f32)
    gains = jnp.sum(hot[:, :, None] * gains.astype(f32)[:, None, :], axis=0)

    def gathered_gain(start, size):
        return gains[:, start : start + size].reshape(1, -1)

    gain1 = gathered_gain(0, depth)
    gain2 = gathered_gain(depth, depth)
    gain_q = jnp.tile(gathered_gain(2 * depth, head), (1, 2))
    gain_k = jnp.tile(gathered_gain(2 * depth + head, head), (1, 2))

    first_chunks, last_chunk = pack(member, w_gate, w_up, w_down, w_out)

    def stack_after(parts, *others):
        return jnp.stack([after(x, *others) for x in parts])

    positions = z * local + jnp.arange(local, dtype=jnp.int32)
    cosine, sine = tables(positions)
    valid = (positions < lengths[0])[:, None]
    grad_y = jnp.where(valid, cotangent[0], jnp.zeros((), bf16))
    inputs = tokens[0].astype(f32)
    scale1 = rms_scale(inputs)
    hidden1 = (inputs * scale1 * gain1).astype(bf16)
    hidden1_t = hidden1.T

    def exchange(x):
        return lax.all_to_all(x, "seq", split_axis=0, concat_axis=0, tiled=True)

    crossed = axes.pass_on(after(first_chunks, *near))
    send, raw = qkv_forward(where, hidden1, cosine, sine, gain_q, gain_k, weights, far_qkv)
    far = axes.gather(jnp.stack(axes.either([after(x, send) for x in crossed])))
    qkv = exchange(send)
    crossed = axes.from_others(after(last_chunk, qkv))
    block = 512
    mixed_heads, lse = attend_forward(qkv, block)
    mixed = exchange(after(mixed_heads, *crossed))
    crossed = jnp.stack([after(x, mixed_heads) for x in crossed])
    far_last = axes.gather(crossed)
    mixed = after(mixed, crossed)
    resid, scale2, hidden2, hidden2_t = out_forward(where, mixed, tokens[0], gain2, w_out, far)

    result, grad_hidden2 = resid, resid

    def chunk(c, result, grad_hidden2):
        last = c == CHUNKS - 1
        source, kind = (far_last, 0) if last else (far, 3 * c)
        return ffn_chunk(
            c, kind, last, where, hidden2, hidden2_t, grad_y, w_gate, w_up, w_down, source,
            result, grad_hidden2, valid.astype(f32),
        )

    result, grad_hidden2, terms = chunk(0, result, grad_hidden2)
    sum0 = axes.scatter(terms)
    result, grad_hidden2, terms = chunk(1, result, grad_hidden2)
    sum1 = axes.scatter(terms)
    output, grad_hidden2, *terms = chunk(2, result, grad_hidden2)
    sum2 = Reduction(axes, *terms)

    grad_resid, term_gain2, branch, send = out_backward(
        where, grad_hidden2, grad_y, resid, scale2, gain2, w_out, far
    )
    grad_heads = exchange(send)
    terms_out = out_terms(where, mixed, after(branch, send))
    sum2.then(terms_out)
    sum2.first().send_first()
    parts0 = cut(after(sum0, grad_heads))
    grad_heads = after(grad_heads, terms_out, *sum2.sent, *parts0)
    others0 = cross_back(parts0)
    back = attend_backward(qkv, grad_heads, mixed_heads, lse, block, 0)
    back_rows = [exchange(back)]
    for j in range(1, KV // shards):
        piece0 = add(parts0[0], after(others0, back))
        grad_heads = after(grad_heads, piece0)
        back = attend_backward(qkv, grad_heads, mixed_heads, lse, block, j)
        back_rows.append(exchange(after(back, back_rows[-1])))
    sum2.then(back)
    sum2.second().send_second()
    parts1 = by_owner(after(sum1, back))
    back_rows[-1] = after(back_rows[-1], parts1, *sum2.sent)
    sum_out = axes.scatter(after(terms_out, piece0))
    piece0 = axes.gather(piece0[None])
    parts1 = exchange(after(parts1, back_rows[-1]))
    grad_tokens, terms, other, sum_q, sum_k, term_gain1 = qkv_backward(
        where, hidden1_t, (cosine, sine, gain_q, gain_k), (tokens[0], scale1, gain1, grad_resid),
        back_rows, raw, weights, far_qkv, 128,
    )

    parts = [
        term_gain1.reshape(shards, depth),
        term_gain2.reshape(shards, depth),
        (sum_q[0, :HD] + sum_q[0, HD:]).reshape(shards, head),
        (sum_k[0, :HD] + sum_k[0, HD:]).reshape(shards, head),
    ]
    parts = jnp.concatenate(parts, axis=1)
    parts = jnp.sum(hot[:, :, None] * parts[None], axis=1)
    each = parts.shape[1] // SPLIT
    parts = parts.reshape(shards, SPLIT, each).transpose(1, 0, 2)
    parts = jnp.pad(parts, ((0, 0), (0, 0), (0, piece * 128 - each)))
    parts = parts.reshape(SPLIT // 2, 2, shards, piece, 128).astype(bf16)
    parity = lax.rem(member, 2)
    pick = lambda i: lax.dynamic_index_in_dim(parts, i, axis=1, keepdims=False)
    start = (0, 0, 0, terms.shape[3] - 128)
    terms = lax.dynamic_update_slice(terms, pick(parity), start)
    other = lax.dynamic_update_slice(other, pick(1 - parity), start)
    tail = Reduction(axes, terms, after(other, parts1, *sum2.state))
    parts2 = by_owner(sum2.third())
    tail.then(parts2)
    parts2 = exchange(parts2)
    tail.first().send_first()
    piece1 = total(after(parts1, *tail.sent))
    tail.second().send_second()
    tail.then(parts2)
    tail = by_owner(jnp.concatenate([tail.third(), sum_out], axis=2))
    late = axes.gather(jnp.concatenate([piece1, total(after(parts2, tail))], axis=0)[None])
    grads = unpack_ffn(after(piece0, tail), 0, 1, (), depth, shards, unit, width)
    even, odd = axes.gather_near(after(total(exchange(tail)), *grads))
    grads = unpack_ffn(late, 1, 2, grads, depth, shards, unit, width)
    grad_gate, grad_up, grad_down = grads
    grad_query, grad_key, grad_value, sums, grad_out = unpack_qkv(
        member, even, odd, shards, columns + [128, width]
    )
    sums = sums.reshape(SPLIT, -1)[:, :each].reshape(-1)
    return (
        output[None],
        grad_tokens[None],
        grad_query,
        grad_key,
        grad_value,
        grad_out,
        grad_gate,
        grad_up,
        grad_down,
        sums[:depth],
        sums[depth : 2 * depth],
        sums[2 * depth : 2 * depth + head],
        sums[2 * depth + head :],
    )


def solution(mesh):
    rows = P("seq", None)
    whole = P("dp", "seq", None)
    return jax.shard_map(
        functools.partial(per_device, Axes(mesh)),
        mesh=mesh,
        in_specs=(whole, P("dp"), whole) + (rows,) * 7 + (P("seq"),) * 4,
        out_specs=(whole, whole) + (rows,) * 7 + (P("seq"),) * 4,
        check_vma=False,
    )
```

```python
import functools
import math

import jax
import jax.numpy as jnp
from jax import lax
from jax.experimental import pallas as pl
from jax.experimental.pallas import tpu as pltpu
from jax.sharding import PartitionSpec as P

H = 16
KV = 8
HD = 64
EPS = 1e-05
ROPE_BASE = 1000000.0
LOG2E = math.log2(math.e)
SPLIT = 8
CHUNKS = 3

f32 = jnp.float32
bf16 = jnp.bfloat16
NN = (((1,), (0,)), ((), ()))
NT = (((1,), (1,)), ((), ()))
TN = (((0,), (0,)), ((), ()))


def dot(left, right, dims=NN):
    return lax.dot_general(left, right, dims, preferred_element_type=f32)


def rms_scale(values):
    return lax.rsqrt(jnp.mean(values * values, axis=-1, keepdims=True) + EPS)


def norm_back(grads, normed, scale):
    return scale * (grads - normed * jnp.mean(grads * normed, axis=-1, keepdims=True))


def tables(positions):
    half = HD // 2
    freq = ROPE_BASE ** (-(jnp.arange(half, dtype=f32) * 2.0 / HD))
    angle = positions.astype(f32)[:, None] * freq[None, :]
    cosine, sine = jnp.cos(angle), jnp.sin(angle)
    return jnp.tile(cosine, (1, 4)), jnp.concatenate([-sine, sine, -sine, sine], axis=1)


def lanes_of(x):
    return lax.broadcasted_iota(jnp.int32, x.shape, 1)


def pair_mean(x):
    row = lax.broadcasted_iota(jnp.int32, (2 * HD, 2 * HD), 0)
    same = (row < HD) == (lax.broadcasted_iota(jnp.int32, (2 * HD, 2 * HD), 1) < HD)
    ones = jnp.where(same, 1.0 / HD, 0.0).astype(bf16)
    high = x.astype(bf16)
    return dot(high, ones) + dot((x - high.astype(f32)).astype(bf16), ones)


def other_half(x):
    low = lax.rem(lanes_of(x), HD) < HD // 2
    return jnp.where(low, pltpu.roll(x, 3 * HD // 2, 1), pltpu.roll(x, HD // 2, 1))


def pair_half(x, first):
    lane = lax.broadcasted_iota(jnp.int32, x.shape, 1)
    rolled = pltpu.roll(x.astype(f32), HD, 1).astype(x.dtype)
    return jnp.where((lane < HD) == first, x, rolled)


def stack_pair(x):
    lane = lax.broadcasted_iota(jnp.int32, x.shape, 1)
    zero = jnp.zeros_like(x)
    return jnp.concatenate([jnp.where(lane < HD, x, zero), jnp.where(lane < HD, zero, x)], axis=0)


def causal(probs, block):
    key = lax.broadcasted_iota(jnp.int32, probs.shape, 0)
    query = lax.broadcasted_iota(jnp.int32, probs.shape, 1)
    query = jnp.where(query >= block, query - block, query)
    return jnp.where(key <= query, probs, 0.0)


def attend_fwd_kernel(block, q_ref, k_ref, v_ref, o_ref, lse_ref, keys, values):
    first = pl.program_id(0) % 2 == 0
    i = pl.program_id(1)

    @pl.when(i == 0)
    def _():
        keys[...] = pair_half(k_ref[...], first)
        values[...] = pair_half(v_ref[...], first)

    queries = stack_pair(q_ref[...])

    def tile(t, diagonal):
        rows = pl.ds(t * block, block)
        probs = jnp.exp2(dot(keys[rows, :], queries, NT) * (HD**-0.5 * LOG2E))
        if diagonal:
            probs = causal(probs, block)
        return dot(values[rows, :], probs.astype(bf16), TN), jnp.sum(probs, axis=0, keepdims=True)

    def body(t, carry):
        part, total = tile(t, False)
        return carry[0] + part, carry[1] + total

    mixed, total = lax.fori_loop(0, i, body, tile(i, True))
    mixed = mixed * (1.0 / total)
    pair = jnp.concatenate([mixed[:HD, :block], mixed[HD:, block:]], axis=0)
    o_ref[...] = pair.T.astype(bf16)
    lse_ref[0, 0] = jnp.log2(total)


def attend_forward(qkv, block):
    length, width = qkv.shape
    kv = width // (4 * HD)
    n = length // block
    key_at = lambda j, i: (0, kv + j // 2)
    value_at = lambda j, i: (0, kv + kv // 2 + j // 2)
    return pl.pallas_call(
        functools.partial(attend_fwd_kernel, block),
        grid=(kv, n),
        in_specs=[
            pl.BlockSpec((block, 2 * HD), lambda j, i: (i, j)),
            pl.BlockSpec((length, 2 * HD), key_at),
            pl.BlockSpec((length, 2 * HD), value_at),
        ],
        out_specs=[
            pl.BlockSpec((block, 2 * HD), lambda j, i: (i, j)),
            pl.BlockSpec((1, 1, 1, 2 * block), lambda j, i: (j, i, 0, 0)),
        ],
        out_shape=[
            jax.ShapeDtypeStruct((length, width // 2), bf16),
            jax.ShapeDtypeStruct((kv, n, 1, 2 * block), f32),
        ],
        scratch_shapes=[pltpu.VMEM((length, 2 * HD), bf16), pltpu.VMEM((length, 2 * HD), bf16)],
        cost_estimate=pl.CostEstimate(
            flops=8 * length * length * 2 * HD * kv,
            transcendentals=length * length * kv,
            bytes_accessed=3 * length * width,
        ),
        name="attend_forward",
    )(qkv, qkv, qkv)


def attend_bwd_kernel(
    block, j, q_ref, k_ref, v_ref, g_ref, o_ref, lse_ref, back_ref,
    queries, grads, delta, keys, values, grad_q,
):
    first = j % 2 == 0
    n = q_ref.shape[0] // block
    keys[...] = pair_half(k_ref[...], first)
    values[...] = pair_half(v_ref[...], first)
    for i in range(n):
        rows = slice(i * block, (i + 1) * block)
        g = g_ref[rows, :]
        queries[i] = stack_pair(q_ref[rows, :])
        grads[i] = stack_pair(g)
        both = (g.astype(f32) * o_ref[rows, :].astype(f32)).T
        delta[i] = jnp.concatenate(
            [jnp.sum(both[:HD], axis=0, keepdims=True), jnp.sum(both[HD:], axis=0, keepdims=True)],
            axis=1,
        )
        grad_q[i] = jnp.zeros(grad_q.shape[1:], f32)

    def tile(key, value, key_t, i, diagonal):
        query, grad = queries[i], grads[i]
        probs = jnp.exp2(dot(key, query, NT) * (HD**-0.5 * LOG2E) - lse_ref[0, i])
        if diagonal:
            probs = causal(probs, block)
        grad_probs = dot(value, grad, NT)
        grad_scores = (probs * (grad_probs - delta[i]) * HD**-0.5).astype(bf16)
        grad_q[i] += dot(key_t, grad_scores)
        return dot(grad_scores, query), dot(probs.astype(bf16), grad)

    def step(t, _):
        rows = pl.ds(t * block, block)
        key, value = keys[rows, :], values[rows, :]
        key_t = key.astype(f32).T.astype(bf16)

        def body(i, carry):
            part_k, part_v = tile(key, value, key_t, i, False)
            return carry[0] + part_k, carry[1] + part_v

        part_k, part_v = lax.fori_loop(t + 1, n, body, tile(key, value, key_t, t, True))
        part_k = part_k + pltpu.roll(part_k, HD, 1)
        part_v = part_v + pltpu.roll(part_v, HD, 1)
        both = jnp.where(lanes_of(part_k) < HD, part_k, part_v)
        back_ref[rows, 2 * HD :] = both.astype(bf16)
        return 0

    lax.fori_loop(0, n, step, 0)
    for i in range(n):
        pair = jnp.concatenate([grad_q[i, :HD, :block], grad_q[i, HD:, block:]], axis=0)
        back_ref[i * block : (i + 1) * block, : 2 * HD] = pair.T.astype(bf16)


def attend_backward(qkv, grads, mixed, lse, block, j):
    length, width = qkv.shape
    kv = width // (4 * HD)
    n = length // block
    column = lambda c: pl.BlockSpec((length, 2 * HD), lambda i: (0, c))
    return pl.pallas_call(
        functools.partial(attend_bwd_kernel, block, j),
        grid=(1,),
        in_specs=[
            column(j),
            column(kv + j // 2),
            column(kv + kv // 2 + j // 2),
            column(j),
            column(j),
            pl.BlockSpec((1, n, 1, 2 * block), lambda i: (j, 0, 0, 0)),
        ],
        out_specs=pl.BlockSpec((length, 4 * HD), lambda i: (0, 0)),
        out_shape=jax.ShapeDtypeStruct((length, 4 * HD), bf16),
        scratch_shapes=[
            pltpu.VMEM((n, 2 * block, 2 * HD), bf16),
            pltpu.VMEM((n, 2 * block, 2 * HD), bf16),
            pltpu.VMEM((n, 1, 2 * block), f32),
            pltpu.VMEM((length, 2 * HD), bf16),
            pltpu.VMEM((length, 2 * HD), bf16),
            pltpu.VMEM((n, 2 * HD, 2 * block), f32),
        ],
        cost_estimate=pl.CostEstimate(
            flops=20 * length * length * 2 * HD,
            transcendentals=length * length,
            bytes_accessed=6 * length * 4 * HD,
        ),
        name="attend_backward",
    )(qkv, qkv, qkv, grads, mixed, lse)


def ffn_kernel(
    shards, begins, z_ref, h_ref, ht_ref, gy_ref, own_g, own_u, own_d, far_g, far_u, far_d,
    out_in, grad_in, valid, out_ref, grad_ref, *refs,
):
    terms, (down, total) = refs[:-2], refs[-2:]
    t = pl.program_id(0)
    z = z_ref[0]
    even = z_ref[1] == 0
    rows = own_g.shape[0]
    piece = rows // SPLIT
    unit = own_g.shape[1]
    lanes = down.shape[1] // SPLIT
    blocks = unit // piece

    @pl.when(t == 0)
    def _():
        total[...] = out_in[...]
        grad_ref[...] = jnp.zeros_like(grad_ref) if begins else grad_in[...]
        down[...] = own_d[...]

    @pl.when(t > 0)
    def _():
        for d in range(SPLIT):
            for k in range(blocks):
                down[k * piece : (k + 1) * piece, d * lanes : (d + 1) * lanes] = far_d[
                    d, 0, 0, :, k * lanes : (k + 1) * lanes
                ]

    def shard_of(r):
        return lax.rem(z + shards - r, shards)

    def weight(own, far):
        parts = [own[...]]
        for r in range(1, shards):
            parts.append(far[:, r - 1, 0].reshape(rows, unit))
        return jnp.concatenate(parts, axis=0)

    weight_g, weight_u = weight(own_g, far_g), weight(own_u, far_u)
    gate, up = dot(h_ref[...], weight_g), dot(h_ref[...], weight_u)
    grad_inner = dot(gy_ref[...], down[...], NT)
    sigma = jax.nn.sigmoid(gate)
    active = gate * sigma
    inner = (active * up).astype(bf16)
    grad_g = (grad_inner * up * sigma * (1.0 + gate * (1.0 - sigma))).astype(bf16)
    grad_u = (grad_inner * active).astype(bf16)
    total[...] += dot(inner, down[...])
    grad_ref[...] += dot(grad_g, weight_g, NT) + dot(grad_u, weight_u, NT)
    seg = pl.ds(pl.multiple_of(shard_of(t) * unit, unit), unit)

    def keep(term, at):
        term = term.astype(bf16)
        for r in range(shards):
            part = term[r * rows : (r + 1) * rows]
            if len(terms) == 1:
                terms[0][:, r, at : at + piece, seg] = part.reshape(SPLIT, piece, unit)
                continue
            part = part.reshape(SPLIT // 2, 2, piece, unit)
            mine, theirs = terms
            mine[:, r, at : at + piece, seg] = jnp.where(even, part[:, 0], part[:, 1])
            theirs[:, r, at : at + piece, seg] = jnp.where(even, part[:, 1], part[:, 0])

    keep(dot(ht_ref[...], grad_g), 0)
    keep(dot(ht_ref[...], grad_u), piece)

    @pl.when(t == shards - 1)
    def _():
        out = total[...]
        if out_ref.dtype == bf16:
            out = jnp.where(valid[...] > 0, out, 0.0).astype(bf16)
        out_ref[...] = out

    term = dot(inner, gy_ref[...], TN).astype(bf16)
    for d in range(SPLIT):
        for k in range(blocks):
            part = term[k * piece : (k + 1) * piece, d * lanes : (d + 1) * lanes]
            to = (t, slice(2 * piece, 3 * piece), slice(k * lanes, (k + 1) * lanes))
            if len(terms) == 1:
                terms[0][(d, *to)] = part
            elif d % 2 == 0:
                even_part = part
            else:
                even_part = term[k * piece : (k + 1) * piece, (d - 1) * lanes : d * lanes]
                terms[0][(d // 2, *to)] = jnp.where(even, even_part, part)
                terms[1][(d // 2, *to)] = jnp.where(even, part, even_part)


def ffn_chunk(
    c, kind, parted, z, hidden, hidden_t, grad_y, w_gate, w_up, w_down, far, out_in, grad_in, valid
):
    rows, width = hidden.shape
    shards = width // w_gate.shape[0]
    depth = w_gate.shape[0]
    unit = w_down.shape[0] // CHUNKS
    piece = depth // SPLIT
    n_far = shards - 1
    far = far.reshape(SPLIT, n_far, -1, piece, shards * unit)
    terms = (SPLIT // 2 if parted else SPLIT, shards, 3 * piece, shards * unit)
    n_terms = 2 if parted else 1
    seg = lambda t, z_ref: lax.rem(z_ref[0] + shards - t, shards)
    whole = lambda shape: pl.BlockSpec(shape, lambda t, z_ref: (0,) * len(shape))
    own = pl.BlockSpec((depth, unit), lambda t, z_ref: (0, seg(t, z_ref) * CHUNKS + c))
    gathered = lambda at: pl.BlockSpec(
        (SPLIT, n_far, 1, piece, unit), lambda t, z_ref: (0, 0, at, 0, seg(t, z_ref))
    )
    source = lambda t, z_ref: jnp.maximum(t - 1, 0)
    return pl.pallas_call(
        functools.partial(ffn_kernel, shards, c == 0),
        grid_spec=pltpu.PrefetchScalarGridSpec(
            num_scalar_prefetch=1,
            grid=(shards,),
            in_specs=[
                whole((rows, width)),
                whole((width, rows)),
                whole((rows, width)),
                own,
                own,
                pl.BlockSpec((unit, width), lambda t, z_ref: (c, 0)),
                gathered(kind),
                gathered(kind + 1),
                pl.BlockSpec(
                    (SPLIT, 1, 1, piece, shards * unit),
                    lambda t, z_ref: (0, source(t, z_ref), kind + 2, 0, 0),
                ),
                whole((rows, width)),
                whole((rows, width)),
                whole((rows, 1)),
            ],
            out_specs=[
                whole((rows, width)),
                whole((rows, width)),
            ]
            + [whole(terms)] * n_terms,
            scratch_shapes=[pltpu.VMEM((unit, width), bf16), pltpu.VMEM((rows, width), f32)],
        ),
        out_shape=[
            jax.ShapeDtypeStruct((rows, width), bf16 if c == CHUNKS - 1 else f32),
            jax.ShapeDtypeStruct((rows, width), f32),
        ]
        + [jax.ShapeDtypeStruct(terms, bf16)] * n_terms,
        cost_estimate=pl.CostEstimate(
            flops=18 * rows * width * shards * unit,
            transcendentals=rows * shards * unit,
            bytes_accessed=12 * width * shards * unit + 20 * rows * width,
        ),
        name="ffn_chunk",
    )(z, hidden, hidden_t, grad_y, w_gate, w_up, w_down, far, far, far, out_in, grad_in, valid)


def pack_kernel(m_ref, gate, up, down, out, first_ref, last_ref):
    piece, width = out.shape
    unit = down.shape[0] // CHUNKS
    shards = gate.shape[1] // down.shape[0]
    lanes = down.shape[1]
    for c in range(CHUNKS):
        ref = last_ref if c == CHUNKS - 1 else first_ref
        at = 0 if c == CHUNKS - 1 else 3 * piece * c
        for s in range(shards):
            source = slice((s * CHUNKS + c) * unit, (s * CHUNKS + c + 1) * unit)
            ref[at : at + piece, s * unit : (s + 1) * unit] = gate[:, source]
            ref[at + piece : at + 2 * piece, s * unit : (s + 1) * unit] = up[:, source]
        for k in range(unit // piece):
            rows = slice(c * unit + k * piece, c * unit + (k + 1) * piece)
            ref[at + 2 * piece : at + 3 * piece, k * lanes : (k + 1) * lanes] = down[rows, :]
    at = 3 * piece * (CHUNKS - 1)
    first_ref[at:, :width] = out[...]
    first_ref[at:, width:] = jnp.zeros_like(first_ref[at:, width:])


def pack(member, w_gate, w_up, w_down, w_out):
    depth, width = w_out.shape
    piece = depth // SPLIT
    lanes = width // SPLIT
    line = w_gate.shape[1] // CHUNKS
    rows = lambda w: pl.BlockSpec((piece, w.shape[1]), lambda i, m_ref: (m_ref[0], 0))
    outs = [((3 * CHUNKS - 2) * piece, line), (3 * piece, line)]
    return pl.pallas_call(
        pack_kernel,
        grid_spec=pltpu.PrefetchScalarGridSpec(
            num_scalar_prefetch=1,
            grid=(1,),
            in_specs=[
                rows(w_gate),
                rows(w_up),
                pl.BlockSpec((w_down.shape[0], lanes), lambda i, m_ref: (0, m_ref[0])),
                rows(w_out),
            ],
            out_specs=[pl.BlockSpec(shape, lambda i, m_ref: (0, 0)) for shape in outs],
        ),
        out_shape=[jax.ShapeDtypeStruct(shape, bf16) for shape in outs],
        name="pack",
    )(member.reshape(1), w_gate, w_up, w_down, w_out)


def unpack_kernel(source, *refs):
    gate_ref, up_ref, down_ref = refs[-3:]
    piece = source.shape[2]
    lanes = down_ref.shape[1] // SPLIT
    blocks = down_ref.shape[0] // piece
    gate_ref[...] = source[:, 0].astype(f32).reshape(gate_ref.shape)
    up_ref[...] = source[:, 1].astype(f32).reshape(up_ref.shape)
    for d in range(SPLIT):
        for k in range(blocks):
            down_ref[k * piece : (k + 1) * piece, d * lanes : (d + 1) * lanes] = source[
                d, 2, :, k * lanes : (k + 1) * lanes
            ].astype(f32)


def unpack_ffn(source, first, count, before, depth, shards, unit, width):
    piece = depth // SPLIT
    source = source.reshape(SPLIT, -1, piece, shards * unit)
    rows = unit // shards
    columns = pl.BlockSpec((depth, unit), lambda c, s: (0, s * CHUNKS + first + c))
    return pl.pallas_call(
        unpack_kernel,
        grid=(count, shards),
        in_specs=[pl.BlockSpec((SPLIT, 3, piece, unit), lambda c, s: (0, c, 0, s))]
        + [pl.BlockSpec(memory_space=pl.ANY)] * len(before),
        out_specs=[
            columns,
            columns,
            pl.BlockSpec((rows, width), lambda c, s: ((first + c) * shards + s, 0)),
        ],
        out_shape=[
            jax.ShapeDtypeStruct((depth, shards * CHUNKS * unit), f32),
            jax.ShapeDtypeStruct((depth, shards * CHUNKS * unit), f32),
            jax.ShapeDtypeStruct((CHUNKS * unit, width), f32),
        ],
        input_output_aliases={i + 1: i for i in range(len(before))},
        name="unpack_ffn",
    )(source, *before)


def unpack_near_kernel(m_ref, even, odd, *refs):
    gate_ref, up_ref, down_ref = refs[-3:]
    piece = gate_ref.shape[0] // SPLIT
    lanes = down_ref.shape[1] // SPLIT
    blocks = down_ref.shape[0] // piece
    for b in range(SPLIT):
        source = (odd if b % 2 else even)[b // 2].astype(f32)
        member = jnp.bitwise_xor(m_ref[0], b)
        rows = pl.ds(pl.multiple_of(member * piece, piece), piece)
        gate_ref[rows, :] = source[:piece]
        up_ref[rows, :] = source[piece : 2 * piece]
        columns = pl.ds(pl.multiple_of(member * lanes, lanes), lanes)
        for k in range(blocks):
            down_ref[k * piece : (k + 1) * piece, columns] = source[
                2 * piece :, k * lanes : (k + 1) * lanes
            ]


def unpack_near(member, even, odd, chunk, before, shards):
    gate, _, down = before
    unit = gate.shape[1] // (shards * CHUNKS)
    columns = pl.BlockSpec((gate.shape[0], unit), lambda s, m_ref: (0, s * CHUNKS + chunk))
    source = pl.BlockSpec((SPLIT // 2, even.shape[1], unit), lambda s, m_ref: (0, 0, s))
    rows = down.shape[0] // (CHUNKS * shards)
    return pl.pallas_call(
        unpack_near_kernel,
        grid_spec=pltpu.PrefetchScalarGridSpec(
            num_scalar_prefetch=1,
            grid=(shards,),
            in_specs=[source, source] + [pl.BlockSpec(memory_space=pl.ANY)] * 3,
            out_specs=[
                columns,
                columns,
                pl.BlockSpec((rows, down.shape[1]), lambda s, m_ref: (chunk * shards + s, 0)),
            ],
        ),
        out_shape=[jax.ShapeDtypeStruct(x.shape, f32) for x in before],
        input_output_aliases={3 + i: i for i in range(3)},
        name="unpack_near",
    )(member.reshape(1), even, odd, *before)


def shard_at(z, r, shards):
    return lax.rem(z + shards - r, shards)


def part_of(z, r, shards, size):
    return pl.ds(pl.multiple_of(shard_at(z, r, shards) * size, size), size)


def joined(own, far, r):
    return own[...] if r == 0 else far[:, r - 1].reshape(own.shape)


def qkv_fwd_kernel(
    shards, z_ref, h_ref, cos_ref, sin_ref, gain_q, gain_k, *refs
):
    own, far, (send_ref, raw_ref) = refs[:3], refs[3:6], refs[6:]
    z = z_ref[0]
    depth = own[0].shape[0]
    total = [None] * 3
    for r in range(shards):
        left = h_ref[:, part_of(z, r, shards, depth)]
        for i in range(3):
            part = dot(left, joined(own[i], far[i], r))
            total[i] = part if r == 0 else total[i] + part
    cosine, sine = cos_ref[...], sin_ref[...]
    at = 0
    for values, gain in ((total[0], gain_q), (total[1], gain_k)):
        for i in range(0, values.shape[1], 2 * HD):
            pair = values[:, i : i + 2 * HD]
            raw_ref[:, at : at + 2 * HD] = pair
            scaled = pair * lax.rsqrt(pair_mean(pair * pair) + EPS) * gain[...]
            rotated = scaled * cosine + other_half(scaled) * sine
            send_ref[:, at : at + 2 * HD] = rotated.astype(bf16)
            at += 2 * HD
    send_ref[:, at:] = total[2].astype(bf16)


def projection_specs(shards, depth, piece, columns):
    sizes = [n // shards for n in columns]
    last = lambda s: jnp.minimum(s, shards - 1)
    own = [pl.BlockSpec((depth, n), lambda s, z_ref: (0, last(s))) for n in sizes]
    starts = [sum(columns[:i]) // sizes[i] for i in range(3)]
    far = [
        pl.BlockSpec(
            (SPLIT, shards - 1, piece, n), lambda s, z_ref, start=start: (0, 0, 0, start + last(s))
        )
        for n, start in zip(sizes, starts)
    ]
    return own + far


def qkv_forward(z, hidden, cosine, sine, gain_q, gain_k, weights, far):
    local, width = hidden.shape
    depth = weights[0].shape[0]
    shards = width // depth
    columns = [w.shape[1] for w in weights]
    each = sum(columns) // shards
    raw = each - columns[2] // shards
    whole = lambda x: pl.BlockSpec(x.shape, lambda s, z_ref: (0,) * x.ndim)
    return pl.pallas_call(
        functools.partial(qkv_fwd_kernel, shards),
        grid_spec=pltpu.PrefetchScalarGridSpec(
            num_scalar_prefetch=1,
            grid=(shards,),
            in_specs=[whole(x) for x in (hidden, cosine, sine, gain_q, gain_k)]
            + projection_specs(shards, depth, far.shape[2], columns),
            out_specs=[
                pl.BlockSpec((local, each), lambda s, z_ref: (s, 0)),
                pl.BlockSpec((local, raw), lambda s, z_ref: (s, 0)),
            ],
        ),
        out_shape=[
            jax.ShapeDtypeStruct((shards * local, each), bf16),
            jax.ShapeDtypeStruct((shards * local, raw), f32),
        ],
        cost_estimate=pl.CostEstimate(
            flops=2 * local * width * sum(columns),
            transcendentals=0,
            bytes_accessed=2 * width * sum(columns) + 8 * local * sum(columns),
        ),
        name="qkv_forward",
    )(z, hidden, cosine, sine, gain_q, gain_k, *weights, far, far, far)


def qkv_bwd_kernel(
    shards, heads, z_ref, ht_ref, cos_ref, sin_ref, gain_q, gain_k,
    tokens, scale_ref, gain_1, resid, sum_2, raw_ref, *refs,
):
    back, refs = refs[:heads], refs[heads:]
    own, far, (tokens_ref, mine, theirs), refs = refs[:3], refs[3:6], refs[6:9], refs[9:]
    sum_q, sum_k, grads, grad_ref = refs
    step = pl.program_id(0)
    z = z_ref[0]
    even = z_ref[1] == 0
    depth = own[0].shape[0]
    piece = depth // SPLIT

    @pl.when(step == 0)
    def _():
        grad_ref[...] = jnp.zeros_like(grad_ref)
        sum_q[...] = jnp.zeros_like(sum_q)
        sum_k[...] = jnp.zeros_like(sum_k)

    @pl.when(step < shards)
    def _():
        cosine, sine = cos_ref[...], sin_ref[...]
        at = 0
        halves = [ref[:, 2 * HD :] for ref in back]
        swapped = [pltpu.roll(half.astype(f32), HD, 1).astype(bf16) for half in halves]
        low = lanes_of(halves[0]) < HD
        arrived = [[ref[:, : 2 * HD] for ref in back]]
        arrived.append([jnp.where(low, halves[i], swapped[i + 1]) for i in range(0, heads, 2)])
        arrived.append([jnp.where(low, swapped[i], halves[i + 1]) for i in range(0, heads, 2)])
        for pairs, gain, total in ((arrived[0], gain_q, sum_q), (arrived[1], gain_k, sum_k)):
            for grad in pairs:
                pair = raw_ref[:, at : at + 2 * HD]
                scale = lax.rsqrt(pair_mean(pair * pair) + EPS)
                hat = pair * scale
                grad = grad.astype(f32)
                grad = grad * cosine + other_half(grad * sine)
                total[...] += jnp.sum(grad * hat, axis=0, keepdims=True)
                grad = grad * gain[...]
                grads[:, at : at + 2 * HD] = (scale * (grad - hat * pair_mean(grad * hat))).astype(bf16)
                at += 2 * HD
        for i, pair in enumerate(arrived[2]):
            grads[:, at + i * 2 * HD : at + (i + 1) * 2 * HD] = pair
        ends = (0, own[0].shape[1], at, grads.shape[1])
        for r in range(shards):
            part = None
            for i in range(3):
                one = dot(grads[:, ends[i] : ends[i + 1]], joined(own[i], far[i], r), NT)
                part = one if i == 0 else part + one
            grad_ref[:, part_of(z, r, shards, depth)] += part
            term = dot(ht_ref[part_of(z, r, shards, depth), :], grads[...]).astype(bf16)
            term = term.reshape(SPLIT // 2, 2, piece, term.shape[1])
            mine[:, r] = jnp.where(even, term[:, 0], term[:, 1])
            theirs[:, r] = jnp.where(even, term[:, 1], term[:, 0])

    @pl.when(step == shards)
    def _():
        scale = scale_ref[...]
        normed = tokens[...].astype(f32) * scale
        grad = grad_ref[...]
        sum_1 = jnp.sum(grad * normed, axis=0, keepdims=True)
        tokens_ref[...] = resid[...] + norm_back(grad * gain_1[...], normed, scale)
        lanes = 2 * HD
        empty = jnp.zeros((piece, mine.shape[3] - lanes), f32)
        turn = [shard_at(z, r, shards) for r in range(shards)]
        grad_ref[0:1, :] = sum_1
        grad_ref[1:2, :] = sum_2[...]
        for r in range(shards):
            rows = []
            for i in range(2):
                for k in range(0, depth, lanes):
                    at = pl.multiple_of(turn[r] * depth + k, lanes)
                    rows.append(grad_ref[i : i + 1, pl.ds(at, lanes)])
            rows += [sum_q[...], sum_k[...]]
            rows.append(jnp.zeros((piece - len(rows), lanes), f32))
            block = jnp.concatenate([jnp.concatenate(rows, axis=0), empty], axis=1).astype(bf16)
            for d in range(SPLIT // 2):
                mine[d, r] = block
                theirs[d, r] = block


def qkv_backward(z, hidden_t, tables_gains, first_norm, back, raw, weights, far):
    width, local = hidden_t.shape
    depth = weights[0].shape[0]
    shards = width // depth
    piece = depth // SPLIT
    columns = [w.shape[1] for w in weights]
    each = sum(columns) // shards
    whole = lambda shape: pl.BlockSpec(shape, lambda s, z_ref: (0,) * len(shape))
    last = lambda s: jnp.minimum(s, shards - 1)
    rows = lambda x: pl.BlockSpec((local, x.shape[1]), lambda s, z_ref: (last(s), 0))
    terms = jax.ShapeDtypeStruct((SPLIT // 2, shards, piece, shards * each + 2 * HD), bf16)
    at_terms = pl.BlockSpec((SPLIT // 2, shards, piece, each), lambda s, z_ref: (0, 0, 0, s))
    return pl.pallas_call(
        functools.partial(qkv_bwd_kernel, shards, len(back)),
        grid_spec=pltpu.PrefetchScalarGridSpec(
            num_scalar_prefetch=1,
            grid=(shards + 1,),
            in_specs=[whole(x.shape) for x in (hidden_t, *tables_gains, *first_norm)]
            + [rows(x) for x in (raw, *back)]
            + projection_specs(shards, depth, piece, columns),
            out_specs=[whole((local, width)), at_terms, at_terms],
            scratch_shapes=[
                pltpu.VMEM((1, 2 * HD), f32),
                pltpu.VMEM((1, 2 * HD), f32),
                pltpu.VMEM((local, each), bf16),
                pltpu.VMEM((local, width), f32),
            ],
        ),
        out_shape=[jax.ShapeDtypeStruct((local, width), f32), terms, terms],
        cost_estimate=pl.CostEstimate(
            flops=4 * local * width * sum(columns),
            transcendentals=0,
            bytes_accessed=4 * width * sum(columns) + 8 * local * sum(columns),
        ),
        name="qkv_backward",
    )(z, hidden_t, *tables_gains, *first_norm, raw, *back, *weights, far, far, far)


def unpack_qkv_kernel(shards, m_ref, even, odd, *refs):
    piece = even.shape[1]
    out = refs[3]
    for b in range(SPLIT):
        source = (odd if b % 2 else even)[b // 2].astype(f32)
        rows = pl.ds(pl.multiple_of(jnp.bitwise_xor(m_ref[0], b) * piece, piece), piece)
        at = 0
        for s in range(shards):
            for ref in refs[:3]:
                n = ref.shape[1] // shards
                ref[rows, s * n : (s + 1) * n] = source[:, at : at + n]
                at += n
        out[rows, :] = source[:, source.shape[1] - out.shape[1] :]


def unpack_qkv(member, even, odd, shards, columns, width):
    piece = even.shape[1]
    columns = columns + [width]
    whole = lambda shape: pl.BlockSpec(shape, lambda i, m_ref: (0,) * len(shape))
    return pl.pallas_call(
        functools.partial(unpack_qkv_kernel, shards),
        grid_spec=pltpu.PrefetchScalarGridSpec(
            num_scalar_prefetch=1,
            grid=(1,),
            in_specs=[whole(even.shape), whole(odd.shape)],
            out_specs=[whole((SPLIT * piece, n)) for n in columns],
        ),
        out_shape=[jax.ShapeDtypeStruct((SPLIT * piece, n), f32) for n in columns],
        name="unpack_qkv",
    )(member.reshape(1), even, odd)


def out_fwd_kernel(shards, z_ref, mixed, tokens, gain, own, far, resid_ref, scale_ref, h_ref, ht_ref):
    z = z_ref[0]
    local = tokens.shape[0]
    resid = tokens[...].astype(f32)
    for r in range(shards):
        weight = own[...] if r == 0 else far[:, r - 1, 0].reshape(own.shape)
        resid = resid + dot(mixed[part_of(z, r, shards, local), :], weight)
    scale = rms_scale(resid)
    hidden = resid * scale * gain[...]
    resid_ref[...] = resid
    scale_ref[...] = scale
    turned = hidden.T.astype(bf16)
    low = hidden.astype(bf16)
    depth = own.shape[0]
    for s in range(shards):
        at = part_of(z, s, shards, depth)
        h_ref[:, at] = low[:, s * depth : (s + 1) * depth]
        ht_ref[at, :] = turned[s * depth : (s + 1) * depth]


def far_out_spec(far, width):
    size = (SPLIT, far.shape[1], 1, far.shape[3], width)
    return pl.BlockSpec(size, lambda i, z_ref: (0, 0, far.shape[2] - 1, 0, 0))


def out_forward(z, mixed, tokens, gain, w_out, far):
    local, width = tokens.shape
    shards = mixed.shape[0] // local
    piece = w_out.shape[0] // SPLIT
    far = far.reshape(SPLIT, shards - 1, -1, piece, far.shape[-1])
    whole = lambda shape: pl.BlockSpec(shape, lambda i, z_ref: (0,) * len(shape))
    outs = [((local, width), f32), ((local, 1), f32), ((local, width), bf16), ((width, local), bf16)]
    return pl.pallas_call(
        functools.partial(out_fwd_kernel, shards),
        grid_spec=pltpu.PrefetchScalarGridSpec(
            num_scalar_prefetch=1,
            grid=(1,),
            in_specs=[whole(x.shape) for x in (mixed, tokens, gain, w_out)]
            + [far_out_spec(far, width)],
            out_specs=[whole(shape) for shape, _ in outs],
        ),
        out_shape=[jax.ShapeDtypeStruct(*out) for out in outs],
        cost_estimate=pl.CostEstimate(
            flops=2 * local * width * width, transcendentals=0, bytes_accessed=14 * local * width
        ),
        name="out_forward",
    )(z, mixed, tokens, gain, w_out, far)


def out_bwd_kernel(
    shards, z_ref, grad, grad_y, resid, scale_ref, gain, own, far, grad_resid, sum_ref, branch, send
):
    z = z_ref[0]
    local = grad.shape[0]
    scale = scale_ref[...]
    normed = resid[...] * scale
    depth = own.shape[0]
    parts = [grad[:, part_of(z, s, shards, depth)] for s in range(shards)]
    come = jnp.concatenate(parts, axis=1)
    sum_ref[...] = jnp.sum(come * normed, axis=0, keepdims=True)
    total = grad_y[...].astype(f32) + norm_back(come * gain[...], normed, scale)
    grad_resid[...] = total
    low = total.astype(bf16)
    branch[...] = low
    for r in range(shards):
        weight = own[...] if r == 0 else far[:, r - 1, 0].reshape(own.shape)
        send[part_of(z, r, shards, local), :] = dot(low, weight, NT).astype(bf16)


def out_backward(z, grad, grad_y, resid, scale, gain, w_out, far):
    local, width = grad.shape
    depth = w_out.shape[0]
    shards = width // depth
    piece = depth // SPLIT
    far = far.reshape(SPLIT, shards - 1, -1, piece, far.shape[-1])
    whole = lambda shape: pl.BlockSpec(shape, lambda i, z_ref: (0,) * len(shape))
    outs = [((local, width), f32), ((1, width), f32), ((local, width), bf16), ((shards * local, depth), bf16)]
    return pl.pallas_call(
        functools.partial(out_bwd_kernel, shards),
        grid_spec=pltpu.PrefetchScalarGridSpec(
            num_scalar_prefetch=1,
            grid=(1,),
            in_specs=[whole(x.shape) for x in (grad, grad_y, resid, scale, gain, w_out)]
            + [far_out_spec(far, width)],
            out_specs=[whole(shape) for shape, _ in outs],
        ),
        out_shape=[jax.ShapeDtypeStruct(*out) for out in outs],
        cost_estimate=pl.CostEstimate(
            flops=2 * local * width * width, transcendentals=0, bytes_accessed=20 * local * width
        ),
        name="out_backward",
    )(z, grad, grad_y, resid, scale, gain, w_out, far)


def out_terms_kernel(shards, z_ref, mixed, branch, terms):
    term = dot(mixed[...], branch[...], TN).astype(bf16)
    terms[:, 0] = term.reshape(terms.shape[0], terms.shape[2], terms.shape[3])


def out_terms(z, mixed, branch):
    local, width = branch.shape
    shards = mixed.shape[0] // local
    depth = mixed.shape[1]
    piece = depth // SPLIT
    return pl.pallas_call(
        functools.partial(out_terms_kernel, shards),
        grid_spec=pltpu.PrefetchScalarGridSpec(
            num_scalar_prefetch=1,
            grid=(shards,),
            in_specs=[
                pl.BlockSpec((local, depth), lambda r, z_ref: (shard_at(z_ref[0], r, shards), 0)),
                pl.BlockSpec((local, width), lambda r, z_ref: (0, 0)),
            ],
            out_specs=pl.BlockSpec((SPLIT, 1, piece, width), lambda r, z_ref: (0, r, 0, 0)),
        ),
        out_shape=jax.ShapeDtypeStruct((SPLIT, shards, piece, width), bf16),
        cost_estimate=pl.CostEstimate(
            flops=2 * local * width * width, transcendentals=0, bytes_accessed=8 * local * width
        ),
        name="out_terms",
    )(z, mixed, branch)


class Axes:
    def __init__(self, mesh):
        self.n_dp = mesh.shape["dp"]
        self.n_seq = mesh.shape["seq"]
        self.groups = None
        self.across = None
        if self.n_dp > SPLIT:
            self.groups = [[g + i for i in range(SPLIT)] for g in range(0, self.n_dp, SPLIT)]
            self.across = [list(range(i, self.n_dp, SPLIT)) for i in range(SPLIT)]

    def member(self):
        return lax.rem(lax.axis_index("dp"), SPLIT)

    def shift(self, x, r):
        n = self.n_seq
        return lax.ppermute(x, "seq", [(i, (i + r) % n) for i in range(n)])

    def from_others(self, x):
        return [self.shift(x, r) for r in range(1, self.n_seq)]

    def pass_on(self, x):
        n = self.n_seq
        up = down = x
        below, above = [], []
        for step in range(1, n):
            up = lax.ppermute(up, "seq", [(i, i + 1) for i in range(step - 1, n - 1)])
            down = lax.ppermute(down, "seq", [(i + 1, i) for i in range(n - step)])
            below.append(up)
            above.append(down)
        return below + above

    def either(self, came):
        n = self.n_seq
        z = lax.axis_index("seq")
        return [jnp.where(z >= r, came[r - 1], came[2 * n - 2 - r]) for r in range(1, n)]

    def gather_all(self, x):
        if self.groups:
            x = self.gather(lax.all_gather(x, "seq")[None])
        else:
            x = lax.all_gather(x, ("dp", "seq"))
        return x.reshape(SPLIT, self.n_seq, *x.shape[-2:])

    def gather_near(self, x, *others):
        even = jnp.stack([after(y, *others) for y in [x] + [self.swap(x, bit) for bit in (2, 4, 6)]])
        return even, self.swap(even, 1)

    def gather(self, x):
        return lax.all_gather(x, "dp", axis=0, tiled=True, axis_index_groups=self.groups)

    def scatter(self, terms):
        flat = terms.reshape(SPLIT * terms.shape[1], *terms.shape[2:])
        return lax.psum_scatter(
            flat, "dp", scatter_dimension=0, tiled=True, axis_index_groups=self.groups
        )

    def over_groups(self, x):
        return lax.psum(x, "dp", axis_index_groups=self.across) if self.across else x

    def swap(self, x, bit):
        return lax.ppermute(x, "dp", [(i, i ^ bit) for i in range(self.n_dp)])


def after(x, *others):
    return lax.optimization_barrier((x, *others))[0]


class Reduction:
    def __init__(self, axes, mine, theirs):
        self.axes = axes
        member = axes.member()
        self.x = lax.rem(lax.div(member, 2), 2)
        self.y = lax.div(member, 4)
        self.mine = mine.reshape(2, 2, *mine.shape[1:])
        self.state = (axes.swap(theirs, 1),)

    def then(self, *others):
        self.state = lax.optimization_barrier((*self.state, *others))[: len(self.state)]

    def _sum(self, y, x, low, *more):
        def cut(arr):
            shards = arr.shape[2] // 2
            start = [y if y is not None else 0, x if x is not None else 0, 0 if low else shards]
            size = [1 if y is not None else 2, 1 if x is not None else 2, shards]
            rest = arr.ndim - 3
            part = lax.dynamic_slice(arr, start + [0] * rest, size + list(arr.shape[3:]))
            drop = tuple(i for i, at in enumerate((y, x)) if at is not None)
            return lax.squeeze(part, drop).astype(f32)

        total = cut(self.mine) + cut(self.recv)
        for arr in more:
            total = total + arr.astype(f32)
        return total

    def first(self):
        (recv,) = self.state
        self.recv = recv.reshape(self.mine.shape)
        to_x = self._sum(None, 1 - self.x, True).astype(bf16)
        to_y = self._sum(1 - self.y, None, False).astype(bf16)
        self.sent = (to_x, to_y)
        return self

    def send_first(self):
        self.state = (self.axes.swap(self.sent[0], 2), self.axes.swap(self.sent[1], 4))
        return self

    def second(self):
        self.got_x, self.got_y = self.state
        pick = lambda arr, i: lax.dynamic_index_in_dim(arr, i, axis=0, keepdims=False)
        to_y = self._sum(1 - self.y, self.x, True, pick(self.got_x, 1 - self.y)).astype(bf16)
        to_x = self._sum(self.y, 1 - self.x, False, pick(self.got_y, 1 - self.x)).astype(bf16)
        self.sent = (to_x, to_y)
        return self

    def send_second(self):
        self.state = (self.axes.swap(self.sent[1], 4), self.axes.swap(self.sent[0], 2))
        return self

    def third(self):
        got_y, got_x = self.state
        pick = lambda arr, i: lax.dynamic_index_in_dim(arr, i, axis=0, keepdims=False)
        low = self._sum(self.y, self.x, True, pick(self.got_x, self.y), got_y)
        high = self._sum(self.y, self.x, False, pick(self.got_y, self.x), got_x)
        return jnp.concatenate([low, high], axis=0).astype(bf16)


def per_device(
    axes, tokens, lengths, cotangent, w_query, w_key, w_value, w_out, w_gate, w_up, w_down,
    gain_attn, gain_ffn, gain_query, gain_key,
):
    slots, local, width = tokens.shape
    assert slots == 1
    shards = axes.n_seq
    depth = width // shards
    piece = depth // SPLIT
    z = lax.axis_index("seq")
    member = axes.member()
    unit = w_down.shape[0] // CHUNKS
    lanes = width // SPLIT
    head = HD // shards
    weights = (w_query, w_key, w_value)
    columns = [w.shape[1] for w in weights]
    where = jnp.stack([z, lax.rem(member, 2)]).astype(jnp.int32)
    mine = lambda x: lax.dynamic_slice_in_dim(x, member * piece, piece, axis=0)

    def cut(parts):
        return lax.optimization_barrier(tuple(parts[r] for r in range(shards)))

    def cross_back(parts):
        return tuple(axes.shift(parts[r], -r) for r in range(1, shards))

    def add(own, others):
        own = own.astype(f32)
        for arr in others:
            own = own + arr.astype(f32)
        return axes.over_groups(own.astype(bf16))

    def by_owner(parts):
        pick = lambda i: lax.dynamic_index_in_dim(parts, lax.rem(z + shards - i, shards), 0)
        return jnp.concatenate([pick(i) for i in range(shards)], axis=0)

    def total(parts):
        return axes.over_groups(jnp.sum(parts.astype(f32), axis=0).astype(bf16))

    gains = jnp.concatenate([gain_attn, gain_ffn, gain_query, gain_key])
    gains = jnp.pad(gains, (0, piece * 128 - gains.shape[0])).reshape(piece, 128)
    packed = jnp.concatenate([mine(w_query), mine(w_key), mine(w_value), gains], axis=1)
    near = axes.from_others(packed)
    far_qkv = axes.gather(jnp.stack([x[:, :-128] for x in near]))
    far_qkv = far_qkv.reshape(SPLIT, shards - 1, piece, -1)
    gains = jnp.stack([x[:, -128:].reshape(-1) for x in [packed] + near])
    order = lax.rem(z + shards - jnp.arange(shards), shards)
    hot = (order[:, None] == jnp.arange(shards)[None, :]).astype(f32)
    gains = jnp.sum(hot[:, :, None] * gains.astype(f32)[:, None, :], axis=0)

    def gathered_gain(start, size):
        return gains[:, start : start + size].reshape(1, -1)

    gain1 = gathered_gain(0, depth)
    gain2 = gathered_gain(depth, depth)
    gain_q = jnp.tile(gathered_gain(2 * depth, head), (1, 2))
    gain_k = jnp.tile(gathered_gain(2 * depth + head, head), (1, 2))

    first_chunks, last_chunk = pack(member, w_gate, w_up, w_down, w_out)

    def stack_after(parts, *others):
        return jnp.stack([after(x, *others) for x in parts])

    positions = z * local + jnp.arange(local, dtype=jnp.int32)
    cosine, sine = tables(positions)
    valid = (positions < lengths[0])[:, None]
    grad_y = jnp.where(valid, cotangent[0], jnp.zeros((), bf16))
    inputs = tokens[0].astype(f32)
    scale1 = rms_scale(inputs)
    hidden1 = (inputs * scale1 * gain1).astype(bf16)
    hidden1_t = hidden1.T

    def exchange(x):
        return lax.all_to_all(x, "seq", split_axis=0, concat_axis=0, tiled=True)

    crossed = axes.pass_on(after(first_chunks, *near))
    send, raw = qkv_forward(where, hidden1, cosine, sine, gain_q, gain_k, weights, far_qkv)
    far = axes.gather(jnp.stack(axes.either([after(x, send) for x in crossed])))
    qkv = exchange(send)
    crossed = axes.from_others(after(last_chunk, qkv))
    block = 512
    mixed_heads, lse = attend_forward(qkv, block)
    mixed = exchange(after(mixed_heads, *crossed))
    crossed = jnp.stack([after(x, mixed_heads) for x in crossed])
    far_last = axes.gather(crossed)
    mixed = after(mixed, crossed)
    resid, scale2, hidden2, hidden2_t = out_forward(where, mixed, tokens[0], gain2, w_out, far)

    result, grad_hidden2 = resid, resid

    def chunk(c, result, grad_hidden2):
        last = c == CHUNKS - 1
        source, kind = (far_last, 0) if last else (far, 3 * c)
        return ffn_chunk(
            c, kind, last, where, hidden2, hidden2_t, grad_y, w_gate, w_up, w_down, source,
            result, grad_hidden2, valid.astype(f32),
        )

    result, grad_hidden2, terms = chunk(0, result, grad_hidden2)
    sum0 = axes.scatter(terms)
    result, grad_hidden2, terms = chunk(1, result, grad_hidden2)
    sum1 = axes.scatter(terms)
    output, grad_hidden2, *terms = chunk(2, result, grad_hidden2)
    sum2 = Reduction(axes, *terms)

    grad_resid, term_gain2, branch, send = out_backward(
        where, grad_hidden2, grad_y, resid, scale2, gain2, w_out, far
    )
    grad_heads = exchange(send)
    terms_out = out_terms(where, mixed, after(branch, send))
    sum2.then(terms_out)
    sum2.first().send_first()
    parts0 = cut(after(sum0, grad_heads))
    grad_heads = after(grad_heads, terms_out, *sum2.sent, *parts0)
    others0 = cross_back(parts0)
    back = attend_backward(qkv, grad_heads, mixed_heads, lse, block, 0)
    back_rows = [exchange(back)]
    for j in range(1, KV // shards):
        piece0 = add(parts0[0], after(others0, back))
        grad_heads = after(grad_heads, piece0)
        back = attend_backward(qkv, grad_heads, mixed_heads, lse, block, j)
        back_rows.append(exchange(after(back, back_rows[-1])))
    sum2.then(back)
    sum2.second().send_second()
    parts1 = by_owner(after(sum1, back))
    back_rows[-1] = after(back_rows[-1], parts1, *sum2.sent)
    sum_out = axes.scatter(after(terms_out, piece0))
    piece0 = axes.gather(piece0[None])
    parts1 = exchange(after(parts1, back_rows[-1]))
    grad_tokens, terms, other = qkv_backward(
        where, hidden1_t, (cosine, sine, gain_q, gain_k),
        (tokens[0], scale1, gain1, grad_resid, term_gain2), back_rows, raw, weights, far_qkv,
    )
    tail = Reduction(axes, terms, after(other, parts1, *sum2.state))
    parts2 = by_owner(sum2.third())
    tail.then(parts2)
    parts2 = exchange(parts2)
    tail.first().send_first()
    piece1 = axes.gather(total(after(parts1, *tail.sent))[None])
    tail.second().send_second()
    tail.then(parts2)
    tail = by_owner(jnp.concatenate([tail.third(), sum_out], axis=2))
    late = total(after(parts2, tail))
    grads = unpack_ffn(after(piece0, tail), 0, 1, (), depth, shards, unit, width)
    tail = total(after(exchange(tail), *grads))
    even, odd = axes.gather_near(tail)
    late = axes.gather_near(late, tail)
    grads = unpack_ffn(piece1, 1, 1, grads, depth, shards, unit, width)
    grads = unpack_near(member, *late, CHUNKS - 1, grads, shards)
    grad_gate, grad_up, grad_down = grads
    grad_query, grad_key, grad_value, grad_out = unpack_qkv(
        member, even, odd, shards, columns, width
    )
    sums = even[0, :, sum(columns) : sum(columns) + 2 * HD].astype(f32)
    n = depth // (2 * HD)
    sum_1, sum_2 = sums[:n].reshape(depth), sums[n : 2 * n].reshape(depth)
    heads = [sums[i, :HD] + sums[i, HD:] for i in (2 * n, 2 * n + 1)]
    sum_q, sum_k = (lax.dynamic_slice_in_dim(x, z * head, head) for x in heads)
    return (
        output[None],
        grad_tokens[None],
        grad_query,
        grad_key,
        grad_value,
        grad_out,
        grad_gate,
        grad_up,
        grad_down,
        sum_1,
        sum_2,
        sum_q,
        sum_k,
    )


def solution(mesh):
    rows = P("seq", None)
    whole = P("dp", "seq", None)
    return jax.shard_map(
        functools.partial(per_device, Axes(mesh)),
        mesh=mesh,
        in_specs=(whole, P("dp"), whole) + (rows,) * 7 + (P("seq"),) * 4,
        out_specs=(whole, whole) + (rows,) * 7 + (P("seq"),) * 4,
        check_vma=False,
    )
```

```python
import functools
import math

import jax
import jax.numpy as jnp
from jax import lax
from jax.experimental import pallas as pl
from jax.experimental.pallas import tpu as pltpu
from jax.sharding import PartitionSpec as P

H = 16
KV = 8
HD = 64
EPS = 1e-05
ROPE_BASE = 1000000.0
LOG2E = math.log2(math.e)
SPLIT = 8
CHUNKS = 3

f32 = jnp.float32
bf16 = jnp.bfloat16
NN = (((1,), (0,)), ((), ()))
NT = (((1,), (1,)), ((), ()))
TN = (((0,), (0,)), ((), ()))


def dot(left, right, dims=NN):
    return lax.dot_general(left, right, dims, preferred_element_type=f32)


def rms_scale(values):
    return lax.rsqrt(jnp.mean(values * values, axis=-1, keepdims=True) + EPS)


def norm_back(grads, normed, scale):
    return scale * (grads - normed * jnp.mean(grads * normed, axis=-1, keepdims=True))


def tables(positions):
    half = HD // 2
    freq = ROPE_BASE ** (-(jnp.arange(half, dtype=f32) * 2.0 / HD))
    angle = positions.astype(f32)[:, None] * freq[None, :]
    cosine, sine = jnp.cos(angle), jnp.sin(angle)
    return jnp.tile(cosine, (1, 4)), jnp.concatenate([-sine, sine, -sine, sine], axis=1)


def lanes_of(x):
    return lax.broadcasted_iota(jnp.int32, x.shape, 1)


def pair_mean(x):
    row = lax.broadcasted_iota(jnp.int32, (2 * HD, 2 * HD), 0)
    same = (row < HD) == (lax.broadcasted_iota(jnp.int32, (2 * HD, 2 * HD), 1) < HD)
    ones = jnp.where(same, 1.0 / HD, 0.0).astype(bf16)
    high = x.astype(bf16)
    return dot(high, ones) + dot((x - high.astype(f32)).astype(bf16), ones)


def other_half(x):
    low = lax.rem(lanes_of(x), HD) < HD // 2
    return jnp.where(low, pltpu.roll(x, 3 * HD // 2, 1), pltpu.roll(x, HD // 2, 1))


def pair_half(x, first):
    lane = lax.broadcasted_iota(jnp.int32, x.shape, 1)
    rolled = pltpu.roll(x.astype(f32), HD, 1).astype(x.dtype)
    return jnp.where((lane < HD) == first, x, rolled)


def stack_pair(x):
    lane = lax.broadcasted_iota(jnp.int32, x.shape, 1)
    zero = jnp.zeros_like(x)
    return jnp.concatenate([jnp.where(lane < HD, x, zero), jnp.where(lane < HD, zero, x)], axis=0)


def causal(probs, block):
    key = lax.broadcasted_iota(jnp.int32, probs.shape, 0)
    query = lax.broadcasted_iota(jnp.int32, probs.shape, 1)
    query = jnp.where(query >= block, query - block, query)
    return jnp.where(key <= query, probs, 0.0)


def attend_fwd_kernel(block, q_ref, k_ref, v_ref, o_ref, lse_ref, keys, values):
    first = pl.program_id(0) % 2 == 0
    i = pl.program_id(1)

    @pl.when(i == 0)
    def _():
        keys[...] = pair_half(k_ref[...], first)
        values[...] = pair_half(v_ref[...], first)

    queries = stack_pair(q_ref[...])

    def tile(t, diagonal):
        rows = pl.ds(t * block, block)
        probs = jnp.exp2(dot(keys[rows, :], queries, NT) * (HD**-0.5 * LOG2E))
        if diagonal:
            probs = causal(probs, block)
        return dot(values[rows, :], probs.astype(bf16), TN), jnp.sum(probs, axis=0, keepdims=True)

    def body(t, carry):
        part, total = tile(t, False)
        return carry[0] + part, carry[1] + total

    mixed, total = lax.fori_loop(0, i, body, tile(i, True))
    mixed = mixed * (1.0 / total)
    pair = jnp.concatenate([mixed[:HD, :block], mixed[HD:, block:]], axis=0)
    o_ref[...] = pair.T.astype(bf16)
    lse_ref[0, 0] = jnp.log2(total)


def attend_forward(qkv, block):
    length, width = qkv.shape
    kv = width // (4 * HD)
    n = length // block
    key_at = lambda j, i: (0, kv + j // 2)
    value_at = lambda j, i: (0, kv + kv // 2 + j // 2)
    return pl.pallas_call(
        functools.partial(attend_fwd_kernel, block),
        grid=(kv, n),
        in_specs=[
            pl.BlockSpec((block, 2 * HD), lambda j, i: (i, j)),
            pl.BlockSpec((length, 2 * HD), key_at),
            pl.BlockSpec((length, 2 * HD), value_at),
        ],
        out_specs=[
            pl.BlockSpec((block, 2 * HD), lambda j, i: (i, j)),
            pl.BlockSpec((1, 1, 1, 2 * block), lambda j, i: (j, i, 0, 0)),
        ],
        out_shape=[
            jax.ShapeDtypeStruct((length, width // 2), bf16),
            jax.ShapeDtypeStruct((kv, n, 1, 2 * block), f32),
        ],
        scratch_shapes=[pltpu.VMEM((length, 2 * HD), bf16), pltpu.VMEM((length, 2 * HD), bf16)],
        cost_estimate=pl.CostEstimate(
            flops=8 * length * length * 2 * HD * kv,
            transcendentals=length * length * kv,
            bytes_accessed=3 * length * width,
        ),
        name="attend_forward",
    )(qkv, qkv, qkv)


def attend_bwd_kernel(
    block, j, q_ref, k_ref, v_ref, g_ref, o_ref, lse_ref, back_ref,
    queries, grads, delta, keys, values, grad_q,
):
    first = j % 2 == 0
    n = q_ref.shape[0] // block
    keys[...] = pair_half(k_ref[...], first)
    values[...] = pair_half(v_ref[...], first)
    for i in range(n):
        rows = slice(i * block, (i + 1) * block)
        g = g_ref[rows, :]
        queries[i] = stack_pair(q_ref[rows, :])
        grads[i] = stack_pair(g)
        both = (g.astype(f32) * o_ref[rows, :].astype(f32)).T
        delta[i] = jnp.concatenate(
            [jnp.sum(both[:HD], axis=0, keepdims=True), jnp.sum(both[HD:], axis=0, keepdims=True)],
            axis=1,
        )
        grad_q[i] = jnp.zeros(grad_q.shape[1:], f32)

    def tile(key, value, key_t, i, diagonal):
        query, grad = queries[i], grads[i]
        probs = jnp.exp2(dot(key, query, NT) * (HD**-0.5 * LOG2E) - lse_ref[0, i])
        if diagonal:
            probs = causal(probs, block)
        grad_probs = dot(value, grad, NT)
        grad_scores = (probs * (grad_probs - delta[i]) * HD**-0.5).astype(bf16)
        grad_q[i] += dot(key_t, grad_scores)
        return dot(grad_scores, query), dot(probs.astype(bf16), grad)

    def step(t, _):
        rows = pl.ds(t * block, block)
        key, value = keys[rows, :], values[rows, :]
        key_t = key.astype(f32).T.astype(bf16)

        def body(i, carry):
            part_k, part_v = tile(key, value, key_t, i, False)
            return carry[0] + part_k, carry[1] + part_v

        part_k, part_v = lax.fori_loop(t + 1, n, body, tile(key, value, key_t, t, True))
        part_k = part_k + pltpu.roll(part_k, HD, 1)
        part_v = part_v + pltpu.roll(part_v, HD, 1)
        both = jnp.where(lanes_of(part_k) < HD, part_k, part_v)
        back_ref[rows, 2 * HD :] = both.astype(bf16)
        return 0

    lax.fori_loop(0, n, step, 0)
    for i in range(n):
        pair = jnp.concatenate([grad_q[i, :HD, :block], grad_q[i, HD:, block:]], axis=0)
        back_ref[i * block : (i + 1) * block, : 2 * HD] = pair.T.astype(bf16)


def attend_backward(qkv, grads, mixed, lse, block, j):
    length, width = qkv.shape
    kv = width // (4 * HD)
    n = length // block
    column = lambda c: pl.BlockSpec((length, 2 * HD), lambda i: (0, c))
    return pl.pallas_call(
        functools.partial(attend_bwd_kernel, block, j),
        grid=(1,),
        in_specs=[
            column(j),
            column(kv + j // 2),
            column(kv + kv // 2 + j // 2),
            column(j),
            column(j),
            pl.BlockSpec((1, n, 1, 2 * block), lambda i: (j, 0, 0, 0)),
        ],
        out_specs=pl.BlockSpec((length, 4 * HD), lambda i: (0, 0)),
        out_shape=jax.ShapeDtypeStruct((length, 4 * HD), bf16),
        scratch_shapes=[
            pltpu.VMEM((n, 2 * block, 2 * HD), bf16),
            pltpu.VMEM((n, 2 * block, 2 * HD), bf16),
            pltpu.VMEM((n, 1, 2 * block), f32),
            pltpu.VMEM((length, 2 * HD), bf16),
            pltpu.VMEM((length, 2 * HD), bf16),
            pltpu.VMEM((n, 2 * HD, 2 * block), f32),
        ],
        cost_estimate=pl.CostEstimate(
            flops=20 * length * length * 2 * HD,
            transcendentals=length * length,
            bytes_accessed=6 * length * 4 * HD,
        ),
        name="attend_backward",
    )(qkv, qkv, qkv, grads, mixed, lse)


def ffn_kernel(
    shards, begins, z_ref, h_ref, ht_ref, gy_ref, own_g, own_u, own_d, far_g, far_u, far_d,
    out_in, grad_in, valid, out_ref, grad_ref, *refs,
):
    terms, (down, total) = refs[:-2], refs[-2:]
    t = pl.program_id(0)
    z = z_ref[0]
    even = z_ref[1] == 0
    rows = own_g.shape[0]
    piece = rows // SPLIT
    unit = own_g.shape[1]
    lanes = down.shape[1] // SPLIT
    blocks = unit // piece

    @pl.when(t == 0)
    def _():
        total[...] = out_in[...]
        grad_ref[...] = jnp.zeros_like(grad_ref) if begins else grad_in[...]
        down[...] = own_d[...]

    @pl.when(t > 0)
    def _():
        for d in range(SPLIT):
            for k in range(blocks):
                down[k * piece : (k + 1) * piece, d * lanes : (d + 1) * lanes] = far_d[
                    d, 0, 0, :, k * lanes : (k + 1) * lanes
                ]

    def shard_of(r):
        return lax.rem(z + shards - r, shards)

    def weight(own, far):
        parts = [own[...]]
        for r in range(1, shards):
            parts.append(far[:, r - 1, 0].reshape(rows, unit))
        return jnp.concatenate(parts, axis=0)

    weight_g, weight_u = weight(own_g, far_g), weight(own_u, far_u)
    gate, up = dot(h_ref[...], weight_g), dot(h_ref[...], weight_u)
    grad_inner = dot(gy_ref[...], down[...], NT)
    sigma = jax.nn.sigmoid(gate)
    active = gate * sigma
    inner = (active * up).astype(bf16)
    grad_g = (grad_inner * up * sigma * (1.0 + gate * (1.0 - sigma))).astype(bf16)
    grad_u = (grad_inner * active).astype(bf16)
    total[...] += dot(inner, down[...])
    grad_ref[...] += dot(grad_g, weight_g, NT) + dot(grad_u, weight_u, NT)
    seg = pl.ds(pl.multiple_of(shard_of(t) * unit, unit), unit)

    def keep(term, at):
        term = term.astype(bf16)
        for r in range(shards):
            part = term[r * rows : (r + 1) * rows]
            if len(terms) == 1:
                terms[0][:, r, at : at + piece, seg] = part.reshape(SPLIT, piece, unit)
                continue
            part = part.reshape(SPLIT // 2, 2, piece, unit)
            mine, theirs = terms
            mine[:, r, at : at + piece, seg] = jnp.where(even, part[:, 0], part[:, 1])
            theirs[:, r, at : at + piece, seg] = jnp.where(even, part[:, 1], part[:, 0])

    keep(dot(ht_ref[...], grad_g), 0)
    keep(dot(ht_ref[...], grad_u), piece)

    @pl.when(t == shards - 1)
    def _():
        out = total[...]
        if out_ref.dtype == bf16:
            out = jnp.where(valid[...] > 0, out, 0.0).astype(bf16)
        out_ref[...] = out

    term = dot(inner, gy_ref[...], TN).astype(bf16)
    for d in range(SPLIT):
        for k in range(blocks):
            part = term[k * piece : (k + 1) * piece, d * lanes : (d + 1) * lanes]
            to = (t, slice(2 * piece, 3 * piece), slice(k * lanes, (k + 1) * lanes))
            if len(terms) == 1:
                terms[0][(d, *to)] = part
            elif d % 2 == 0:
                even_part = part
            else:
                even_part = term[k * piece : (k + 1) * piece, (d - 1) * lanes : d * lanes]
                terms[0][(d // 2, *to)] = jnp.where(even, even_part, part)
                terms[1][(d // 2, *to)] = jnp.where(even, part, even_part)


def ffn_chunk(
    c, kind, parted, z, hidden, hidden_t, grad_y, w_gate, w_up, w_down, far, out_in, grad_in, valid
):
    rows, width = hidden.shape
    shards = width // w_gate.shape[0]
    depth = w_gate.shape[0]
    unit = w_down.shape[0] // CHUNKS
    piece = depth // SPLIT
    n_far = shards - 1
    far = far.reshape(SPLIT, n_far, -1, piece, shards * unit)
    terms = (SPLIT // 2 if parted else SPLIT, shards, 3 * piece, shards * unit)
    n_terms = 2 if parted else 1
    seg = lambda t, z_ref: lax.rem(z_ref[0] + shards - t, shards)
    whole = lambda shape: pl.BlockSpec(shape, lambda t, z_ref: (0,) * len(shape))
    own = pl.BlockSpec((depth, unit), lambda t, z_ref: (0, seg(t, z_ref) * CHUNKS + c))
    gathered = lambda at: pl.BlockSpec(
        (SPLIT, n_far, 1, piece, unit), lambda t, z_ref: (0, 0, at, 0, seg(t, z_ref))
    )
    source = lambda t, z_ref: jnp.maximum(t - 1, 0)
    return pl.pallas_call(
        functools.partial(ffn_kernel, shards, c == 0),
        grid_spec=pltpu.PrefetchScalarGridSpec(
            num_scalar_prefetch=1,
            grid=(shards,),
            in_specs=[
                whole((rows, width)),
                whole((width, rows)),
                whole((rows, width)),
                own,
                own,
                pl.BlockSpec((unit, width), lambda t, z_ref: (c, 0)),
                gathered(kind),
                gathered(kind + 1),
                pl.BlockSpec(
                    (SPLIT, 1, 1, piece, shards * unit),
                    lambda t, z_ref: (0, source(t, z_ref), kind + 2, 0, 0),
                ),
                whole((rows, width)),
                whole((rows, width)),
                whole((rows, 1)),
            ],
            out_specs=[
                whole((rows, width)),
                whole((rows, width)),
            ]
            + [whole(terms)] * n_terms,
            scratch_shapes=[pltpu.VMEM((unit, width), bf16), pltpu.VMEM((rows, width), f32)],
        ),
        out_shape=[
            jax.ShapeDtypeStruct((rows, width), bf16 if c == CHUNKS - 1 else f32),
            jax.ShapeDtypeStruct((rows, width), f32),
        ]
        + [jax.ShapeDtypeStruct(terms, bf16)] * n_terms,
        cost_estimate=pl.CostEstimate(
            flops=18 * rows * width * shards * unit,
            transcendentals=rows * shards * unit,
            bytes_accessed=12 * width * shards * unit + 20 * rows * width,
        ),
        name="ffn_chunk",
    )(z, hidden, hidden_t, grad_y, w_gate, w_up, w_down, far, far, far, out_in, grad_in, valid)


def pack_kernel(m_ref, gate, up, down, out, first_ref, last_ref):
    piece, width = out.shape
    unit = down.shape[0] // CHUNKS
    shards = gate.shape[1] // down.shape[0]
    lanes = down.shape[1]
    for c in range(CHUNKS):
        ref = last_ref if c == CHUNKS - 1 else first_ref
        at = 0 if c == CHUNKS - 1 else 3 * piece * c
        for s in range(shards):
            source = slice((s * CHUNKS + c) * unit, (s * CHUNKS + c + 1) * unit)
            ref[at : at + piece, s * unit : (s + 1) * unit] = gate[:, source]
            ref[at + piece : at + 2 * piece, s * unit : (s + 1) * unit] = up[:, source]
        for k in range(unit // piece):
            rows = slice(c * unit + k * piece, c * unit + (k + 1) * piece)
            ref[at + 2 * piece : at + 3 * piece, k * lanes : (k + 1) * lanes] = down[rows, :]
    at = 3 * piece * (CHUNKS - 1)
    first_ref[at:, :width] = out[...]
    first_ref[at:, width:] = jnp.zeros_like(first_ref[at:, width:])


def pack(member, w_gate, w_up, w_down, w_out):
    depth, width = w_out.shape
    piece = depth // SPLIT
    lanes = width // SPLIT
    line = w_gate.shape[1] // CHUNKS
    rows = lambda w: pl.BlockSpec((piece, w.shape[1]), lambda i, m_ref: (m_ref[0], 0))
    outs = [((3 * CHUNKS - 2) * piece, line), (3 * piece, line)]
    return pl.pallas_call(
        pack_kernel,
        grid_spec=pltpu.PrefetchScalarGridSpec(
            num_scalar_prefetch=1,
            grid=(1,),
            in_specs=[
                rows(w_gate),
                rows(w_up),
                pl.BlockSpec((w_down.shape[0], lanes), lambda i, m_ref: (0, m_ref[0])),
                rows(w_out),
            ],
            out_specs=[pl.BlockSpec(shape, lambda i, m_ref: (0, 0)) for shape in outs],
        ),
        out_shape=[jax.ShapeDtypeStruct(shape, bf16) for shape in outs],
        name="pack",
    )(member.reshape(1), w_gate, w_up, w_down, w_out)


def unpack_kernel(source, *refs):
    gate_ref, up_ref, down_ref = refs[-3:]
    piece = source.shape[2]
    lanes = down_ref.shape[1] // SPLIT
    blocks = down_ref.shape[0] // piece
    gate_ref[...] = source[:, 0].astype(f32).reshape(gate_ref.shape)
    up_ref[...] = source[:, 1].astype(f32).reshape(up_ref.shape)
    for d in range(SPLIT):
        for k in range(blocks):
            down_ref[k * piece : (k + 1) * piece, d * lanes : (d + 1) * lanes] = source[
                d, 2, :, k * lanes : (k + 1) * lanes
            ].astype(f32)


def unpack_ffn(source, first, count, before, depth, shards, unit, width):
    piece = depth // SPLIT
    source = source.reshape(SPLIT, -1, piece, shards * unit)
    rows = unit // shards
    columns = pl.BlockSpec((depth, unit), lambda c, s: (0, s * CHUNKS + first + c))
    return pl.pallas_call(
        unpack_kernel,
        grid=(count, shards),
        in_specs=[pl.BlockSpec((SPLIT, 3, piece, unit), lambda c, s: (0, c, 0, s))]
        + [pl.BlockSpec(memory_space=pl.ANY)] * len(before),
        out_specs=[
            columns,
            columns,
            pl.BlockSpec((rows, width), lambda c, s: ((first + c) * shards + s, 0)),
        ],
        out_shape=[
            jax.ShapeDtypeStruct((depth, shards * CHUNKS * unit), f32),
            jax.ShapeDtypeStruct((depth, shards * CHUNKS * unit), f32),
            jax.ShapeDtypeStruct((CHUNKS * unit, width), f32),
        ],
        input_output_aliases={i + 1: i for i in range(len(before))},
        name="unpack_ffn",
    )(source, *before)


def unpack_near_kernel(m_ref, even, odd, *refs):
    gate_ref, up_ref, down_ref = refs[-3:]
    piece = gate_ref.shape[0] // SPLIT
    lanes = down_ref.shape[1] // SPLIT
    blocks = down_ref.shape[0] // piece
    for b in range(SPLIT):
        source = (odd if b % 2 else even)[b // 2].astype(f32)
        member = jnp.bitwise_xor(m_ref[0], b)
        rows = pl.ds(pl.multiple_of(member * piece, piece), piece)
        gate_ref[rows, :] = source[:piece]
        up_ref[rows, :] = source[piece : 2 * piece]
        columns = pl.ds(pl.multiple_of(member * lanes, lanes), lanes)
        for k in range(blocks):
            down_ref[k * piece : (k + 1) * piece, columns] = source[
                2 * piece :, k * lanes : (k + 1) * lanes
            ]


def unpack_near(member, even, odd, chunk, before, shards):
    gate, _, down = before
    unit = gate.shape[1] // (shards * CHUNKS)
    columns = pl.BlockSpec((gate.shape[0], unit), lambda s, m_ref: (0, s * CHUNKS + chunk))
    source = pl.BlockSpec((SPLIT // 2, even.shape[1], unit), lambda s, m_ref: (0, 0, s))
    rows = down.shape[0] // (CHUNKS * shards)
    return pl.pallas_call(
        unpack_near_kernel,
        grid_spec=pltpu.PrefetchScalarGridSpec(
            num_scalar_prefetch=1,
            grid=(shards,),
            in_specs=[source, source] + [pl.BlockSpec(memory_space=pl.ANY)] * 3,
            out_specs=[
                columns,
                columns,
                pl.BlockSpec((rows, down.shape[1]), lambda s, m_ref: (chunk * shards + s, 0)),
            ],
        ),
        out_shape=[jax.ShapeDtypeStruct(x.shape, f32) for x in before],
        input_output_aliases={3 + i: i for i in range(3)},
        name="unpack_near",
    )(member.reshape(1), even, odd, *before)


def shard_at(z, r, shards):
    return lax.rem(z + shards - r, shards)


def part_of(z, r, shards, size):
    return pl.ds(pl.multiple_of(shard_at(z, r, shards) * size, size), size)


def joined(own, far, r):
    return own[...] if r == 0 else far[:, r - 1].reshape(own.shape)


def qkv_fwd_kernel(
    shards, z_ref, h_ref, cos_ref, sin_ref, gain_q, gain_k, *refs
):
    own, far, (send_ref, raw_ref) = refs[:3], refs[3:6], refs[6:]
    z = z_ref[0]
    depth = own[0].shape[0]
    total = [None] * 3
    for r in range(shards):
        left = h_ref[:, part_of(z, r, shards, depth)]
        for i in range(3):
            part = dot(left, joined(own[i], far[i], r))
            total[i] = part if r == 0 else total[i] + part
    cosine, sine = cos_ref[...], sin_ref[...]
    at = 0
    for values, gain in ((total[0], gain_q), (total[1], gain_k)):
        for i in range(0, values.shape[1], 2 * HD):
            pair = values[:, i : i + 2 * HD]
            raw_ref[:, at : at + 2 * HD] = pair
            scaled = pair * lax.rsqrt(pair_mean(pair * pair) + EPS) * gain[...]
            rotated = scaled * cosine + other_half(scaled) * sine
            send_ref[:, at : at + 2 * HD] = rotated.astype(bf16)
            at += 2 * HD
    send_ref[:, at:] = total[2].astype(bf16)


def projection_specs(shards, depth, piece, columns):
    sizes = [n // shards for n in columns]
    last = lambda s: jnp.minimum(s, shards - 1)
    own = [pl.BlockSpec((depth, n), lambda s, z_ref: (0, last(s))) for n in sizes]
    starts = [sum(columns[:i]) // sizes[i] for i in range(3)]
    far = [
        pl.BlockSpec(
            (SPLIT, shards - 1, piece, n), lambda s, z_ref, start=start: (0, 0, 0, start + last(s))
        )
        for n, start in zip(sizes, starts)
    ]
    return own + far


def qkv_forward(z, hidden, cosine, sine, gain_q, gain_k, weights, far):
    local, width = hidden.shape
    depth = weights[0].shape[0]
    shards = width // depth
    columns = [w.shape[1] for w in weights]
    each = sum(columns) // shards
    raw = each - columns[2] // shards
    whole = lambda x: pl.BlockSpec(x.shape, lambda s, z_ref: (0,) * x.ndim)
    return pl.pallas_call(
        functools.partial(qkv_fwd_kernel, shards),
        grid_spec=pltpu.PrefetchScalarGridSpec(
            num_scalar_prefetch=1,
            grid=(shards,),
            in_specs=[whole(x) for x in (hidden, cosine, sine, gain_q, gain_k)]
            + projection_specs(shards, depth, far.shape[2], columns),
            out_specs=[
                pl.BlockSpec((local, each), lambda s, z_ref: (s, 0)),
                pl.BlockSpec((local, raw), lambda s, z_ref: (s, 0)),
            ],
        ),
        out_shape=[
            jax.ShapeDtypeStruct((shards * local, each), bf16),
            jax.ShapeDtypeStruct((shards * local, raw), f32),
        ],
        cost_estimate=pl.CostEstimate(
            flops=2 * local * width * sum(columns),
            transcendentals=0,
            bytes_accessed=2 * width * sum(columns) + 8 * local * sum(columns),
        ),
        name="qkv_forward",
    )(z, hidden, cosine, sine, gain_q, gain_k, *weights, far, far, far)


def qkv_bwd_kernel(
    shards, heads, z_ref, ht_ref, cos_ref, sin_ref, gain_q, gain_k,
    tokens, scale_ref, gain_1, resid, sum_2, raw_ref, *refs,
):
    back, refs = refs[:heads], refs[heads:]
    own, far, (tokens_ref, mine, theirs), refs = refs[:3], refs[3:6], refs[6:9], refs[9:]
    sum_q, sum_k, grads, grad_ref = refs
    step = pl.program_id(0)
    z = z_ref[0]
    even = z_ref[1] == 0
    depth = own[0].shape[0]
    piece = depth // SPLIT

    @pl.when(step == 0)
    def _():
        grad_ref[...] = jnp.zeros_like(grad_ref)
        sum_q[...] = jnp.zeros_like(sum_q)
        sum_k[...] = jnp.zeros_like(sum_k)

    @pl.when(step < shards)
    def _():
        cosine, sine = cos_ref[...], sin_ref[...]
        at = 0
        halves = [ref[:, 2 * HD :] for ref in back]
        swapped = [pltpu.roll(half.astype(f32), HD, 1).astype(bf16) for half in halves]
        low = lanes_of(halves[0]) < HD
        arrived = [[ref[:, : 2 * HD] for ref in back]]
        arrived.append([jnp.where(low, halves[i], swapped[i + 1]) for i in range(0, heads, 2)])
        arrived.append([jnp.where(low, swapped[i], halves[i + 1]) for i in range(0, heads, 2)])
        for pairs, gain, total in ((arrived[0], gain_q, sum_q), (arrived[1], gain_k, sum_k)):
            for grad in pairs:
                pair = raw_ref[:, at : at + 2 * HD]
                scale = lax.rsqrt(pair_mean(pair * pair) + EPS)
                hat = pair * scale
                grad = grad.astype(f32)
                grad = grad * cosine + other_half(grad * sine)
                total[...] += jnp.sum(grad * hat, axis=0, keepdims=True)
                grad = grad * gain[...]
                grads[:, at : at + 2 * HD] = (scale * (grad - hat * pair_mean(grad * hat))).astype(bf16)
                at += 2 * HD
        for i, pair in enumerate(arrived[2]):
            grads[:, at + i * 2 * HD : at + (i + 1) * 2 * HD] = pair
        ends = (0, own[0].shape[1], at, grads.shape[1])
        for r in range(shards):
            part = None
            for i in range(3):
                one = dot(grads[:, ends[i] : ends[i + 1]], joined(own[i], far[i], r), NT)
                part = one if i == 0 else part + one
            grad_ref[:, part_of(z, r, shards, depth)] += part
            term = dot(ht_ref[part_of(z, r, shards, depth), :], grads[...]).astype(bf16)
            term = term.reshape(SPLIT // 2, 2, piece, term.shape[1])
            mine[:, r] = jnp.where(even, term[:, 0], term[:, 1])
            theirs[:, r] = jnp.where(even, term[:, 1], term[:, 0])

    @pl.when(step == shards)
    def _():
        scale = scale_ref[...]
        normed = tokens[...].astype(f32) * scale
        grad = grad_ref[...]
        sum_1 = jnp.sum(grad * normed, axis=0, keepdims=True)
        tokens_ref[...] = resid[...] + norm_back(grad * gain_1[...], normed, scale)
        lanes = 2 * HD
        empty = jnp.zeros((piece, mine.shape[3] - lanes), f32)
        turn = [shard_at(z, r, shards) for r in range(shards)]
        grad_ref[0:1, :] = sum_1
        grad_ref[1:2, :] = sum_2[...]
        for r in range(shards):
            rows = []
            for i in range(2):
                for k in range(0, depth, lanes):
                    at = pl.multiple_of(turn[r] * depth + k, lanes)
                    rows.append(grad_ref[i : i + 1, pl.ds(at, lanes)])
            rows += [sum_q[...], sum_k[...]]
            rows.append(jnp.zeros((piece - len(rows), lanes), f32))
            block = jnp.concatenate([jnp.concatenate(rows, axis=0), empty], axis=1).astype(bf16)
            for d in range(SPLIT // 2):
                mine[d, r] = block
                theirs[d, r] = block


def qkv_backward(z, hidden_t, tables_gains, first_norm, back, raw, weights, far):
    width, local = hidden_t.shape
    depth = weights[0].shape[0]
    shards = width // depth
    piece = depth // SPLIT
    columns = [w.shape[1] for w in weights]
    each = sum(columns) // shards
    whole = lambda shape: pl.BlockSpec(shape, lambda s, z_ref: (0,) * len(shape))
    last = lambda s: jnp.minimum(s, shards - 1)
    rows = lambda x: pl.BlockSpec((local, x.shape[1]), lambda s, z_ref: (last(s), 0))
    terms = jax.ShapeDtypeStruct((SPLIT // 2, shards, piece, shards * each + 2 * HD), bf16)
    at_terms = pl.BlockSpec((SPLIT // 2, shards, piece, each), lambda s, z_ref: (0, 0, 0, s))
    return pl.pallas_call(
        functools.partial(qkv_bwd_kernel, shards, len(back)),
        grid_spec=pltpu.PrefetchScalarGridSpec(
            num_scalar_prefetch=1,
            grid=(shards + 1,),
            in_specs=[whole(x.shape) for x in (hidden_t, *tables_gains, *first_norm)]
            + [rows(x) for x in (raw, *back)]
            + projection_specs(shards, depth, piece, columns),
            out_specs=[whole((local, width)), at_terms, at_terms],
            scratch_shapes=[
                pltpu.VMEM((1, 2 * HD), f32),
                pltpu.VMEM((1, 2 * HD), f32),
                pltpu.VMEM((local, each), bf16),
                pltpu.VMEM((local, width), f32),
            ],
        ),
        out_shape=[jax.ShapeDtypeStruct((local, width), f32), terms, terms],
        cost_estimate=pl.CostEstimate(
            flops=4 * local * width * sum(columns),
            transcendentals=0,
            bytes_accessed=4 * width * sum(columns) + 8 * local * sum(columns),
        ),
        name="qkv_backward",
    )(z, hidden_t, *tables_gains, *first_norm, raw, *back, *weights, far, far, far)


def unpack_qkv_kernel(shards, m_ref, even, odd, *refs):
    piece = even.shape[1]
    out = refs[3]
    for b in range(SPLIT):
        source = (odd if b % 2 else even)[b // 2].astype(f32)
        rows = pl.ds(pl.multiple_of(jnp.bitwise_xor(m_ref[0], b) * piece, piece), piece)
        at = 0
        for s in range(shards):
            for ref in refs[:3]:
                n = ref.shape[1] // shards
                ref[rows, s * n : (s + 1) * n] = source[:, at : at + n]
                at += n
        out[rows, :] = source[:, source.shape[1] - out.shape[1] :]


def unpack_qkv(member, even, odd, shards, columns, width):
    piece = even.shape[1]
    columns = columns + [width]
    whole = lambda shape: pl.BlockSpec(shape, lambda i, m_ref: (0,) * len(shape))
    return pl.pallas_call(
        functools.partial(unpack_qkv_kernel, shards),
        grid_spec=pltpu.PrefetchScalarGridSpec(
            num_scalar_prefetch=1,
            grid=(1,),
            in_specs=[whole(even.shape), whole(odd.shape)],
            out_specs=[whole((SPLIT * piece, n)) for n in columns],
        ),
        out_shape=[jax.ShapeDtypeStruct((SPLIT * piece, n), f32) for n in columns],
        name="unpack_qkv",
    )(member.reshape(1), even, odd)


def out_fwd_kernel(shards, z_ref, mixed, tokens, gain, own, far, resid_ref, scale_ref, h_ref, ht_ref):
    z = z_ref[0]
    local = tokens.shape[0]
    resid = tokens[...].astype(f32)
    for r in range(shards):
        weight = own[...] if r == 0 else far[:, r - 1, 0].reshape(own.shape)
        resid = resid + dot(mixed[part_of(z, r, shards, local), :], weight)
    scale = rms_scale(resid)
    hidden = resid * scale * gain[...]
    resid_ref[...] = resid
    scale_ref[...] = scale
    turned = hidden.T.astype(bf16)
    low = hidden.astype(bf16)
    depth = own.shape[0]
    for s in range(shards):
        at = part_of(z, s, shards, depth)
        h_ref[:, at] = low[:, s * depth : (s + 1) * depth]
        ht_ref[at, :] = turned[s * depth : (s + 1) * depth]


def far_out_spec(far, width):
    size = (SPLIT, far.shape[1], 1, far.shape[3], width)
    return pl.BlockSpec(size, lambda i, z_ref: (0, 0, far.shape[2] - 1, 0, 0))


def out_forward(z, mixed, tokens, gain, w_out, far):
    local, width = tokens.shape
    shards = mixed.shape[0] // local
    piece = w_out.shape[0] // SPLIT
    far = far.reshape(SPLIT, shards - 1, -1, piece, far.shape[-1])
    whole = lambda shape: pl.BlockSpec(shape, lambda i, z_ref: (0,) * len(shape))
    outs = [((local, width), f32), ((local, 1), f32), ((local, width), bf16), ((width, local), bf16)]
    return pl.pallas_call(
        functools.partial(out_fwd_kernel, shards),
        grid_spec=pltpu.PrefetchScalarGridSpec(
            num_scalar_prefetch=1,
            grid=(1,),
            in_specs=[whole(x.shape) for x in (mixed, tokens, gain, w_out)]
            + [far_out_spec(far, width)],
            out_specs=[whole(shape) for shape, _ in outs],
        ),
        out_shape=[jax.ShapeDtypeStruct(*out) for out in outs],
        cost_estimate=pl.CostEstimate(
            flops=2 * local * width * width, transcendentals=0, bytes_accessed=14 * local * width
        ),
        name="out_forward",
    )(z, mixed, tokens, gain, w_out, far)


def out_bwd_kernel(
    shards, z_ref, grad, grad_y, resid, scale_ref, gain, own, far, grad_resid, sum_ref, branch, send
):
    z = z_ref[0]
    local = grad.shape[0]
    scale = scale_ref[...]
    normed = resid[...] * scale
    depth = own.shape[0]
    parts = [grad[:, part_of(z, s, shards, depth)] for s in range(shards)]
    come = jnp.concatenate(parts, axis=1)
    sum_ref[...] = jnp.sum(come * normed, axis=0, keepdims=True)
    total = grad_y[...].astype(f32) + norm_back(come * gain[...], normed, scale)
    grad_resid[...] = total
    low = total.astype(bf16)
    branch[...] = low
    for r in range(shards):
        weight = own[...] if r == 0 else far[:, r - 1, 0].reshape(own.shape)
        send[part_of(z, r, shards, local), :] = dot(low, weight, NT).astype(bf16)


def out_backward(z, grad, grad_y, resid, scale, gain, w_out, far):
    local, width = grad.shape
    depth = w_out.shape[0]
    shards = width // depth
    piece = depth // SPLIT
    far = far.reshape(SPLIT, shards - 1, -1, piece, far.shape[-1])
    whole = lambda shape: pl.BlockSpec(shape, lambda i, z_ref: (0,) * len(shape))
    outs = [((local, width), f32), ((1, width), f32), ((local, width), bf16), ((shards * local, depth), bf16)]
    return pl.pallas_call(
        functools.partial(out_bwd_kernel, shards),
        grid_spec=pltpu.PrefetchScalarGridSpec(
            num_scalar_prefetch=1,
            grid=(1,),
            in_specs=[whole(x.shape) for x in (grad, grad_y, resid, scale, gain, w_out)]
            + [far_out_spec(far, width)],
            out_specs=[whole(shape) for shape, _ in outs],
        ),
        out_shape=[jax.ShapeDtypeStruct(*out) for out in outs],
        cost_estimate=pl.CostEstimate(
            flops=2 * local * width * width, transcendentals=0, bytes_accessed=20 * local * width
        ),
        name="out_backward",
    )(z, grad, grad_y, resid, scale, gain, w_out, far)


def out_terms_kernel(shards, z_ref, mixed, branch, terms):
    term = dot(mixed[...], branch[...], TN).astype(bf16)
    terms[:, 0] = term.reshape(terms.shape[0], terms.shape[2], terms.shape[3])


def out_terms(z, mixed, branch):
    local, width = branch.shape
    shards = mixed.shape[0] // local
    depth = mixed.shape[1]
    piece = depth // SPLIT
    return pl.pallas_call(
        functools.partial(out_terms_kernel, shards),
        grid_spec=pltpu.PrefetchScalarGridSpec(
            num_scalar_prefetch=1,
            grid=(shards,),
            in_specs=[
                pl.BlockSpec((local, depth), lambda r, z_ref: (shard_at(z_ref[0], r, shards), 0)),
                pl.BlockSpec((local, width), lambda r, z_ref: (0, 0)),
            ],
            out_specs=pl.BlockSpec((SPLIT, 1, piece, width), lambda r, z_ref: (0, r, 0, 0)),
        ),
        out_shape=jax.ShapeDtypeStruct((SPLIT, shards, piece, width), bf16),
        cost_estimate=pl.CostEstimate(
            flops=2 * local * width * width, transcendentals=0, bytes_accessed=8 * local * width
        ),
        name="out_terms",
    )(z, mixed, branch)


def either_kernel(n, z_ref, *refs):
    came, out = refs[:-1], refs[-1]
    for r in range(1, n):
        out[r - 1] = jnp.where(z_ref[0] >= r, came[r - 1][...], came[2 * n - 2 - r][...])


class Axes:
    def __init__(self, mesh):
        self.n_dp = mesh.shape["dp"]
        self.n_seq = mesh.shape["seq"]
        self.groups = None
        self.across = None
        if self.n_dp > SPLIT:
            self.groups = [[g + i for i in range(SPLIT)] for g in range(0, self.n_dp, SPLIT)]
            self.across = [list(range(i, self.n_dp, SPLIT)) for i in range(SPLIT)]

    def member(self):
        return lax.rem(lax.axis_index("dp"), SPLIT)

    def shift(self, x, r):
        n = self.n_seq
        return lax.ppermute(x, "seq", [(i, (i + r) % n) for i in range(n)])

    def from_others(self, x):
        return [self.shift(x, r) for r in range(1, self.n_seq)]

    def pass_on(self, x):
        n = self.n_seq
        up = down = x
        below, above = [], []
        for step in range(1, n):
            up = lax.ppermute(up, "seq", [(i, i + 1) for i in range(step - 1, n - 1)])
            down = lax.ppermute(down, "seq", [(i + 1, i) for i in range(n - step)])
            below.append(up)
            above.append(down)
        return below + above

    def either(self, came):
        n = self.n_seq
        rows, width = came[0].shape
        block = rows // (7 if rows % 7 == 0 else 1)
        spec = pl.BlockSpec((block, width), lambda i, z_ref: (i, 0))
        return pl.pallas_call(
            functools.partial(either_kernel, n),
            grid_spec=pltpu.PrefetchScalarGridSpec(
                num_scalar_prefetch=1,
                grid=(rows // block,),
                in_specs=[spec] * len(came),
                out_specs=pl.BlockSpec((n - 1, block, width), lambda i, z_ref: (0, i, 0)),
            ),
            out_shape=jax.ShapeDtypeStruct((n - 1, rows, width), came[0].dtype),
            name="either",
        )(lax.axis_index("seq").reshape(1), *came)

    def gather_all(self, x):
        if self.groups:
            x = self.gather(lax.all_gather(x, "seq")[None])
        else:
            x = lax.all_gather(x, ("dp", "seq"))
        return x.reshape(SPLIT, self.n_seq, *x.shape[-2:])

    def gather_near(self, x, *others):
        even = jnp.stack([after(y, *others) for y in [x] + [self.swap(x, bit) for bit in (2, 4, 6)]])
        return even, self.swap(even, 1)

    def gather(self, x):
        return lax.all_gather(x, "dp", axis=0, tiled=True, axis_index_groups=self.groups)

    def scatter(self, terms):
        flat = terms.reshape(SPLIT * terms.shape[1], *terms.shape[2:])
        return lax.psum_scatter(
            flat, "dp", scatter_dimension=0, tiled=True, axis_index_groups=self.groups
        )

    def over_groups(self, x):
        return lax.psum(x, "dp", axis_index_groups=self.across) if self.across else x

    def swap(self, x, bit):
        return lax.ppermute(x, "dp", [(i, i ^ bit) for i in range(self.n_dp)])


def after(x, *others):
    return lax.optimization_barrier((x, *others))[0]


class Reduction:
    def __init__(self, axes, mine, theirs):
        self.axes = axes
        member = axes.member()
        self.x = lax.rem(lax.div(member, 2), 2)
        self.y = lax.div(member, 4)
        self.mine = mine.reshape(2, 2, *mine.shape[1:])
        self.state = (axes.swap(theirs, 1),)

    def then(self, *others):
        self.state = lax.optimization_barrier((*self.state, *others))[: len(self.state)]

    def _sum(self, y, x, low, *more):
        def cut(arr):
            shards = arr.shape[2] // 2
            start = [y if y is not None else 0, x if x is not None else 0, 0 if low else shards]
            size = [1 if y is not None else 2, 1 if x is not None else 2, shards]
            rest = arr.ndim - 3
            part = lax.dynamic_slice(arr, start + [0] * rest, size + list(arr.shape[3:]))
            drop = tuple(i for i, at in enumerate((y, x)) if at is not None)
            return lax.squeeze(part, drop).astype(f32)

        total = cut(self.mine) + cut(self.recv)
        for arr in more:
            total = total + arr.astype(f32)
        return total

    def first(self):
        (recv,) = self.state
        self.recv = recv.reshape(self.mine.shape)
        to_x = self._sum(None, 1 - self.x, True).astype(bf16)
        to_y = self._sum(1 - self.y, None, False).astype(bf16)
        self.sent = (to_x, to_y)
        return self

    def send_first(self):
        self.state = (self.axes.swap(self.sent[0], 2), self.axes.swap(self.sent[1], 4))
        return self

    def second(self):
        self.got_x, self.got_y = self.state
        pick = lambda arr, i: lax.dynamic_index_in_dim(arr, i, axis=0, keepdims=False)
        to_y = self._sum(1 - self.y, self.x, True, pick(self.got_x, 1 - self.y)).astype(bf16)
        to_x = self._sum(self.y, 1 - self.x, False, pick(self.got_y, 1 - self.x)).astype(bf16)
        self.sent = (to_x, to_y)
        return self

    def send_second(self):
        self.state = (self.axes.swap(self.sent[1], 4), self.axes.swap(self.sent[0], 2))
        return self

    def third(self):
        got_y, got_x = self.state
        pick = lambda arr, i: lax.dynamic_index_in_dim(arr, i, axis=0, keepdims=False)
        low = self._sum(self.y, self.x, True, pick(self.got_x, self.y), got_y)
        high = self._sum(self.y, self.x, False, pick(self.got_y, self.x), got_x)
        return jnp.concatenate([low, high], axis=0).astype(bf16)


def per_device(
    axes, tokens, lengths, cotangent, w_query, w_key, w_value, w_out, w_gate, w_up, w_down,
    gain_attn, gain_ffn, gain_query, gain_key,
):
    slots, local, width = tokens.shape
    assert slots == 1
    shards = axes.n_seq
    depth = width // shards
    piece = depth // SPLIT
    z = lax.axis_index("seq")
    member = axes.member()
    unit = w_down.shape[0] // CHUNKS
    lanes = width // SPLIT
    head = HD // shards
    weights = (w_query, w_key, w_value)
    columns = [w.shape[1] for w in weights]
    where = jnp.stack([z, lax.rem(member, 2)]).astype(jnp.int32)
    mine = lambda x: lax.dynamic_slice_in_dim(x, member * piece, piece, axis=0)

    def cut(parts):
        return lax.optimization_barrier(tuple(parts[r] for r in range(shards)))

    def cross_back(parts):
        return tuple(axes.shift(parts[r], -r) for r in range(1, shards))

    def add(own, others):
        own = own.astype(f32)
        for arr in others:
            own = own + arr.astype(f32)
        return axes.over_groups(own.astype(bf16))

    def by_owner(parts):
        pick = lambda i: lax.dynamic_index_in_dim(parts, lax.rem(z + shards - i, shards), 0)
        return jnp.concatenate([pick(i) for i in range(shards)], axis=0)

    def total(parts):
        return axes.over_groups(jnp.sum(parts.astype(f32), axis=0).astype(bf16))

    gains = jnp.concatenate([gain_attn, gain_ffn, gain_query, gain_key])
    gains = jnp.pad(gains, (0, piece * 128 - gains.shape[0])).reshape(piece, 128)
    packed = jnp.concatenate([mine(w_query), mine(w_key), mine(w_value), gains], axis=1)
    near = axes.from_others(packed)
    first_chunks, last_chunk = pack(member, w_gate, w_up, w_down, w_out)
    near = [after(x, first_chunks) for x in near]
    far_qkv = axes.gather(jnp.stack([x[:, :-128] for x in near]))
    far_qkv = far_qkv.reshape(SPLIT, shards - 1, piece, -1)
    gains = jnp.stack([x[:, -128:].reshape(-1) for x in [packed] + near])
    order = lax.rem(z + shards - jnp.arange(shards), shards)
    hot = (order[:, None] == jnp.arange(shards)[None, :]).astype(f32)
    gains = jnp.sum(hot[:, :, None] * gains.astype(f32)[:, None, :], axis=0)

    def gathered_gain(start, size):
        return gains[:, start : start + size].reshape(1, -1)

    gain1 = gathered_gain(0, depth)
    gain2 = gathered_gain(depth, depth)
    gain_q = jnp.tile(gathered_gain(2 * depth, head), (1, 2))
    gain_k = jnp.tile(gathered_gain(2 * depth + head, head), (1, 2))


    def stack_after(parts, *others):
        return jnp.stack([after(x, *others) for x in parts])

    positions = z * local + jnp.arange(local, dtype=jnp.int32)
    cosine, sine = tables(positions)
    valid = (positions < lengths[0])[:, None]
    grad_y = jnp.where(valid, cotangent[0], jnp.zeros((), bf16))
    inputs = tokens[0].astype(f32)
    scale1 = rms_scale(inputs)
    hidden1 = (inputs * scale1 * gain1).astype(bf16)
    hidden1_t = hidden1.T

    def exchange(x):
        return lax.all_to_all(x, "seq", split_axis=0, concat_axis=0, tiled=True)

    crossed = axes.pass_on(after(first_chunks, *near))
    send, raw = qkv_forward(where, hidden1, cosine, sine, gain_q, gain_k, weights, far_qkv)
    far = axes.gather(axes.either([after(x, send) for x in crossed]))
    qkv = exchange(send)
    crossed = axes.from_others(after(last_chunk, qkv))
    block = 512
    mixed_heads, lse = attend_forward(qkv, block)
    mixed = exchange(after(mixed_heads, *crossed))
    crossed = jnp.stack([after(x, mixed_heads) for x in crossed])
    far_last = axes.gather(crossed)
    mixed = after(mixed, crossed)
    resid, scale2, hidden2, hidden2_t = out_forward(where, mixed, tokens[0], gain2, w_out, far)

    result, grad_hidden2 = resid, resid

    def chunk(c, result, grad_hidden2):
        last = c == CHUNKS - 1
        source, kind = (far_last, 0) if last else (far, 3 * c)
        return ffn_chunk(
            c, kind, last, where, hidden2, hidden2_t, grad_y, w_gate, w_up, w_down, source,
            result, grad_hidden2, valid.astype(f32),
        )

    result, grad_hidden2, terms = chunk(0, result, grad_hidden2)
    sum0 = axes.scatter(terms)
    result, grad_hidden2, terms = chunk(1, result, grad_hidden2)
    sum1 = axes.scatter(terms)
    output, grad_hidden2, *terms = chunk(2, result, grad_hidden2)
    sum2 = Reduction(axes, *terms)

    grad_resid, term_gain2, branch, send = out_backward(
        where, grad_hidden2, grad_y, resid, scale2, gain2, w_out, far
    )
    grad_heads = exchange(send)
    terms_out = out_terms(where, mixed, after(branch, send))
    sum2.then(terms_out)
    sum2.first().send_first()
    parts0 = cut(after(sum0, grad_heads))
    grad_heads = after(grad_heads, terms_out, *sum2.sent, *parts0)
    others0 = cross_back(parts0)
    back = attend_backward(qkv, grad_heads, mixed_heads, lse, block, 0)
    back_rows = [exchange(back)]
    for j in range(1, KV // shards):
        piece0 = add(parts0[0], after(others0, back))
        grad_heads = after(grad_heads, piece0)
        back = attend_backward(qkv, grad_heads, mixed_heads, lse, block, j)
        back_rows.append(exchange(after(back, back_rows[-1])))
    sum2.then(back)
    sum2.second().send_second()
    parts1 = by_owner(after(sum1, back))
    back_rows[-1] = after(back_rows[-1], parts1, *sum2.sent)
    sum_out = axes.scatter(after(terms_out, piece0))
    piece0 = axes.gather(piece0[None])
    parts1 = exchange(after(parts1, back_rows[-1]))
    grad_tokens, terms, other = qkv_backward(
        where, hidden1_t, (cosine, sine, gain_q, gain_k),
        (tokens[0], scale1, gain1, grad_resid, term_gain2), back_rows, raw, weights, far_qkv,
    )
    tail = Reduction(axes, terms, after(other, parts1, *sum2.state))
    parts2 = by_owner(sum2.third())
    tail.then(parts2)
    parts2 = exchange(parts2)
    tail.first().send_first()
    piece1 = axes.gather(total(after(parts1, *tail.sent))[None])
    tail.second().send_second()
    tail.then(parts2)
    tail = by_owner(jnp.concatenate([tail.third(), sum_out], axis=2))
    late = total(after(parts2, tail))
    grads = unpack_ffn(after(piece0, tail), 0, 1, (), depth, shards, unit, width)
    tail = total(after(exchange(tail), *grads))
    even, odd = axes.gather_near(tail)
    late = axes.gather_near(late, tail)
    grads = unpack_ffn(piece1, 1, 1, grads, depth, shards, unit, width)
    grads = unpack_near(member, *late, CHUNKS - 1, grads, shards)
    grad_gate, grad_up, grad_down = grads
    grad_query, grad_key, grad_value, grad_out = unpack_qkv(
        member, even, odd, shards, columns, width
    )
    sums = even[0, :, sum(columns) : sum(columns) + 2 * HD].astype(f32)
    n = depth // (2 * HD)
    sum_1, sum_2 = sums[:n].reshape(depth), sums[n : 2 * n].reshape(depth)
    heads = [sums[i, :HD] + sums[i, HD:] for i in (2 * n, 2 * n + 1)]
    sum_q, sum_k = (lax.dynamic_slice_in_dim(x, z * head, head) for x in heads)
    return (
        output[None],
        grad_tokens[None],
        grad_query,
        grad_key,
        grad_value,
        grad_out,
        grad_gate,
        grad_up,
        grad_down,
        sum_1,
        sum_2,
        sum_q,
        sum_k,
    )


def solution(mesh):
    rows = P("seq", None)
    whole = P("dp", "seq", None)
    return jax.shard_map(
        functools.partial(per_device, Axes(mesh)),
        mesh=mesh,
        in_specs=(whole, P("dp"), whole) + (rows,) * 7 + (P("seq"),) * 4,
        out_specs=(whole, whole) + (rows,) * 7 + (P("seq"),) * 4,
        check_vma=False,
    )
```

```python
import functools
import math

import jax
import jax.numpy as jnp
from jax import lax
from jax.experimental import pallas as pl
from jax.experimental.pallas import tpu as pltpu
from jax.sharding import PartitionSpec as P

H = 16
KV = 8
HD = 64
EPS = 1e-05
ROPE_BASE = 1000000.0
LOG2E = math.log2(math.e)
SPLIT = 8
CHUNKS = 3

f32 = jnp.float32
bf16 = jnp.bfloat16
NN = (((1,), (0,)), ((), ()))
NT = (((1,), (1,)), ((), ()))
TN = (((0,), (0,)), ((), ()))


def dot(left, right, dims=NN):
    return lax.dot_general(left, right, dims, preferred_element_type=f32)


def rms_scale(values):
    return lax.rsqrt(jnp.mean(values * values, axis=-1, keepdims=True) + EPS)


def norm_back(grads, normed, scale):
    return scale * (grads - normed * jnp.mean(grads * normed, axis=-1, keepdims=True))


def tables(positions):
    half = HD // 2
    freq = ROPE_BASE ** (-(jnp.arange(half, dtype=f32) * 2.0 / HD))
    angle = positions.astype(f32)[:, None] * freq[None, :]
    cosine, sine = jnp.cos(angle), jnp.sin(angle)
    return jnp.tile(cosine, (1, 4)), jnp.concatenate([-sine, sine, -sine, sine], axis=1)


def lanes_of(x):
    return lax.broadcasted_iota(jnp.int32, x.shape, 1)


def pair_mean(x):
    row = lax.broadcasted_iota(jnp.int32, (2 * HD, 2 * HD), 0)
    same = (row < HD) == (lax.broadcasted_iota(jnp.int32, (2 * HD, 2 * HD), 1) < HD)
    ones = jnp.where(same, 1.0 / HD, 0.0).astype(bf16)
    high = x.astype(bf16)
    return dot(high, ones) + dot((x - high.astype(f32)).astype(bf16), ones)


def other_half(x):
    low = lax.rem(lanes_of(x), HD) < HD // 2
    return jnp.where(low, pltpu.roll(x, 3 * HD // 2, 1), pltpu.roll(x, HD // 2, 1))


def pair_half(x, first):
    lane = lax.broadcasted_iota(jnp.int32, x.shape, 1)
    rolled = pltpu.roll(x.astype(f32), HD, 1).astype(x.dtype)
    return jnp.where((lane < HD) == first, x, rolled)


def stack_pair(x):
    lane = lax.broadcasted_iota(jnp.int32, x.shape, 1)
    zero = jnp.zeros_like(x)
    return jnp.concatenate([jnp.where(lane < HD, x, zero), jnp.where(lane < HD, zero, x)], axis=0)


def causal(probs, block):
    key = lax.broadcasted_iota(jnp.int32, probs.shape, 0)
    query = lax.broadcasted_iota(jnp.int32, probs.shape, 1)
    query = jnp.where(query >= block, query - block, query)
    return jnp.where(key <= query, probs, 0.0)


def attend_fwd_kernel(block, q_ref, k_ref, v_ref, o_ref, lse_ref, keys, values):
    first = pl.program_id(0) % 2 == 0
    i = pl.program_id(1)

    @pl.when(i == 0)
    def _():
        keys[...] = pair_half(k_ref[...], first)
        values[...] = pair_half(v_ref[...], first)

    queries = stack_pair(q_ref[...])

    def tile(t, diagonal):
        rows = pl.ds(t * block, block)
        probs = jnp.exp2(dot(keys[rows, :], queries, NT) * (HD**-0.5 * LOG2E))
        if diagonal:
            probs = causal(probs, block)
        return dot(values[rows, :], probs.astype(bf16), TN), jnp.sum(probs, axis=0, keepdims=True)

    def body(t, carry):
        part, total = tile(t, False)
        return carry[0] + part, carry[1] + total

    mixed, total = lax.fori_loop(0, i, body, tile(i, True))
    mixed = mixed * (1.0 / total)
    pair = jnp.concatenate([mixed[:HD, :block], mixed[HD:, block:]], axis=0)
    o_ref[...] = pair.T.astype(bf16)
    lse_ref[0, 0] = jnp.log2(total)


def attend_forward(qkv, block):
    length, width = qkv.shape
    kv = width // (4 * HD)
    n = length // block
    key_at = lambda j, i: (0, kv + j // 2)
    value_at = lambda j, i: (0, kv + kv // 2 + j // 2)
    return pl.pallas_call(
        functools.partial(attend_fwd_kernel, block),
        grid=(kv, n),
        in_specs=[
            pl.BlockSpec((block, 2 * HD), lambda j, i: (i, j)),
            pl.BlockSpec((length, 2 * HD), key_at),
            pl.BlockSpec((length, 2 * HD), value_at),
        ],
        out_specs=[
            pl.BlockSpec((block, 2 * HD), lambda j, i: (i, j)),
            pl.BlockSpec((1, 1, 1, 2 * block), lambda j, i: (j, i, 0, 0)),
        ],
        out_shape=[
            jax.ShapeDtypeStruct((length, width // 2), bf16),
            jax.ShapeDtypeStruct((kv, n, 1, 2 * block), f32),
        ],
        scratch_shapes=[pltpu.VMEM((length, 2 * HD), bf16), pltpu.VMEM((length, 2 * HD), bf16)],
        cost_estimate=pl.CostEstimate(
            flops=8 * length * length * 2 * HD * kv,
            transcendentals=length * length * kv,
            bytes_accessed=3 * length * width,
        ),
        name="attend_forward",
    )(qkv, qkv, qkv)


def attend_bwd_kernel(
    block, j, q_ref, k_ref, v_ref, g_ref, o_ref, lse_ref, back_ref,
    queries, grads, delta, keys, values, grad_q,
):
    first = j % 2 == 0
    n = q_ref.shape[0] // block
    keys[...] = pair_half(k_ref[...], first)
    values[...] = pair_half(v_ref[...], first)
    for i in range(n):
        rows = slice(i * block, (i + 1) * block)
        g = g_ref[rows, :]
        queries[i] = stack_pair(q_ref[rows, :])
        grads[i] = stack_pair(g)
        both = (g.astype(f32) * o_ref[rows, :].astype(f32)).T
        delta[i] = jnp.concatenate(
            [jnp.sum(both[:HD], axis=0, keepdims=True), jnp.sum(both[HD:], axis=0, keepdims=True)],
            axis=1,
        )
        grad_q[i] = jnp.zeros(grad_q.shape[1:], f32)

    def tile(key, value, key_t, i, diagonal):
        query, grad = queries[i], grads[i]
        probs = jnp.exp2(dot(key, query, NT) * (HD**-0.5 * LOG2E) - lse_ref[0, i])
        if diagonal:
            probs = causal(probs, block)
        grad_probs = dot(value, grad, NT)
        grad_scores = (probs * (grad_probs - delta[i]) * HD**-0.5).astype(bf16)
        grad_q[i] += dot(key_t, grad_scores)
        return dot(grad_scores, query), dot(probs.astype(bf16), grad)

    def step(t, _):
        rows = pl.ds(t * block, block)
        key, value = keys[rows, :], values[rows, :]
        key_t = key.astype(f32).T.astype(bf16)

        def body(i, carry):
            part_k, part_v = tile(key, value, key_t, i, False)
            return carry[0] + part_k, carry[1] + part_v

        part_k, part_v = lax.fori_loop(t + 1, n, body, tile(key, value, key_t, t, True))
        part_k = part_k + pltpu.roll(part_k, HD, 1)
        part_v = part_v + pltpu.roll(part_v, HD, 1)
        both = jnp.where(lanes_of(part_k) < HD, part_k, part_v)
        back_ref[rows, 2 * HD :] = both.astype(bf16)
        return 0

    lax.fori_loop(0, n, step, 0)
    for i in range(n):
        pair = jnp.concatenate([grad_q[i, :HD, :block], grad_q[i, HD:, block:]], axis=0)
        back_ref[i * block : (i + 1) * block, : 2 * HD] = pair.T.astype(bf16)


def attend_backward(qkv, grads, mixed, lse, block, j):
    length, width = qkv.shape
    kv = width // (4 * HD)
    n = length // block
    column = lambda c: pl.BlockSpec((length, 2 * HD), lambda i: (0, c))
    return pl.pallas_call(
        functools.partial(attend_bwd_kernel, block, j),
        grid=(1,),
        in_specs=[
            column(j),
            column(kv + j // 2),
            column(kv + kv // 2 + j // 2),
            column(j),
            column(j),
            pl.BlockSpec((1, n, 1, 2 * block), lambda i: (j, 0, 0, 0)),
        ],
        out_specs=pl.BlockSpec((length, 4 * HD), lambda i: (0, 0)),
        out_shape=jax.ShapeDtypeStruct((length, 4 * HD), bf16),
        scratch_shapes=[
            pltpu.VMEM((n, 2 * block, 2 * HD), bf16),
            pltpu.VMEM((n, 2 * block, 2 * HD), bf16),
            pltpu.VMEM((n, 1, 2 * block), f32),
            pltpu.VMEM((length, 2 * HD), bf16),
            pltpu.VMEM((length, 2 * HD), bf16),
            pltpu.VMEM((n, 2 * HD, 2 * block), f32),
        ],
        cost_estimate=pl.CostEstimate(
            flops=20 * length * length * 2 * HD,
            transcendentals=length * length,
            bytes_accessed=6 * length * 4 * HD,
        ),
        name="attend_backward",
    )(qkv, qkv, qkv, grads, mixed, lse)


def ffn_kernel(
    shards, begins, z_ref, h_ref, ht_ref, gy_ref, own_g, own_u, own_d, far_g, far_u, far_d,
    out_in, grad_in, valid, out_ref, grad_ref, *refs,
):
    terms, (down, total) = refs[:-2], refs[-2:]
    t = pl.program_id(0)
    z = z_ref[0]
    even = z_ref[1] == 0
    rows = own_g.shape[0]
    piece = rows // SPLIT
    unit = own_g.shape[1]
    lanes = down.shape[1] // SPLIT
    blocks = unit // piece

    @pl.when(t == 0)
    def _():
        total[...] = out_in[...]
        grad_ref[...] = jnp.zeros_like(grad_ref) if begins else grad_in[...]
        down[...] = own_d[...]

    @pl.when(t > 0)
    def _():
        for d in range(SPLIT):
            for k in range(blocks):
                down[k * piece : (k + 1) * piece, d * lanes : (d + 1) * lanes] = far_d[
                    d, 0, 0, :, k * lanes : (k + 1) * lanes
                ]

    def shard_of(r):
        return lax.rem(z + shards - r, shards)

    def weight(own, far):
        parts = [own[...]]
        for r in range(1, shards):
            parts.append(far[:, r - 1, 0].reshape(rows, unit))
        return jnp.concatenate(parts, axis=0)

    weight_g, weight_u = weight(own_g, far_g), weight(own_u, far_u)
    gate, up = dot(h_ref[...], weight_g), dot(h_ref[...], weight_u)
    grad_inner = dot(gy_ref[...], down[...], NT)
    sigma = jax.nn.sigmoid(gate)
    active = gate * sigma
    inner = (active * up).astype(bf16)
    grad_g = (grad_inner * up * sigma * (1.0 + gate * (1.0 - sigma))).astype(bf16)
    grad_u = (grad_inner * active).astype(bf16)
    total[...] += dot(inner, down[...])
    grad_ref[...] += dot(grad_g, weight_g, NT) + dot(grad_u, weight_u, NT)
    seg = pl.ds(pl.multiple_of(shard_of(t) * unit, unit), unit)

    def keep(term, at):
        term = term.astype(bf16)
        for r in range(shards):
            part = term[r * rows : (r + 1) * rows]
            if len(terms) == 1:
                terms[0][:, r, at : at + piece, seg] = part.reshape(SPLIT, piece, unit)
                continue
            part = part.reshape(SPLIT // 2, 2, piece, unit)
            mine, theirs = terms
            mine[:, r, at : at + piece, seg] = jnp.where(even, part[:, 0], part[:, 1])
            theirs[:, r, at : at + piece, seg] = jnp.where(even, part[:, 1], part[:, 0])

    keep(dot(ht_ref[...], grad_g), 0)
    keep(dot(ht_ref[...], grad_u), piece)

    @pl.when(t == shards - 1)
    def _():
        out = total[...]
        if out_ref.dtype == bf16:
            out = jnp.where(valid[...] > 0, out, 0.0).astype(bf16)
        out_ref[...] = out

    term = dot(inner, gy_ref[...], TN).astype(bf16)
    for d in range(SPLIT):
        for k in range(blocks):
            part = term[k * piece : (k + 1) * piece, d * lanes : (d + 1) * lanes]
            to = (t, slice(2 * piece, 3 * piece), slice(k * lanes, (k + 1) * lanes))
            if len(terms) == 1:
                terms[0][(d, *to)] = part
            elif d % 2 == 0:
                even_part = part
            else:
                even_part = term[k * piece : (k + 1) * piece, (d - 1) * lanes : d * lanes]
                terms[0][(d // 2, *to)] = jnp.where(even, even_part, part)
                terms[1][(d // 2, *to)] = jnp.where(even, part, even_part)


def ffn_chunk(
    c, kind, parted, z, hidden, hidden_t, grad_y, w_gate, w_up, w_down, far, out_in, grad_in, valid
):
    rows, width = hidden.shape
    shards = width // w_gate.shape[0]
    depth = w_gate.shape[0]
    unit = w_down.shape[0] // CHUNKS
    piece = depth // SPLIT
    n_far = shards - 1
    far = far.reshape(SPLIT, n_far, -1, piece, shards * unit)
    terms = (SPLIT // 2 if parted else SPLIT, shards, 3 * piece, shards * unit)
    n_terms = 2 if parted else 1
    seg = lambda t, z_ref: lax.rem(z_ref[0] + shards - t, shards)
    whole = lambda shape: pl.BlockSpec(shape, lambda t, z_ref: (0,) * len(shape))
    own = pl.BlockSpec((depth, unit), lambda t, z_ref: (0, seg(t, z_ref) * CHUNKS + c))
    gathered = lambda at: pl.BlockSpec(
        (SPLIT, n_far, 1, piece, unit), lambda t, z_ref: (0, 0, at, 0, seg(t, z_ref))
    )
    source = lambda t, z_ref: jnp.maximum(t - 1, 0)
    return pl.pallas_call(
        functools.partial(ffn_kernel, shards, c == 0),
        grid_spec=pltpu.PrefetchScalarGridSpec(
            num_scalar_prefetch=1,
            grid=(shards,),
            in_specs=[
                whole((rows, width)),
                whole((width, rows)),
                whole((rows, width)),
                own,
                own,
                pl.BlockSpec((unit, width), lambda t, z_ref: (c, 0)),
                gathered(kind),
                gathered(kind + 1),
                pl.BlockSpec(
                    (SPLIT, 1, 1, piece, shards * unit),
                    lambda t, z_ref: (0, source(t, z_ref), kind + 2, 0, 0),
                ),
                whole((rows, width)),
                whole((rows, width)),
                whole((rows, 1)),
            ],
            out_specs=[
                whole((rows, width)),
                whole((rows, width)),
            ]
            + [whole(terms)] * n_terms,
            scratch_shapes=[pltpu.VMEM((unit, width), bf16), pltpu.VMEM((rows, width), f32)],
        ),
        out_shape=[
            jax.ShapeDtypeStruct((rows, width), bf16 if c == CHUNKS - 1 else f32),
            jax.ShapeDtypeStruct((rows, width), f32),
        ]
        + [jax.ShapeDtypeStruct(terms, bf16)] * n_terms,
        cost_estimate=pl.CostEstimate(
            flops=18 * rows * width * shards * unit,
            transcendentals=rows * shards * unit,
            bytes_accessed=12 * width * shards * unit + 20 * rows * width,
        ),
        name="ffn_chunk",
    )(z, hidden, hidden_t, grad_y, w_gate, w_up, w_down, far, far, far, out_in, grad_in, valid)


def pack_kernel(m_ref, gate, up, down, out, first_ref, last_ref):
    piece, width = out.shape
    unit = down.shape[0] // CHUNKS
    shards = gate.shape[1] // down.shape[0]
    lanes = down.shape[1]
    for c in range(CHUNKS):
        ref = last_ref if c == CHUNKS - 1 else first_ref
        at = 0 if c == CHUNKS - 1 else 3 * piece * c
        for s in range(shards):
            source = slice((s * CHUNKS + c) * unit, (s * CHUNKS + c + 1) * unit)
            ref[at : at + piece, s * unit : (s + 1) * unit] = gate[:, source]
            ref[at + piece : at + 2 * piece, s * unit : (s + 1) * unit] = up[:, source]
        for k in range(unit // piece):
            rows = slice(c * unit + k * piece, c * unit + (k + 1) * piece)
            ref[at + 2 * piece : at + 3 * piece, k * lanes : (k + 1) * lanes] = down[rows, :]
    at = 3 * piece * (CHUNKS - 1)
    first_ref[at:, :width] = out[...]
    first_ref[at:, width:] = jnp.zeros_like(first_ref[at:, width:])


def pack(member, w_gate, w_up, w_down, w_out):
    depth, width = w_out.shape
    piece = depth // SPLIT
    lanes = width // SPLIT
    line = w_gate.shape[1] // CHUNKS
    rows = lambda w: pl.BlockSpec((piece, w.shape[1]), lambda i, m_ref: (m_ref[0], 0))
    outs = [((3 * CHUNKS - 2) * piece, line), (3 * piece, line)]
    return pl.pallas_call(
        pack_kernel,
        grid_spec=pltpu.PrefetchScalarGridSpec(
            num_scalar_prefetch=1,
            grid=(1,),
            in_specs=[
                rows(w_gate),
                rows(w_up),
                pl.BlockSpec((w_down.shape[0], lanes), lambda i, m_ref: (0, m_ref[0])),
                rows(w_out),
            ],
            out_specs=[pl.BlockSpec(shape, lambda i, m_ref: (0, 0)) for shape in outs],
        ),
        out_shape=[jax.ShapeDtypeStruct(shape, bf16) for shape in outs],
        name="pack",
    )(member.reshape(1), w_gate, w_up, w_down, w_out)


def unpack_kernel(source, *refs):
    gate_ref, up_ref, down_ref = refs[-3:]
    piece = source.shape[2]
    lanes = down_ref.shape[1] // SPLIT
    blocks = down_ref.shape[0] // piece
    gate_ref[...] = source[:, 0].astype(f32).reshape(gate_ref.shape)
    up_ref[...] = source[:, 1].astype(f32).reshape(up_ref.shape)
    for d in range(SPLIT):
        for k in range(blocks):
            down_ref[k * piece : (k + 1) * piece, d * lanes : (d + 1) * lanes] = source[
                d, 2, :, k * lanes : (k + 1) * lanes
            ].astype(f32)


def unpack_ffn(source, first, count, before, depth, shards, unit, width):
    piece = depth // SPLIT
    source = source.reshape(SPLIT, -1, piece, shards * unit)
    rows = unit // shards
    columns = pl.BlockSpec((depth, unit), lambda c, s: (0, s * CHUNKS + first + c))
    return pl.pallas_call(
        unpack_kernel,
        grid=(count, shards),
        in_specs=[pl.BlockSpec((SPLIT, 3, piece, unit), lambda c, s: (0, c, 0, s))]
        + [pl.BlockSpec(memory_space=pl.ANY)] * len(before),
        out_specs=[
            columns,
            columns,
            pl.BlockSpec((rows, width), lambda c, s: ((first + c) * shards + s, 0)),
        ],
        out_shape=[
            jax.ShapeDtypeStruct((depth, shards * CHUNKS * unit), f32),
            jax.ShapeDtypeStruct((depth, shards * CHUNKS * unit), f32),
            jax.ShapeDtypeStruct((CHUNKS * unit, width), f32),
        ],
        input_output_aliases={i + 1: i for i in range(len(before))},
        name="unpack_ffn",
    )(source, *before)


def unpack_near_kernel(m_ref, even, odd, *refs):
    gate_ref, up_ref, down_ref = refs[-3:]
    piece = gate_ref.shape[0] // SPLIT
    lanes = down_ref.shape[1] // SPLIT
    blocks = down_ref.shape[0] // piece
    for b in range(SPLIT):
        source = (odd if b % 2 else even)[b // 2].astype(f32)
        member = jnp.bitwise_xor(m_ref[0], b)
        rows = pl.ds(pl.multiple_of(member * piece, piece), piece)
        gate_ref[rows, :] = source[:piece]
        up_ref[rows, :] = source[piece : 2 * piece]
        columns = pl.ds(pl.multiple_of(member * lanes, lanes), lanes)
        for k in range(blocks):
            down_ref[k * piece : (k + 1) * piece, columns] = source[
                2 * piece :, k * lanes : (k + 1) * lanes
            ]


def unpack_near(member, even, odd, chunk, before, shards):
    gate, _, down = before
    unit = gate.shape[1] // (shards * CHUNKS)
    columns = pl.BlockSpec((gate.shape[0], unit), lambda s, m_ref: (0, s * CHUNKS + chunk))
    source = pl.BlockSpec((SPLIT // 2, even.shape[1], unit), lambda s, m_ref: (0, 0, s))
    rows = down.shape[0] // (CHUNKS * shards)
    return pl.pallas_call(
        unpack_near_kernel,
        grid_spec=pltpu.PrefetchScalarGridSpec(
            num_scalar_prefetch=1,
            grid=(shards,),
            in_specs=[source, source] + [pl.BlockSpec(memory_space=pl.ANY)] * 3,
            out_specs=[
                columns,
                columns,
                pl.BlockSpec((rows, down.shape[1]), lambda s, m_ref: (chunk * shards + s, 0)),
            ],
        ),
        out_shape=[jax.ShapeDtypeStruct(x.shape, f32) for x in before],
        input_output_aliases={3 + i: i for i in range(3)},
        name="unpack_near",
    )(member.reshape(1), even, odd, *before)


def shard_at(z, r, shards):
    return lax.rem(z + shards - r, shards)


def part_of(z, r, shards, size):
    return pl.ds(pl.multiple_of(shard_at(z, r, shards) * size, size), size)


def joined(own, far, r):
    return own[...] if r == 0 else far[:, r - 1].reshape(own.shape)


def qkv_fwd_kernel(
    shards, z_ref, h_ref, cos_ref, sin_ref, gain_q, gain_k, *refs
):
    own, far, (send_ref, raw_ref) = refs[:3], refs[3:6], refs[6:]
    z = z_ref[0]
    depth = own[0].shape[0]
    total = [None] * 3
    for r in range(shards):
        left = h_ref[:, part_of(z, r, shards, depth)]
        for i in range(3):
            part = dot(left, joined(own[i], far[i], r))
            total[i] = part if r == 0 else total[i] + part
    cosine, sine = cos_ref[...], sin_ref[...]
    at = 0
    for values, gain in ((total[0], gain_q), (total[1], gain_k)):
        for i in range(0, values.shape[1], 2 * HD):
            pair = values[:, i : i + 2 * HD]
            raw_ref[:, at : at + 2 * HD] = pair
            scaled = pair * lax.rsqrt(pair_mean(pair * pair) + EPS) * gain[...]
            rotated = scaled * cosine + other_half(scaled) * sine
            send_ref[:, at : at + 2 * HD] = rotated.astype(bf16)
            at += 2 * HD
    send_ref[:, at:] = total[2].astype(bf16)


def projection_specs(shards, depth, piece, columns):
    sizes = [n // shards for n in columns]
    last = lambda s: jnp.minimum(s, shards - 1)
    own = [pl.BlockSpec((depth, n), lambda s, z_ref: (0, last(s))) for n in sizes]
    starts = [sum(columns[:i]) // sizes[i] for i in range(3)]
    far = [
        pl.BlockSpec(
            (SPLIT, shards - 1, piece, n), lambda s, z_ref, start=start: (0, 0, 0, start + last(s))
        )
        for n, start in zip(sizes, starts)
    ]
    return own + far


def qkv_forward(z, hidden, cosine, sine, gain_q, gain_k, weights, far):
    local, width = hidden.shape
    depth = weights[0].shape[0]
    shards = width // depth
    columns = [w.shape[1] for w in weights]
    each = sum(columns) // shards
    raw = each - columns[2] // shards
    whole = lambda x: pl.BlockSpec(x.shape, lambda s, z_ref: (0,) * x.ndim)
    return pl.pallas_call(
        functools.partial(qkv_fwd_kernel, shards),
        grid_spec=pltpu.PrefetchScalarGridSpec(
            num_scalar_prefetch=1,
            grid=(shards,),
            in_specs=[whole(x) for x in (hidden, cosine, sine, gain_q, gain_k)]
            + projection_specs(shards, depth, far.shape[2], columns),
            out_specs=[
                pl.BlockSpec((local, each), lambda s, z_ref: (s, 0)),
                pl.BlockSpec((local, raw), lambda s, z_ref: (s, 0)),
            ],
        ),
        out_shape=[
            jax.ShapeDtypeStruct((shards * local, each), bf16),
            jax.ShapeDtypeStruct((shards * local, raw), f32),
        ],
        cost_estimate=pl.CostEstimate(
            flops=2 * local * width * sum(columns),
            transcendentals=0,
            bytes_accessed=2 * width * sum(columns) + 8 * local * sum(columns),
        ),
        name="qkv_forward",
    )(z, hidden, cosine, sine, gain_q, gain_k, *weights, far, far, far)


def qkv_bwd_kernel(
    shards, heads, z_ref, ht_ref, cos_ref, sin_ref, gain_q, gain_k,
    tokens, scale_ref, gain_1, resid, sum_2, raw_ref, *refs,
):
    back, refs = refs[:heads], refs[heads:]
    own, far, (tokens_ref, mine, theirs), refs = refs[:3], refs[3:6], refs[6:9], refs[9:]
    sum_q, sum_k, grads, grad_ref = refs
    step = pl.program_id(0)
    z = z_ref[0]
    even = z_ref[1] == 0
    depth = own[0].shape[0]
    piece = depth // SPLIT

    @pl.when(step == 0)
    def _():
        grad_ref[...] = jnp.zeros_like(grad_ref)
        sum_q[...] = jnp.zeros_like(sum_q)
        sum_k[...] = jnp.zeros_like(sum_k)

    @pl.when(step < shards)
    def _():
        cosine, sine = cos_ref[...], sin_ref[...]
        at = 0
        halves = [ref[:, 2 * HD :] for ref in back]
        swapped = [pltpu.roll(half.astype(f32), HD, 1).astype(bf16) for half in halves]
        low = lanes_of(halves[0]) < HD
        arrived = [[ref[:, : 2 * HD] for ref in back]]
        arrived.append([jnp.where(low, halves[i], swapped[i + 1]) for i in range(0, heads, 2)])
        arrived.append([jnp.where(low, swapped[i], halves[i + 1]) for i in range(0, heads, 2)])
        for pairs, gain, total in ((arrived[0], gain_q, sum_q), (arrived[1], gain_k, sum_k)):
            for grad in pairs:
                pair = raw_ref[:, at : at + 2 * HD]
                scale = lax.rsqrt(pair_mean(pair * pair) + EPS)
                hat = pair * scale
                grad = grad.astype(f32)
                grad = grad * cosine + other_half(grad * sine)
                total[...] += jnp.sum(grad * hat, axis=0, keepdims=True)
                grad = grad * gain[...]
                grads[:, at : at + 2 * HD] = (scale * (grad - hat * pair_mean(grad * hat))).astype(bf16)
                at += 2 * HD
        for i, pair in enumerate(arrived[2]):
            grads[:, at + i * 2 * HD : at + (i + 1) * 2 * HD] = pair
        ends = (0, own[0].shape[1], at, grads.shape[1])
        for r in range(shards):
            part = None
            for i in range(3):
                one = dot(grads[:, ends[i] : ends[i + 1]], joined(own[i], far[i], r), NT)
                part = one if i == 0 else part + one
            grad_ref[:, part_of(z, r, shards, depth)] += part
            term = dot(ht_ref[part_of(z, r, shards, depth), :], grads[...]).astype(bf16)
            term = term.reshape(SPLIT // 2, 2, piece, term.shape[1])
            mine[:, r] = jnp.where(even, term[:, 0], term[:, 1])
            theirs[:, r] = jnp.where(even, term[:, 1], term[:, 0])

    @pl.when(step == shards)
    def _():
        scale = scale_ref[...]
        normed = tokens[...].astype(f32) * scale
        grad = grad_ref[...]
        sum_1 = jnp.sum(grad * normed, axis=0, keepdims=True)
        tokens_ref[...] = resid[...] + norm_back(grad * gain_1[...], normed, scale)
        lanes = 2 * HD
        empty = jnp.zeros((piece, mine.shape[3] - lanes), f32)
        turn = [shard_at(z, r, shards) for r in range(shards)]
        grad_ref[0:1, :] = sum_1
        grad_ref[1:2, :] = sum_2[...]
        for r in range(shards):
            rows = []
            for i in range(2):
                for k in range(0, depth, lanes):
                    at = pl.multiple_of(turn[r] * depth + k, lanes)
                    rows.append(grad_ref[i : i + 1, pl.ds(at, lanes)])
            rows += [sum_q[...], sum_k[...]]
            rows.append(jnp.zeros((piece - len(rows), lanes), f32))
            block = jnp.concatenate([jnp.concatenate(rows, axis=0), empty], axis=1).astype(bf16)
            for d in range(SPLIT // 2):
                mine[d, r] = block
                theirs[d, r] = block


def qkv_backward(z, hidden_t, tables_gains, first_norm, back, raw, weights, far):
    width, local = hidden_t.shape
    depth = weights[0].shape[0]
    shards = width // depth
    piece = depth // SPLIT
    columns = [w.shape[1] for w in weights]
    each = sum(columns) // shards
    whole = lambda shape: pl.BlockSpec(shape, lambda s, z_ref: (0,) * len(shape))
    last = lambda s: jnp.minimum(s, shards - 1)
    rows = lambda x: pl.BlockSpec((local, x.shape[1]), lambda s, z_ref: (last(s), 0))
    terms = jax.ShapeDtypeStruct((SPLIT // 2, shards, piece, shards * each + 2 * HD), bf16)
    at_terms = pl.BlockSpec((SPLIT // 2, shards, piece, each), lambda s, z_ref: (0, 0, 0, s))
    return pl.pallas_call(
        functools.partial(qkv_bwd_kernel, shards, len(back)),
        grid_spec=pltpu.PrefetchScalarGridSpec(
            num_scalar_prefetch=1,
            grid=(shards + 1,),
            in_specs=[whole(x.shape) for x in (hidden_t, *tables_gains, *first_norm)]
            + [rows(x) for x in (raw, *back)]
            + projection_specs(shards, depth, piece, columns),
            out_specs=[whole((local, width)), at_terms, at_terms],
            scratch_shapes=[
                pltpu.VMEM((1, 2 * HD), f32),
                pltpu.VMEM((1, 2 * HD), f32),
                pltpu.VMEM((local, each), bf16),
                pltpu.VMEM((local, width), f32),
            ],
        ),
        out_shape=[jax.ShapeDtypeStruct((local, width), f32), terms, terms],
        cost_estimate=pl.CostEstimate(
            flops=4 * local * width * sum(columns),
            transcendentals=0,
            bytes_accessed=4 * width * sum(columns) + 8 * local * sum(columns),
        ),
        name="qkv_backward",
    )(z, hidden_t, *tables_gains, *first_norm, raw, *back, *weights, far, far, far)


def unpack_qkv_kernel(shards, m_ref, even, odd, *refs):
    piece = even.shape[1]
    out = refs[3]
    for b in range(SPLIT):
        source = (odd if b % 2 else even)[b // 2].astype(f32)
        rows = pl.ds(pl.multiple_of(jnp.bitwise_xor(m_ref[0], b) * piece, piece), piece)
        at = 0
        for s in range(shards):
            for ref in refs[:3]:
                n = ref.shape[1] // shards
                ref[rows, s * n : (s + 1) * n] = source[:, at : at + n]
                at += n
        out[rows, :] = source[:, source.shape[1] - out.shape[1] :]


def unpack_qkv(member, even, odd, shards, columns, width):
    piece = even.shape[1]
    columns = columns + [width]
    whole = lambda shape: pl.BlockSpec(shape, lambda i, m_ref: (0,) * len(shape))
    return pl.pallas_call(
        functools.partial(unpack_qkv_kernel, shards),
        grid_spec=pltpu.PrefetchScalarGridSpec(
            num_scalar_prefetch=1,
            grid=(1,),
            in_specs=[whole(even.shape), whole(odd.shape)],
            out_specs=[whole((SPLIT * piece, n)) for n in columns],
        ),
        out_shape=[jax.ShapeDtypeStruct((SPLIT * piece, n), f32) for n in columns],
        name="unpack_qkv",
    )(member.reshape(1), even, odd)


def out_fwd_kernel(shards, z_ref, mixed, tokens, gain, own, far, resid_ref, scale_ref, h_ref, ht_ref):
    z = z_ref[0]
    local = tokens.shape[0]
    resid = tokens[...].astype(f32)
    for r in range(shards):
        weight = own[...] if r == 0 else far[:, r - 1, 0].reshape(own.shape)
        resid = resid + dot(mixed[part_of(z, r, shards, local), :], weight)
    scale = rms_scale(resid)
    hidden = resid * scale * gain[...]
    resid_ref[...] = resid
    scale_ref[...] = scale
    turned = hidden.T.astype(bf16)
    low = hidden.astype(bf16)
    depth = own.shape[0]
    for s in range(shards):
        at = part_of(z, s, shards, depth)
        h_ref[:, at] = low[:, s * depth : (s + 1) * depth]
        ht_ref[at, :] = turned[s * depth : (s + 1) * depth]


def far_out_spec(far, width):
    size = (SPLIT, far.shape[1], 1, far.shape[3], width)
    return pl.BlockSpec(size, lambda i, z_ref: (0, 0, far.shape[2] - 1, 0, 0))


def out_forward(z, mixed, tokens, gain, w_out, far):
    local, width = tokens.shape
    shards = mixed.shape[0] // local
    piece = w_out.shape[0] // SPLIT
    far = far.reshape(SPLIT, shards - 1, -1, piece, far.shape[-1])
    whole = lambda shape: pl.BlockSpec(shape, lambda i, z_ref: (0,) * len(shape))
    outs = [((local, width), f32), ((local, 1), f32), ((local, width), bf16), ((width, local), bf16)]
    return pl.pallas_call(
        functools.partial(out_fwd_kernel, shards),
        grid_spec=pltpu.PrefetchScalarGridSpec(
            num_scalar_prefetch=1,
            grid=(1,),
            in_specs=[whole(x.shape) for x in (mixed, tokens, gain, w_out)]
            + [far_out_spec(far, width)],
            out_specs=[whole(shape) for shape, _ in outs],
        ),
        out_shape=[jax.ShapeDtypeStruct(*out) for out in outs],
        cost_estimate=pl.CostEstimate(
            flops=2 * local * width * width, transcendentals=0, bytes_accessed=14 * local * width
        ),
        name="out_forward",
    )(z, mixed, tokens, gain, w_out, far)


def out_bwd_kernel(
    shards, z_ref, grad, grad_y, resid, scale_ref, gain, own, far, grad_resid, sum_ref, branch, send
):
    z = z_ref[0]
    local = grad.shape[0]
    scale = scale_ref[...]
    normed = resid[...] * scale
    depth = own.shape[0]
    parts = [grad[:, part_of(z, s, shards, depth)] for s in range(shards)]
    come = jnp.concatenate(parts, axis=1)
    sum_ref[...] = jnp.sum(come * normed, axis=0, keepdims=True)
    total = grad_y[...].astype(f32) + norm_back(come * gain[...], normed, scale)
    grad_resid[...] = total
    low = total.astype(bf16)
    branch[...] = low
    for r in range(shards):
        weight = own[...] if r == 0 else far[:, r - 1, 0].reshape(own.shape)
        send[part_of(z, r, shards, local), :] = dot(low, weight, NT).astype(bf16)


def out_backward(z, grad, grad_y, resid, scale, gain, w_out, far):
    local, width = grad.shape
    depth = w_out.shape[0]
    shards = width // depth
    piece = depth // SPLIT
    far = far.reshape(SPLIT, shards - 1, -1, piece, far.shape[-1])
    whole = lambda shape: pl.BlockSpec(shape, lambda i, z_ref: (0,) * len(shape))
    outs = [((local, width), f32), ((1, width), f32), ((local, width), bf16), ((shards * local, depth), bf16)]
    return pl.pallas_call(
        functools.partial(out_bwd_kernel, shards),
        grid_spec=pltpu.PrefetchScalarGridSpec(
            num_scalar_prefetch=1,
            grid=(1,),
            in_specs=[whole(x.shape) for x in (grad, grad_y, resid, scale, gain, w_out)]
            + [far_out_spec(far, width)],
            out_specs=[whole(shape) for shape, _ in outs],
        ),
        out_shape=[jax.ShapeDtypeStruct(*out) for out in outs],
        cost_estimate=pl.CostEstimate(
            flops=2 * local * width * width, transcendentals=0, bytes_accessed=20 * local * width
        ),
        name="out_backward",
    )(z, grad, grad_y, resid, scale, gain, w_out, far)


def out_terms_kernel(shards, z_ref, mixed, branch, terms):
    term = dot(mixed[...], branch[...], TN).astype(bf16)
    terms[:, 0] = term.reshape(terms.shape[0], terms.shape[2], terms.shape[3])


def out_terms(z, mixed, branch):
    local, width = branch.shape
    shards = mixed.shape[0] // local
    depth = mixed.shape[1]
    piece = depth // SPLIT
    return pl.pallas_call(
        functools.partial(out_terms_kernel, shards),
        grid_spec=pltpu.PrefetchScalarGridSpec(
            num_scalar_prefetch=1,
            grid=(shards,),
            in_specs=[
                pl.BlockSpec((local, depth), lambda r, z_ref: (shard_at(z_ref[0], r, shards), 0)),
                pl.BlockSpec((local, width), lambda r, z_ref: (0, 0)),
            ],
            out_specs=pl.BlockSpec((SPLIT, 1, piece, width), lambda r, z_ref: (0, r, 0, 0)),
        ),
        out_shape=jax.ShapeDtypeStruct((SPLIT, shards, piece, width), bf16),
        cost_estimate=pl.CostEstimate(
            flops=2 * local * width * width, transcendentals=0, bytes_accessed=8 * local * width
        ),
        name="out_terms",
    )(z, mixed, branch)


def either_kernel(n, z_ref, *refs):
    came, out = refs[:-1], refs[-1]
    for r in range(1, n):
        out[r - 1] = jnp.where(z_ref[0] >= r, came[r - 1][...], came[2 * n - 2 - r][...])


class Axes:
    def __init__(self, mesh):
        self.n_dp = mesh.shape["dp"]
        self.n_seq = mesh.shape["seq"]
        self.groups = None
        self.across = None
        if self.n_dp > SPLIT:
            self.groups = [[g + i for i in range(SPLIT)] for g in range(0, self.n_dp, SPLIT)]
            self.across = [list(range(i, self.n_dp, SPLIT)) for i in range(SPLIT)]

    def member(self):
        return lax.rem(lax.axis_index("dp"), SPLIT)

    def shift(self, x, r):
        n = self.n_seq
        return lax.ppermute(x, "seq", [(i, (i + r) % n) for i in range(n)])

    def from_others(self, x):
        return [self.shift(x, r) for r in range(1, self.n_seq)]

    def pass_on(self, x):
        n = self.n_seq
        up = down = x
        below, above = [], []
        for step in range(1, n):
            up = lax.ppermute(up, "seq", [(i, i + 1) for i in range(step - 1, n - 1)])
            down = lax.ppermute(down, "seq", [(i + 1, i) for i in range(n - step)])
            below.append(up)
            above.append(down)
        return below + above

    def either(self, came):
        n = self.n_seq
        rows, width = came[0].shape
        block = rows // (7 if rows % 7 == 0 else 1)
        spec = pl.BlockSpec((block, width), lambda i, z_ref: (i, 0))
        return pl.pallas_call(
            functools.partial(either_kernel, n),
            grid_spec=pltpu.PrefetchScalarGridSpec(
                num_scalar_prefetch=1,
                grid=(rows // block,),
                in_specs=[spec] * len(came),
                out_specs=pl.BlockSpec((n - 1, block, width), lambda i, z_ref: (0, i, 0)),
            ),
            out_shape=jax.ShapeDtypeStruct((n - 1, rows, width), came[0].dtype),
            name="either",
        )(lax.axis_index("seq").reshape(1), *came)

    def gather_all(self, x):
        if self.groups:
            x = self.gather(lax.all_gather(x, "seq")[None])
        else:
            x = lax.all_gather(x, ("dp", "seq"))
        return x.reshape(SPLIT, self.n_seq, *x.shape[-2:])

    def gather_near(self, x, *others):
        even = jnp.stack([after(y, *others) for y in [x] + [self.swap(x, bit) for bit in (2, 4, 6)]])
        return even, self.swap(even, 1)

    def gather(self, x):
        return lax.all_gather(x, "dp", axis=0, tiled=True, axis_index_groups=self.groups)

    def scatter(self, terms):
        flat = terms.reshape(SPLIT * terms.shape[1], *terms.shape[2:])
        return lax.psum_scatter(
            flat, "dp", scatter_dimension=0, tiled=True, axis_index_groups=self.groups
        )

    def over_groups(self, x):
        return lax.psum(x, "dp", axis_index_groups=self.across) if self.across else x

    def swap(self, x, bit):
        return lax.ppermute(x, "dp", [(i, i ^ bit) for i in range(self.n_dp)])


def after(x, *others):
    return lax.optimization_barrier((x, *others))[0]


class Reduction:
    def __init__(self, axes, mine, theirs):
        self.axes = axes
        member = axes.member()
        self.x = lax.rem(lax.div(member, 2), 2)
        self.y = lax.div(member, 4)
        self.mine = mine.reshape(2, 2, *mine.shape[1:])
        self.state = (axes.swap(theirs, 1),)

    def then(self, *others):
        self.state = lax.optimization_barrier((*self.state, *others))[: len(self.state)]

    def _sum(self, y, x, low, *more):
        def cut(arr):
            shards = arr.shape[2] // 2
            start = [y if y is not None else 0, x if x is not None else 0, 0 if low else shards]
            size = [1 if y is not None else 2, 1 if x is not None else 2, shards]
            rest = arr.ndim - 3
            part = lax.dynamic_slice(arr, start + [0] * rest, size + list(arr.shape[3:]))
            drop = tuple(i for i, at in enumerate((y, x)) if at is not None)
            return lax.squeeze(part, drop).astype(f32)

        total = cut(self.mine) + cut(self.recv)
        for arr in more:
            total = total + arr.astype(f32)
        return total

    def first(self):
        (recv,) = self.state
        self.recv = recv.reshape(self.mine.shape)
        to_x = self._sum(None, 1 - self.x, True).astype(bf16)
        to_y = self._sum(1 - self.y, None, False).astype(bf16)
        self.sent = (to_x, to_y)
        return self

    def send_first(self):
        self.state = (self.axes.swap(self.sent[0], 2), self.axes.swap(self.sent[1], 4))
        return self

    def second(self):
        self.got_x, self.got_y = self.state
        pick = lambda arr, i: lax.dynamic_index_in_dim(arr, i, axis=0, keepdims=False)
        to_y = self._sum(1 - self.y, self.x, True, pick(self.got_x, 1 - self.y)).astype(bf16)
        to_x = self._sum(self.y, 1 - self.x, False, pick(self.got_y, 1 - self.x)).astype(bf16)
        self.sent = (to_x, to_y)
        return self

    def send_second(self):
        self.state = (self.axes.swap(self.sent[1], 4), self.axes.swap(self.sent[0], 2))
        return self

    def third(self):
        got_y, got_x = self.state
        pick = lambda arr, i: lax.dynamic_index_in_dim(arr, i, axis=0, keepdims=False)
        low = self._sum(self.y, self.x, True, pick(self.got_x, self.y), got_y)
        high = self._sum(self.y, self.x, False, pick(self.got_y, self.x), got_x)
        return jnp.concatenate([low, high], axis=0).astype(bf16)


def per_device(
    axes, tokens, lengths, cotangent, w_query, w_key, w_value, w_out, w_gate, w_up, w_down,
    gain_attn, gain_ffn, gain_query, gain_key,
):
    slots, local, width = tokens.shape
    assert slots == 1
    shards = axes.n_seq
    depth = width // shards
    piece = depth // SPLIT
    z = lax.axis_index("seq")
    member = axes.member()
    unit = w_down.shape[0] // CHUNKS
    lanes = width // SPLIT
    head = HD // shards
    weights = (w_query, w_key, w_value)
    columns = [w.shape[1] for w in weights]
    where = jnp.stack([z, lax.rem(member, 2)]).astype(jnp.int32)
    mine = lambda x: lax.dynamic_slice_in_dim(x, member * piece, piece, axis=0)

    def cut(parts):
        return lax.optimization_barrier(tuple(parts[r] for r in range(shards)))

    def cross_back(parts):
        return tuple(axes.shift(parts[r], -r) for r in range(1, shards))

    def add(own, others):
        own = own.astype(f32)
        for arr in others:
            own = own + arr.astype(f32)
        return axes.over_groups(own.astype(bf16))

    def by_owner(parts):
        pick = lambda i: lax.dynamic_index_in_dim(parts, lax.rem(z + shards - i, shards), 0)
        return jnp.concatenate([pick(i) for i in range(shards)], axis=0)

    def total(parts):
        return axes.over_groups(jnp.sum(parts.astype(f32), axis=0).astype(bf16))

    gains = jnp.concatenate([gain_attn, gain_ffn, gain_query, gain_key])
    gains = jnp.pad(gains, (0, piece * 128 - gains.shape[0])).reshape(piece, 128)
    packed = jnp.concatenate([mine(w_query), mine(w_key), mine(w_value), gains], axis=1)
    near = axes.from_others(packed)
    first_chunks, last_chunk = pack(member, w_gate, w_up, w_down, w_out)
    positions = z * local + jnp.arange(local, dtype=jnp.int32)
    cosine, sine = tables(positions)
    near = [after(x, first_chunks, cosine, sine) for x in near]
    far_qkv = axes.gather(jnp.stack([x[:, :-128] for x in near]))
    far_qkv = far_qkv.reshape(SPLIT, shards - 1, piece, -1)
    gains = jnp.stack([x[:, -128:].reshape(-1) for x in [packed] + near])
    order = lax.rem(z + shards - jnp.arange(shards), shards)
    hot = (order[:, None] == jnp.arange(shards)[None, :]).astype(f32)
    gains = jnp.sum(hot[:, :, None] * gains.astype(f32)[:, None, :], axis=0)

    def gathered_gain(start, size):
        return gains[:, start : start + size].reshape(1, -1)

    gain1 = gathered_gain(0, depth)
    gain2 = gathered_gain(depth, depth)
    gain_q = jnp.tile(gathered_gain(2 * depth, head), (1, 2))
    gain_k = jnp.tile(gathered_gain(2 * depth + head, head), (1, 2))


    def stack_after(parts, *others):
        return jnp.stack([after(x, *others) for x in parts])

    valid = (positions < lengths[0])[:, None]
    grad_y = jnp.where(valid, cotangent[0], jnp.zeros((), bf16))
    inputs = tokens[0].astype(f32)
    scale1 = rms_scale(inputs)
    hidden1 = (inputs * scale1 * gain1).astype(bf16)
    hidden1_t = hidden1.T

    def exchange(x):
        return lax.all_to_all(x, "seq", split_axis=0, concat_axis=0, tiled=True)

    crossed = axes.pass_on(after(first_chunks, *near))
    send, raw = qkv_forward(where, hidden1, cosine, sine, gain_q, gain_k, weights, far_qkv)
    far = axes.gather(axes.either([after(x, send) for x in crossed]))
    qkv = exchange(send)
    crossed = axes.from_others(after(last_chunk, qkv))
    block = 512
    mixed_heads, lse = attend_forward(qkv, block)
    mixed = exchange(after(mixed_heads, *crossed))
    crossed = jnp.stack([after(x, mixed_heads) for x in crossed])
    far_last = axes.gather(crossed)
    mixed = after(mixed, crossed)
    resid, scale2, hidden2, hidden2_t = out_forward(where, mixed, tokens[0], gain2, w_out, far)

    result, grad_hidden2 = resid, resid

    def chunk(c, result, grad_hidden2):
        last = c == CHUNKS - 1
        source, kind = (far_last, 0) if last else (far, 3 * c)
        return ffn_chunk(
            c, kind, last, where, hidden2, hidden2_t, grad_y, w_gate, w_up, w_down, source,
            result, grad_hidden2, valid.astype(f32),
        )

    result, grad_hidden2, terms = chunk(0, result, grad_hidden2)
    sum0 = axes.scatter(terms)
    result, grad_hidden2, terms = chunk(1, result, grad_hidden2)
    sum1 = axes.scatter(terms)
    output, grad_hidden2, *terms = chunk(2, result, grad_hidden2)
    sum2 = Reduction(axes, *terms)

    grad_resid, term_gain2, branch, send = out_backward(
        where, grad_hidden2, grad_y, resid, scale2, gain2, w_out, far
    )
    grad_heads = exchange(send)
    terms_out = out_terms(where, mixed, after(branch, send))
    sum2.then(terms_out)
    sum2.first().send_first()
    parts0 = cut(after(sum0, grad_heads))
    grad_heads = after(grad_heads, terms_out, *sum2.sent, *parts0)
    others0 = cross_back(parts0)
    back = attend_backward(qkv, grad_heads, mixed_heads, lse, block, 0)
    back_rows = [exchange(back)]
    for j in range(1, KV // shards):
        piece0 = add(parts0[0], after(others0, back))
        grad_heads = after(grad_heads, piece0)
        back = attend_backward(qkv, grad_heads, mixed_heads, lse, block, j)
        back_rows.append(exchange(after(back, back_rows[-1])))
    sum2.then(back)
    sum2.second().send_second()
    parts1 = by_owner(after(sum1, back))
    back_rows[-1] = after(back_rows[-1], parts1, *sum2.sent)
    sum_out = axes.scatter(after(terms_out, piece0))
    piece0 = axes.gather(piece0[None])
    parts1 = exchange(after(parts1, back_rows[-1]))
    grad_tokens, terms, other = qkv_backward(
        where, hidden1_t, (cosine, sine, gain_q, gain_k),
        (tokens[0], scale1, gain1, grad_resid, term_gain2), back_rows, raw, weights, far_qkv,
    )
    tail = Reduction(axes, terms, after(other, parts1, *sum2.state))
    parts2 = by_owner(sum2.third())
    tail.then(parts2)
    parts2 = exchange(parts2)
    tail.first().send_first()
    piece1 = axes.gather(total(after(parts1, *tail.sent))[None])
    tail.second().send_second()
    tail.then(parts2)
    tail = by_owner(jnp.concatenate([tail.third(), sum_out], axis=2))
    late = total(after(parts2, tail))
    grads = unpack_ffn(after(piece0, tail), 0, 1, (), depth, shards, unit, width)
    tail = total(after(exchange(tail), *grads))
    even, odd = axes.gather_near(tail)
    late = axes.gather_near(late, tail)
    grads = unpack_ffn(piece1, 1, 1, grads, depth, shards, unit, width)
    grads = unpack_near(member, *late, CHUNKS - 1, grads, shards)
    grad_gate, grad_up, grad_down = grads
    grad_query, grad_key, grad_value, grad_out = unpack_qkv(
        member, even, odd, shards, columns, width
    )
    sums = even[0, :, sum(columns) : sum(columns) + 2 * HD].astype(f32)
    n = depth // (2 * HD)
    sum_1, sum_2 = sums[:n].reshape(depth), sums[n : 2 * n].reshape(depth)
    heads = [sums[i, :HD] + sums[i, HD:] for i in (2 * n, 2 * n + 1)]
    sum_q, sum_k = (lax.dynamic_slice_in_dim(x, z * head, head) for x in heads)
    return (
        output[None],
        grad_tokens[None],
        grad_query,
        grad_key,
        grad_value,
        grad_out,
        grad_gate,
        grad_up,
        grad_down,
        sum_1,
        sum_2,
        sum_q,
        sum_k,
    )


def solution(mesh):
    rows = P("seq", None)
    whole = P("dp", "seq", None)
    return jax.shard_map(
        functools.partial(per_device, Axes(mesh)),
        mesh=mesh,
        in_specs=(whole, P("dp"), whole) + (rows,) * 7 + (P("seq"),) * 4,
        out_specs=(whole, whole) + (rows,) * 7 + (P("seq"),) * 4,
        check_vma=False,
    )
```
